32 devices in a mesh: dp: 8 (over y, x, core), seq: 4 (over z).
Axes of the slice: x: 2, y: 2, z: 4, core: 2. Of those that a mesh axis runs over, the one named last changes fastest.
Arguments:
- hidden_in: bfloat16 [2, 8, 512, 768], P(None, 'dp', 'seq'), may hold values from -6 to 6
- segment_ids: int32 [2, 8, 512], P(None, 'dp'), may hold values from 0 to 3, never falling along the last dimension, each value on 1 to 180 neighbouring positions
- query_emb: bfloat16 [2, 32, 32, 128], P(None, 'dp'), may hold values from -0.5 to 0.5
- positives: int32 [2, 32], replicated, may hold values from 0 to 31
- w_qkv: bfloat16 [768, 2304], replicated, may hold values from -0.21875 to 0.21875
- query_bias: float32 [768], replicated, may hold values from -0.625 to 0.625
- value_bias: float32 [768], replicated, may hold values from -0.625 to 0.625
- w_out: bfloat16 [768, 768], replicated, may hold values from -1.25 to 1.25
- out_bias: float32 [768], replicated, may hold values from -0.625 to 0.625
- norm1_gain: float32 [768], replicated, may hold values from 0.5 to 1.5
- norm1_bias: float32 [768], replicated, may hold values from -0.625 to 0.625
- w_up: bfloat16 [768, 3072], replicated, may hold values from -0.21875 to 0.21875
- up_bias: float32 [3072], replicated, may hold values from -0.625 to 0.625
- w_down: bfloat16 [3072, 768], replicated, may hold values from -0.109375 to 0.109375
- down_bias: float32 [768], replicated, may hold values from -0.625 to 0.625
- norm2_gain: float32 [768], replicated, may hold values from 0.5 to 1.5
- norm2_bias: float32 [768], replicated, may hold values from -0.625 to 0.625
- w_proj: bfloat16 [768, 128], replicated, may hold values from -0.21875 to 0.21875
Outputs:
- embeddings: bfloat16 [2, 8, 512, 128], P(None, 'dp', 'seq')
- losses: float32 [2, 32], P(None, 'dp')
- grad_in: float32 [2, 8, 512, 768], P(None, 'dp', 'seq')
- grad_qkv: float32 [1769472], P(('dp', 'seq'))
- grad_out: float32 [589824], P(('dp', 'seq'))
- grad_up: float32 [2359296], P(('dp', 'seq'))
- grad_down: float32 [2359296], P(('dp', 'seq'))
- grad_proj: float32 [98304], P(('dp', 'seq'))
- lower_vector_grads: float32 [3072], P(('dp', 'seq'))
- upper_vector_grads: float32 [6144], P(('dp', 'seq'))
The draws below stay inside these ranges and needn't reach their ends.
Inputs may be any that keep to these rules, and one draw needn't show every extreme that they name: `segment_ids`: within each row of 512 tokens the ids never fall, and each of the 4 passages holds 1 to 180 tokens. positives[m, q] numbers a passage of micro-batch m as row * 4 + segment id.
All inputs are finite; a program needn't handle non-finite values.
Results may differ from the reference program's by a relative error of at most 0.025.
Values may be sent and summed in bfloat16 or wider, within the bound.
No kernel may reach another device: no remote copies, remote signals or barrier semaphores. Data moves between devices by JAX's collectives and lax.ppermute only.
A program may use at most 192 MiB of HBM per device.

```python
import math
import jax
import jax.numpy as jnp
import numpy as np
from jax import lax

D = 768
HEADS = 12
HEAD_DIM = 64
FF = 3072
DOUT = 128
SEQLEN = 512
QTOK = 32
SEGS = 4
PASSAGE_MOST = 180
MICRO = 2
QUERIES = 32
ROWS_ALL = 8
PASSAGES = 32


def set_ends(array, own_key, low, top_value):
    longest = array.shape.index(max(array.shape))
    spots = []
    for shift in (0, 1):
        where = [jax.random.randint(jax.random.fold_in(own_key, axis), (), 0, length) for axis, length in enumerate(array.shape)]
        where[longest] = (where[longest] + shift) % array.shape[longest]
        spots.append(tuple(where))
    return array.at[spots[0]].set(low).at[spots[1]].set(top_value)


def block_scale(own_key, shape, cuts, smallest, high):
    def one(position, shards_of):
        steps = jax.random.uniform(jax.random.fold_in(jax.random.fold_in(own_key, 6), position), (shards_of,), jnp.float32, smallest / len(cuts), high / len(cuts))
        return jnp.repeat(jnp.exp(steps), shape[position] // shards_of).reshape((-1,) + (1,) * (len(shape) - position - 1))

    loudness = one(*cuts[0])
    for cut in cuts[1:]:
        loudness = loudness * one(*cut)
    return loudness


def split_up(number_of, total, most, skew):
    weights = [(1 << 20) // math.isqrt(rank ** skew) + 1 for rank in range(2, number_of + 1)]
    spare, holding = total - most - (number_of - 1), [1] * (number_of - 1)
    while spare > 0:
        free = [i for i in range(number_of - 1) if holding[i] < most]
        pool, left = sum([weights[i] for i in free]), spare
        for i in free:
            extra = min(most - holding[i], max(1, left * weights[i] // pool), spare)
            holding[i] = holding[i] + extra
            spare = spare - extra
    return np.array([most] + holding)


def uneven_parts(stream_key, count, total, bound, slope):
    if count == 2:
        one = jax.random.randint(stream_key, (), max(1, total - bound), min(bound, total - 1) + 1)
        return jnp.stack([one, total - one])
    tallies = jnp.asarray(split_up(count, total, bound, slope), jnp.int32)
    pairs = (count - 1) // 2
    source_of, sink = tallies[1:1 + 2 * pairs:2], tallies[2:2 + 2 * pairs:2]
    slack = jnp.minimum(source_of - 1, bound - sink)
    passed = jax.random.randint(jax.random.fold_in(stream_key, 1), (pairs,), 0, 1 << 20) % (slack + 1)
    tallies = tallies.at[1:1 + 2 * pairs:2].set(source_of - passed).at[2:2 + 2 * pairs:2].set(sink + passed)
    return tallies[jax.random.permutation(jax.random.fold_in(stream_key, 2), count)]


def gaussian(stream_key, shape, scale, most, shards=(), kind=jnp.bfloat16):
    drawn = scale * jax.random.normal(stream_key, shape, jnp.float32)
    if shards:
        drawn = drawn * block_scale(stream_key, shape, shards, -0.22, 0.18)
    return jnp.clip(drawn, -most, most).astype(kind)


def setup_inputs(seed: int = 0) -> dict:
    arg_keys = jax.random.split(jax.random.key(seed), 19)
    return {
        "hidden_in": gaussian(arg_keys[0], (MICRO, ROWS_ALL, SEQLEN, D), 1.0, 6.0, ((1, 8), (2, 4))),
        "segment_ids": jax.vmap(lambda own: jnp.searchsorted(jnp.cumsum(uneven_parts(own, SEGS, SEQLEN, PASSAGE_MOST, 2)), jnp.arange(SEQLEN), side="right"))(jax.random.split(arg_keys[1], MICRO * ROWS_ALL)).reshape((MICRO, ROWS_ALL, SEQLEN)).astype(jnp.int32),
        "query_emb": gaussian(arg_keys[2], (MICRO, QUERIES, QTOK, DOUT), (DOUT ** -0.5), 0.5, ((1, 8),)),
        "positives": set_ends(jax.random.randint(arg_keys[3], (MICRO, QUERIES), 0, PASSAGES), jax.random.fold_in(arg_keys[3], 1), 0, PASSAGES - 1).astype(jnp.int32),
        "w_qkv": gaussian(arg_keys[4], (D, 3 * D), D ** -0.5, 0.21875),
        "query_bias": gaussian(arg_keys[5], (D,), 0.1, 0.625, (), jnp.float32),
        "value_bias": gaussian(arg_keys[6], (D,), 0.1, 0.625, (), jnp.float32),
        "w_out": gaussian(arg_keys[7], (D, D), (D // 32) ** -0.5, 1.25),
        "out_bias": gaussian(arg_keys[8], (D,), 0.1, 0.625, (), jnp.float32),
        "norm1_gain": jnp.clip(1.0 + 0.1 * jax.random.normal(arg_keys[9], (D,), jnp.float32), 0.5, 1.5),
        "norm1_bias": gaussian(arg_keys[10], (D,), 0.1, 0.625, (), jnp.float32),
        "w_up": gaussian(arg_keys[11], (D, FF), D ** -0.5, 0.21875),
        "up_bias": gaussian(arg_keys[12], (FF,), 0.1, 0.625, (), jnp.float32),
        "w_down": gaussian(arg_keys[13], (FF, D), FF ** -0.5, 0.109375),
        "down_bias": gaussian(arg_keys[14], (D,), 0.1, 0.625, (), jnp.float32),
        "norm2_gain": jnp.clip(1.0 + 0.1 * jax.random.normal(arg_keys[15], (D,), jnp.float32), 0.5, 1.5),
        "norm2_bias": gaussian(arg_keys[16], (D,), 0.1, 0.625, (), jnp.float32),
        "w_proj": gaussian(arg_keys[17], (D, DOUT), D ** -0.5, 0.21875),
    }


@jax.custom_vjp
def low(v):
    return lax.optimization_barrier(v.astype(jnp.bfloat16)).astype(jnp.float32)

@jax.custom_vjp
def low_back(v):
    return v

def low_keep(v):
    return (low(v), None)

def low_pass(kept, grad):
    return (grad,)

def back_keep(v):
    return (v, None)

def back_low(kept, grad):
    return (low(grad),)
low.defvjp(low_keep, low_pass)
low_back.defvjp(back_keep, back_low)
HIGH = lax.Precision.HIGHEST
SHARP = 20.0
LN_EPS = 1e-12
NORM_EPS = 1e-12
MASKED = -1e+30

def matmul(left, right):
    return jnp.dot(left, right, precision=HIGH, preferred_element_type=jnp.float32)

def layer_norm(values_in, gain_vec, shift_vec):
    row_mean = lax.optimization_barrier(jnp.mean(values_in, axis=-1, keepdims=True))
    centred = values_in - row_mean
    spread = lax.optimization_barrier(jnp.mean(centred * centred, axis=-1, keepdims=True))
    return centred * lax.rsqrt(spread + LN_EPS) * gain_vec + shift_vec

def encode_row(params, tokens_row, segment_row, flat_queries):
    w_qkv, query_bias, value_bias, w_out, out_bias, norm1_gain, norm1_bias, w_up, up_bias, w_down, down_bias, norm2_gain, norm2_bias, w_proj = params
    qkv = matmul(tokens_row, w_qkv)
    query = low(low_back(qkv[:, :D] + query_bias))
    keys = low(low_back(qkv[:, D:2 * D]))
    values = low(low_back(qkv[:, 2 * D:] + value_bias))
    query_heads = query.reshape(SEQLEN, HEADS, HEAD_DIM)
    key_heads = keys.reshape(SEQLEN, HEADS, HEAD_DIM)
    value_heads = values.reshape(SEQLEN, HEADS, HEAD_DIM)
    raw = jnp.einsum('ihd,jhd->hij', query_heads, key_heads, precision=HIGH) * HEAD_DIM ** (-0.5)
    scores = low_back(raw)
    same_segment = segment_row[:, None] == segment_row[None, :]
    scores = jnp.where(same_segment[None, :, :], scores, MASKED)
    shift = lax.optimization_barrier(jnp.max(scores, axis=-1, keepdims=True))
    expo = jnp.exp(scores - shift)
    attn_probs = expo / lax.optimization_barrier(jnp.sum(expo, axis=-1, keepdims=True))
    context = jnp.einsum('hij,jhd->ihd', low(attn_probs), value_heads, precision=HIGH).reshape(SEQLEN, D)
    context = low(low_back(context))
    attended = low_back(matmul(context, w_out) + out_bias)
    hidden1 = layer_norm(tokens_row + attended, norm1_gain, norm1_bias)
    up_pre = low_back(matmul(low(hidden1), w_up) + up_bias)
    act_low = low(jax.nn.gelu(up_pre, approximate=False))
    ffn_out = low_back(matmul(act_low, w_down) + down_bias)
    hidden2 = layer_norm(hidden1 + ffn_out, norm2_gain, norm2_bias)
    proj_out = low_back(matmul(low(hidden2), w_proj))
    embedded = low(proj_out * lax.rsqrt(lax.optimization_barrier(jnp.sum(proj_out * proj_out, axis=-1, keepdims=True)) + NORM_EPS))
    similarity = low_back(matmul(flat_queries, embedded.T))
    sharpened = SHARP * similarity
    in_passage = segment_row[:, None] == jnp.arange(SEGS, dtype=jnp.int32)[None, :]
    member = in_passage.astype(jnp.float32)
    masked_sharp = jnp.where(in_passage[None, :, :], sharpened[:, :, None], MASKED)
    top_pass = lax.optimization_barrier(jnp.max(masked_sharp, axis=1))
    totals = lax.optimization_barrier(jnp.sum(jnp.exp(masked_sharp - top_pass[:, None, :]), axis=1))
    counts = lax.optimization_barrier(jnp.sum(member, axis=0))
    match = top_pass + jnp.log(totals) - jnp.log(counts)[None, :]
    score = lax.optimization_barrier(jnp.sum(match.reshape(QUERIES, QTOK, SEGS), axis=1))
    return (score, embedded)

def forward(params, hidden, segment_ids, queries, positives):
    row_fn = jax.checkpoint(encode_row)
    total_loss = jnp.zeros((), jnp.float32)
    loss_rows = []
    embed_rows = []
    for micro_step in range(MICRO):
        flat_queries = queries[micro_step].reshape(QUERIES * QTOK, DOUT)

        def one_row(pair):
            return row_fn(params, pair[0], pair[1], flat_queries)
        scores, embedded = lax.map(one_row, (hidden[micro_step], segment_ids[micro_step]))
        logits = jnp.transpose(scores, (1, 0, 2)).reshape(QUERIES, PASSAGES)
        top_logit = lax.optimization_barrier(jnp.max(logits, axis=1, keepdims=True))
        log_total = top_logit[:, 0] + jnp.log(lax.optimization_barrier(jnp.sum(jnp.exp(logits - top_logit), axis=1)))
        chosen = (jnp.arange(PASSAGES, dtype=jnp.int32)[None, :] == positives[micro_step][:, None]).astype(jnp.float32)
        query_loss = log_total - lax.optimization_barrier(jnp.sum(logits * chosen, axis=1))
        total_loss = total_loss + jnp.sum(query_loss)
        loss_rows.append(query_loss)
        embed_rows.append(embedded)
    return (total_loss, (jnp.stack(embed_rows), jnp.stack(loss_rows)))

def reference(hidden_in, segment_ids, query_emb, positives, w_qkv, query_bias, value_bias, w_out, out_bias, norm1_gain, norm1_bias, w_up, up_bias, w_down, down_bias, norm2_gain, norm2_bias, w_proj):
    params = tuple((weight_item.astype(jnp.float32) for weight_item in (w_qkv, query_bias, value_bias, w_out, out_bias, norm1_gain, norm1_bias, w_up, up_bias, w_down, down_bias, norm2_gain, norm2_bias, w_proj)))
    hidden = hidden_in.astype(jnp.float32)
    queries = query_emb.astype(jnp.float32)

    def objective(params_in, hidden_value):
        return forward(params_in, hidden_value, segment_ids, queries, positives)
    total_loss, pullback, aux_out = jax.vjp(objective, params, hidden, has_aux=True)
    embedded, losses = aux_out
    grad_params, grad_hidden = pullback(jnp.ones_like(total_loss))
    g_qkv, g_qbias, g_vbias, g_out, g_obias, g_gain1, g_shift1, g_up, g_ubias, g_down, g_dbias, g_gain2, g_shift2, g_proj = grad_params
    lower_vec = jnp.concatenate([g_qbias, g_vbias, g_obias, g_gain1])
    upper_vec = jnp.concatenate([g_shift1, g_dbias, g_gain2, g_shift2, g_ubias])
    return (embedded.astype(jnp.bfloat16), losses, grad_hidden, g_qkv.reshape(-1), g_out.reshape(-1), g_up.reshape(-1), g_down.reshape(-1), g_proj.reshape(-1), lower_vec, upper_vec)
```

```python
import jax
import jax.numpy as jnp
from jax import lax
from jax.sharding import PartitionSpec as P

HEADS = 12
SEGS = 4
PASSAGE_MOST = 180

SHARP = 20.0
LN_EPS = 1e-12
NORM_EPS = 1e-12
MASKED = -1e30
HIGH = lax.Precision.HIGHEST
bf16 = jnp.bfloat16
f32 = jnp.float32


def layer_norm(values_in, gain_vec, shift_vec):
    row_mean = jnp.mean(values_in, axis=-1, keepdims=True)
    centred = values_in - row_mean
    spread = jnp.mean(centred * centred, axis=-1, keepdims=True)
    return centred * lax.rsqrt(spread + LN_EPS) * gain_vec + shift_vec


def unit_rows(values_in):
    return values_in * lax.rsqrt(jnp.sum(values_in * values_in, axis=-1, keepdims=True) + NORM_EPS)


def gelu_exact(values_in):
    return jax.nn.gelu(values_in, approximate=False)


def bits_of(count):
    return [1 << k for k in range(count.bit_length() - 1)]


def swap(value, axis, bit, count):
    return lax.ppermute(value, axis, [(i, i ^ bit) for i in range(count)])


def shifted(value, axis, step, count):
    return lax.ppermute(value, axis, [(i, i + step) for i in range(count) if 0 <= i + step < count])


def halve(grad, bit, dp_pos, dp_count):
    lead = grad.shape[0]
    size = grad.shape[1]
    mine_at = (dp_pos // bit) % 2
    del lead, size
    mine = lax.dynamic_index_in_dim(grad, mine_at, 1, keepdims=False)
    other = lax.dynamic_index_in_dim(grad, 1 - mine_at, 1, keepdims=False)
    recv = swap(other, "dp", bit, dp_count)
    return (mine.astype(f32) + recv.astype(f32)).astype(bf16)


def reduce_dp(grad, order, dp_pos, dp_count):
    tail = grad.shape[1:]
    left = sorted(bits_of(dp_count))
    for bit in order:
        low = len([b for b in left if b < bit])
        high = len(left) - low - 1
        g = grad.reshape((1 << high, 2, 1 << low) + tail)
        grad = halve(g, bit, dp_pos, dp_count)
        left.remove(bit)
    return grad.reshape(tail)


def reduce_seq(grad, seq_pos, seq_count):
    total = lax.dynamic_index_in_dim(grad, seq_pos, 0, keepdims=False).astype(f32)
    for step in range(1, seq_count):
        piece = lax.dynamic_index_in_dim(grad, (seq_pos + step) % seq_count, 0, keepdims=False)
        recv = lax.ppermute(piece, "seq", [(i, (i + step) % seq_count) for i in range(seq_count)])
        total = total + recv.astype(f32)
    return total


def body(
    hidden_in,
    segment_ids,
    query_emb,
    positives,
    w_qkv,
    query_bias,
    value_bias,
    w_out,
    out_bias,
    norm1_gain,
    norm1_bias,
    w_up,
    up_bias,
    w_down,
    down_bias,
    norm2_gain,
    norm2_bias,
    w_proj,
):
    micro_count, row_count, local_len, width = hidden_in.shape
    full_len = segment_ids.shape[2]
    heads = HEADS
    head_dim = width // heads
    score_scale = head_dim ** (-0.5)
    embed_width = w_proj.shape[1]
    queries_local = query_emb.shape[1]
    query_tokens = query_emb.shape[2]
    seq_count = lax.axis_size("seq")
    dp_count = lax.axis_size("dp")
    seq_pos = lax.axis_index("seq")
    dp_pos = lax.axis_index("dp")
    rows = micro_count * row_count
    tokens = rows * local_len
    near = local_len
    far = 64
    reach = near + far
    window = local_len + 2 * reach

    x_own = hidden_in.reshape(rows, local_len, width)
    x_win = jnp.concatenate(
        [
            shifted(x_own[:, local_len - far :], "seq", 2, seq_count),
            shifted(x_own, "seq", 1, seq_count),
            x_own,
            shifted(x_own, "seq", -1, seq_count),
            shifted(x_own[:, :far], "seq", -2, seq_count),
        ],
        axis=1,
    )
    seg_full = segment_ids.reshape(rows, full_len)
    seg_own = lax.dynamic_slice_in_dim(seg_full, seq_pos * local_len, local_len, 1)
    seg_pad = jnp.pad(seg_full, ((0, 0), (reach, reach)), constant_values=-1)
    seg_win = lax.dynamic_slice_in_dim(seg_pad, seq_pos * local_len, window, 1)

    queries = query_emb.reshape(micro_count, queries_local * query_tokens, embed_width)
    for bit in bits_of(dp_count):
        recv = swap(queries, "dp", bit, dp_count)
        upper = (dp_pos // bit) % 2
        queries = jnp.where(
            upper == 0,
            jnp.concatenate([queries, recv], axis=1),
            jnp.concatenate([recv, queries], axis=1),
        )
    query_all = queries.shape[1]
    query_count = query_all // query_tokens

    x_flat = x_own.reshape(tokens, width)
    query_low = (
        jnp.dot(x_flat, w_qkv[:, :width], preferred_element_type=f32) + query_bias
    ).astype(bf16)
    kv = jnp.dot(x_win.reshape(rows * window, width), w_qkv[:, width:], preferred_element_type=f32)
    key_low = kv[:, :width].astype(bf16).reshape(rows, window, heads, head_dim)
    value_low = (kv[:, width:] + value_bias).astype(bf16).reshape(rows, window, heads, head_dim)
    query_heads = query_low.reshape(rows, local_len, heads, head_dim)
    same = (seg_own[:, :, None] == seg_win[:, None, :])[:, None, :, :]
    raw = (
        jnp.einsum("rihd,rjhd->rhij", query_heads, key_low, preferred_element_type=f32)
        * score_scale
    )
    scores = jnp.where(same, raw, MASKED)
    expo = jnp.exp(scores - jnp.max(scores, axis=-1, keepdims=True))
    probs = expo / jnp.sum(expo, axis=-1, keepdims=True)
    probs_low = probs.astype(bf16)
    context = (
        jnp.einsum("rhij,rjhd->rihd", probs_low, value_low, preferred_element_type=f32)
        .reshape(tokens, width)
        .astype(bf16)
    )
    attended = jnp.dot(context, w_out, preferred_element_type=f32) + out_bias
    resid1 = x_flat.astype(f32) + attended
    hidden1, norm1_back = jax.vjp(layer_norm, resid1, norm1_gain, norm1_bias)
    hidden1_low = hidden1.astype(bf16)
    up_pre = jnp.dot(hidden1_low, w_up, preferred_element_type=f32) + up_bias
    gelu_out, gelu_back = jax.vjp(gelu_exact, up_pre)
    act_low = gelu_out.astype(bf16)
    ffn_out = jnp.dot(act_low, w_down, preferred_element_type=f32) + down_bias
    resid2 = hidden1 + ffn_out
    hidden2, norm2_back = jax.vjp(layer_norm, resid2, norm2_gain, norm2_bias)
    hidden2_low = hidden2.astype(bf16)
    proj_out = jnp.dot(hidden2_low, w_proj, preferred_element_type=f32)
    unit_out, unit_back = jax.vjp(unit_rows, proj_out)
    embed_low = unit_out.astype(bf16)

    embed_micro = embed_low.reshape(micro_count, row_count, local_len, embed_width)
    sharpened = SHARP * jnp.einsum(
        "mrtc,mkc->mrtk", embed_micro, queries, preferred_element_type=f32
    )
    seg_range = jnp.arange(SEGS, dtype=jnp.int32)
    seg_own4 = seg_own.reshape(micro_count, row_count, local_len)
    in_local = seg_own4[..., None] == seg_range
    member = in_local.astype(f32)
    top_parts = []
    sum_parts = []
    for s in range(SEGS):
        masked = jnp.where(in_local[..., s : s + 1], sharpened, MASKED)
        top = jnp.max(masked, axis=2)
        top_parts.append(top)
        sum_parts.append(jnp.sum(jnp.exp(masked - top[:, :, None, :]), axis=2))
    top_all = jnp.stack(top_parts, axis=2)
    totals = jnp.stack(sum_parts, axis=2)
    for bit in bits_of(seq_count):
        recv = swap(jnp.stack([top_all, totals]), "seq", bit, seq_count)
        both = jnp.maximum(top_all, recv[0])
        totals = totals * jnp.exp(top_all - both) + recv[1] * jnp.exp(recv[0] - both)
        top_all = both
    counts = jnp.sum(
        (seg_full.reshape(micro_count, row_count, full_len)[..., None] == seg_range).astype(f32),
        axis=2,
    )
    match = top_all + jnp.log(totals) - jnp.log(counts)[..., None]
    score = jnp.sum(
        match.reshape(micro_count, row_count * SEGS, query_count, query_tokens), axis=3
    )
    passage = dp_pos * row_count * SEGS + jnp.arange(row_count * SEGS, dtype=jnp.int32)
    chosen = (passage[None, :, None] == positives[:, None, :]).astype(f32)
    top_logit = jnp.max(score, axis=1)
    sum_logit = jnp.sum(jnp.exp(score - top_logit[:, None, :]), axis=1)
    hit = jnp.sum(score * chosen, axis=1)
    for bit in bits_of(dp_count):
        recv = swap(jnp.stack([top_logit, sum_logit, hit]), "dp", bit, dp_count)
        both = jnp.maximum(top_logit, recv[0])
        sum_logit = sum_logit * jnp.exp(top_logit - both) + recv[1] * jnp.exp(recv[0] - both)
        top_logit = both
        hit = hit + recv[2]
    query_loss = top_logit + jnp.log(sum_logit) - hit
    losses = lax.dynamic_slice_in_dim(query_loss, dp_pos * queries_local, queries_local, 1)
    grad_score = jnp.exp(score - top_logit[:, None, :]) / sum_logit[:, None, :] - chosen
    grad_match = jnp.broadcast_to(
        grad_score[..., None], grad_score.shape + (query_tokens,)
    ).reshape(micro_count, row_count, SEGS, query_all)
    factor = SHARP * grad_match / totals
    shift_tok = jnp.zeros_like(sharpened)
    scale_tok = jnp.zeros_like(sharpened)
    for s in range(SEGS):
        shift_tok = jnp.where(in_local[..., s : s + 1], top_all[:, :, None, s], shift_tok)
        scale_tok = jnp.where(in_local[..., s : s + 1], factor[:, :, None, s], scale_tok)
    del member
    grad_sims = (scale_tok * jnp.exp(sharpened - shift_tok)).astype(bf16)
    grad_embed = jnp.einsum(
        "mrtk,mkc->mrtc", grad_sims, queries, preferred_element_type=f32
    ).reshape(tokens, embed_width)
    grad_proj_low = unit_back(grad_embed)[0].astype(bf16)
    sum_proj = jnp.einsum("tc,te->ce", hidden2_low, grad_proj_low, preferred_element_type=f32)
    grad_hidden2 = jnp.einsum("te,ce->tc", grad_proj_low, w_proj, preferred_element_type=f32)
    grad_resid2, sum_gain2, sum_shift2 = norm2_back(grad_hidden2)
    grad_ffn = grad_resid2.astype(bf16)
    sum_dbias = jnp.sum(grad_ffn.astype(f32), axis=0)
    sum_down = jnp.einsum("tf,td->fd", act_low, grad_ffn, preferred_element_type=f32)
    grad_act = jnp.einsum("td,fd->tf", grad_ffn, w_down, preferred_element_type=f32)
    grad_up_low = gelu_back(grad_act)[0].astype(bf16)
    sum_ubias = jnp.sum(grad_up_low.astype(f32), axis=0)
    sum_up = jnp.einsum("td,tf->df", hidden1_low, grad_up_low, preferred_element_type=f32)
    grad_hidden1 = grad_resid2 + jnp.einsum(
        "tf,df->td", grad_up_low, w_up, preferred_element_type=f32
    )
    grad_resid1, sum_gain1, sum_shift1 = norm1_back(grad_hidden1)
    grad_attended = grad_resid1.astype(bf16)
    sum_obias = jnp.sum(grad_attended.astype(f32), axis=0)
    sum_out = jnp.einsum("tc,td->cd", context, grad_attended, preferred_element_type=f32)
    grad_context = (
        jnp.einsum("td,cd->tc", grad_attended, w_out, preferred_element_type=f32)
        .astype(bf16)
        .reshape(rows, local_len, heads, head_dim)
    )
    grad_probs = jnp.einsum("rihd,rjhd->rhij", grad_context, value_low, preferred_element_type=f32)
    grad_values = jnp.einsum(
        "rhij,rihd->rjhd", probs_low, grad_context, preferred_element_type=f32
    )
    inner_sum = jnp.sum(probs * grad_probs, axis=-1, keepdims=True)
    grad_scores = (probs * (grad_probs - inner_sum)).astype(bf16)
    grad_query = (
        jnp.einsum("rhij,rjhd->rihd", grad_scores, key_low, preferred_element_type=f32)
        * score_scale
    )
    grad_query = grad_query.reshape(tokens, width).astype(bf16)
    grad_keys = (
        jnp.einsum("rhij,rihd->rjhd", grad_scores, query_heads, preferred_element_type=f32)
        * score_scale
    )
    grad_kv = jnp.concatenate(
        [
            grad_keys.reshape(rows * window, width),
            grad_values.reshape(rows * window, width),
        ],
        axis=1,
    ).astype(bf16)
    sum_q = jnp.einsum("tc,te->ce", x_flat, grad_query, preferred_element_type=f32)
    sum_kv = jnp.einsum(
        "tc,te->ce", x_win.reshape(rows * window, width), grad_kv, preferred_element_type=f32
    )
    sum_qbias = jnp.sum(grad_query.astype(f32), axis=0)
    sum_vbias = jnp.sum(grad_kv[:, width:].astype(f32), axis=0)
    back_q = jnp.einsum("te,ce->tc", grad_query, w_qkv[:, :width], preferred_element_type=f32)
    back_kv = jnp.einsum(
        "te,ce->tc", grad_kv, w_qkv[:, width:], preferred_element_type=f32
    ).reshape(rows, window, width)
    back_low = back_kv.astype(bf16)
    grad_in = (
        (grad_resid1 + back_q).reshape(rows, local_len, width)
        + back_kv[:, reach : reach + local_len]
        + shifted(back_low[:, far:reach], "seq", -1, seq_count).astype(f32)
        + shifted(back_low[:, reach + local_len : window - far], "seq", 1, seq_count).astype(f32)
        + jnp.pad(
            shifted(back_low[:, :far], "seq", -2, seq_count).astype(f32),
            ((0, 0), (local_len - far, 0), (0, 0)),
        )
        + jnp.pad(
            shifted(back_low[:, window - far :], "seq", 2, seq_count).astype(f32),
            ((0, 0), (0, local_len - far), (0, 0)),
        )
    )

    devices = dp_count * seq_count
    lower_vec = jnp.concatenate([sum_qbias, sum_vbias, sum_obias, sum_gain1])
    upper_vec = jnp.concatenate([sum_shift1, sum_dbias, sum_gain2, sum_shift2, sum_ubias])
    vec = jnp.concatenate(
        [lower_vec.reshape(devices, -1), upper_vec.reshape(devices, -1)], axis=1
    )
    bits = bits_of(dp_count)
    order_a = bits
    order_b = bits[:1] + bits[1:][::-1]

    def reduced(grad, cut):
        part = grad.astype(bf16).reshape(dp_count, seq_count, grad.shape[0] // devices, -1)
        first = reduce_dp(part[..., :cut], order_a, dp_pos, dp_count)
        second = reduce_dp(part[..., cut:], order_b, dp_pos, dp_count)
        return reduce_seq(jnp.concatenate([first, second], axis=-1), seq_pos, seq_count)

    down_part = reduced(sum_down, width // 2)
    up_part = reduced(sum_up, w_up.shape[1] // 2)
    vec_rows = vec.reshape(width, -1)
    vec_rows = jnp.pad(vec_rows, ((0, 0), (0, 128 - vec_rows.shape[1])))
    last = reduced(jnp.concatenate([sum_q, sum_kv, sum_out, sum_proj, vec_rows], axis=1), 1664)
    at = 3 * width
    qkv_part = last[:, :at]
    out_part = last[:, at : at + width]
    proj_part = last[:, at + width : at + width + embed_width]
    vec_part = last[:, at + width + embed_width :][:, : vec.size // width].reshape(-1)
    lower_size = lower_vec.size // devices
    return (
        embed_micro,
        losses,
        grad_in.reshape(micro_count, row_count, local_len, width),
        qkv_part.reshape(-1),
        out_part.reshape(-1),
        up_part.reshape(-1),
        down_part.reshape(-1),
        proj_part.reshape(-1),
        vec_part[:lower_size],
        vec_part[lower_size:],
    )


def solution(mesh):
    in_specs = (
        P(None, "dp", "seq", None),
        P(None, "dp", None),
        P(None, "dp", None, None),
    ) + (P(),) * 15
    out_specs = (
        P(None, "dp", "seq", None),
        P(None, "dp"),
        P(None, "dp", "seq", None),
    ) + (P(("dp", "seq")),) * 7
    return jax.shard_map(body, mesh=mesh, in_specs=in_specs, out_specs=out_specs, check_vma=False)
```

```python
import functools

import jax
import jax.numpy as jnp
from jax import lax
from jax.experimental import pallas as pl
from jax.experimental.pallas import tpu as pltpu
from jax.sharding import PartitionSpec as P

HEADS = 12
SEGS = 4
PASSAGE_MOST = 180

SHARP = 20.0
LN_EPS = 1e-12
NORM_EPS = 1e-12
MASKED = -1e30
HIGH = lax.Precision.HIGHEST
bf16 = jnp.bfloat16
f32 = jnp.float32
VMEM = pl.BlockSpec(memory_space=pltpu.VMEM)
SMEM = pl.BlockSpec(memory_space=pltpu.SMEM)
PARAMS = pltpu.CompilerParams(vmem_limit_bytes=58 << 20)


def bits_of(count):
    return [1 << k for k in range(count.bit_length() - 1)]


def swap(value, axis, bit, count):
    return lax.ppermute(value, axis, [(i, i ^ bit) for i in range(count)])


def shifted(value, axis, step, count):
    return lax.ppermute(value, axis, [(i, i + step) for i in range(count) if 0 <= i + step < count])


def dot(left, right, left_dim, right_dim, precision=None):
    return lax.dot_general(
        left,
        right,
        (((left_dim,), (right_dim,)), ((), ())),
        precision=precision,
        preferred_element_type=f32,
    )


def ident(pos, meta, row, length):
    seg = jnp.zeros(pos.shape, jnp.int32)
    for s in range(SEGS - 1):
        seg = seg + (pos >= meta[2 + row * (SEGS - 1) + s]).astype(jnp.int32)
    return jnp.where((pos >= 0) & (pos < length), seg, -1)


def key_positions(base, local, far, shape):
    w = lax.broadcasted_iota(jnp.int32, shape, 0)
    pos = base + w
    pos = jnp.where(w >= local, base - 2 * local + w, pos)
    pos = jnp.where(w >= 2 * local, base - local + w, pos)
    pos = jnp.where(w >= 3 * local, base - 4 * local - far + w, pos)
    return jnp.where(w >= 3 * local + far, base - local - far + w, pos)


def pair_rows(block, even):
    zero = jnp.zeros_like(block)
    return jnp.concatenate([jnp.where(even, block, zero), jnp.where(even, zero, block)], axis=0)


def attention_bias(meta, row, local, far, window, length):
    base = meta[0]
    key_seg = ident(key_positions(base, local, far, (window, local)), meta, row, length)
    query_seg = ident(
        base + lax.broadcasted_iota(jnp.int32, (window, local), 1), meta, row, length
    )
    return jnp.where(key_seg == query_seg, 0.0, MASKED).astype(f32)


def forward_kernel(
    dims,
    meta,
    x_own,
    prev,
    follow,
    far_prev,
    far_follow,
    qkv,
    w_qkv,
    value_bias,
    w_out,
    out_bias,
    gain1,
    shift1,
    w_up,
    up_bias,
    w_down,
    down_bias,
    gain2,
    shift2,
    w_proj,
    queries,
    kv,
    context,
    lse,
    cols,
    norm1,
    act,
    slope,
    norm2,
    proj,
    embed,
    tops,
    bias_scr,
):
    rows, local, far, window, length, width, row_count = dims
    w2 = 2 * width
    w_kv = w_qkv[:, width:]
    offset = local
    for r in range(rows):
        kv[r * window : r * window + local, :] = qkv[r * local : (r + 1) * local, width:]
    for piece, size in ((prev, local), (follow, local), (far_prev, far), (far_follow, far)):
        got = dot(piece[...], w_kv, 1, 0)
        got_k = got[:, :width].astype(bf16)
        got_v = (got[:, width:] + value_bias[...]).astype(bf16)
        for r in range(rows):
            at = r * window + offset
            kv[at : at + size, :width] = got_k[r * size : (r + 1) * size]
            kv[at : at + size, width:] = got_v[r * size : (r + 1) * size]
        offset += size
    even = lax.broadcasted_iota(jnp.int32, (local, 128), 1) < 64
    upper = lax.broadcasted_iota(jnp.int32, (128, local), 0) < 64
    pairs = width // 128
    for r in range(rows):
        bias_scr[...] = attention_bias(meta, r, local, far, window, length)
        for p in range(pairs):
            lanes = slice(p * 128, (p + 1) * 128)
            q2 = pair_rows(qkv[r * local : (r + 1) * local, lanes] * bf16(0.125), even)
            k2 = kv[r * window : (r + 1) * window, lanes]
            v2 = kv[r * window : (r + 1) * window, width + p * 128 : width + (p + 1) * 128]
            bias = bias_scr[...]
            s = dot(k2, q2, 1, 1) + jnp.concatenate([bias, bias], axis=1)
            top = jnp.max(s, axis=0, keepdims=True)
            e = jnp.exp(s - top)
            total = jnp.sum(e, axis=0, keepdims=True)
            lse[r * pairs + p : r * pairs + p + 1, :] = top + jnp.log(total)
            o = dot(v2, e.astype(bf16), 0, 0) * (1.0 / total)
            o = jnp.where(upper, o[:, :local], o[:, local:])
            context[r * local : (r + 1) * local, lanes] = o.T.astype(bf16)
    attended = dot(context[...], w_out[...], 1, 0) + out_bias[...]
    resid = x_own[...].astype(f32) + attended
    centred = resid - jnp.mean(resid, axis=-1, keepdims=True)
    rstd1 = lax.rsqrt(jnp.mean(centred * centred, axis=-1, keepdims=True) + LN_EPS)
    n1 = centred * rstd1
    norm1[...] = n1
    hidden1 = n1 * gain1[...] + shift1[...]
    hidden1_low = hidden1.astype(bf16)
    ffn = jnp.zeros(hidden1.shape, f32)
    step = 512
    for c in range(w_up.shape[1] // step):
        cut = slice(c * step, (c + 1) * step)
        up = dot(hidden1_low, w_up[:, cut], 1, 0) + up_bias[:, cut]
        cdf = 0.5 * (1.0 + lax.erf(up * (0.5**0.5)))
        act_low = (up * cdf).astype(bf16)
        act[:, cut] = act_low
        slope[:, cut] = (cdf + up * (jnp.exp(-0.5 * up * up) * 0.3989422804014327)).astype(bf16)
        ffn = ffn + dot(act_low, w_down[cut, :], 1, 0)
    resid = hidden1 + ffn + down_bias[...]
    centred = resid - jnp.mean(resid, axis=-1, keepdims=True)
    rstd2 = lax.rsqrt(jnp.mean(centred * centred, axis=-1, keepdims=True) + LN_EPS)
    n2 = centred * rstd2
    norm2[...] = n2
    lane = lax.broadcasted_iota(jnp.int32, cols.shape, 1)
    cols[...] = jnp.where(lane == 0, rstd1, rstd2)
    hidden2_low = (n2 * gain2[...] + shift2[...]).astype(bf16)
    out = dot(hidden2_low, w_proj[...], 1, 0)
    proj[...] = out
    inv = lax.rsqrt(jnp.sum(out * out, axis=-1, keepdims=True) + NORM_EPS)
    low = (out * inv).astype(bf16)
    embed[...] = low
    base = meta[0]
    for r in range(rows):
        sharp = dot(low[r * local : (r + 1) * local], queries[r // row_count], 1, 1) * SHARP
        seg = ident(base + lax.broadcasted_iota(jnp.int32, (local, 1), 0), meta, r, length)
        shift = jnp.zeros_like(sharp)
        for s in range(SEGS):
            inside = seg == s
            top = jnp.max(jnp.where(inside, sharp, MASKED), axis=0, keepdims=True)
            tops[r * SEGS + s : r * SEGS + s + 1, :] = top
            shift = jnp.where(inside, top, shift)
        e = jnp.exp(sharp - shift)
        for s in range(SEGS):
            at = rows * SEGS + r * SEGS + s
            tops[at : at + 1, :] = jnp.sum(
                jnp.where(seg == s, e, 0.0), axis=0, keepdims=True
            )


def score_kernel(dims, meta, first, second, third, fourth, positives, merged, score, stats):
    rows, length, row_count, query_tokens = dims
    half = rows * SEGS
    parts = [ref[...] for ref in (first, second, third, fourth)]
    tops = [part[:half] for part in parts]
    top = jnp.maximum(jnp.maximum(tops[0], tops[1]), jnp.maximum(tops[2], tops[3]))
    sums = [part[half:] * jnp.exp(part[:half] - top) for part in parts]
    total = (sums[0] + sums[1]) + (sums[2] + sums[3])
    merged[:half, :] = top
    merged[half:, :] = total
    sub = lax.broadcasted_iota(jnp.int32, (half, 1), 0)
    count = jnp.zeros((half, 1), f32)
    for r in range(rows):
        edges = [0] + [meta[2 + r * (SEGS - 1) + s] for s in range(SEGS - 1)] + [length]
        for s in range(SEGS):
            size = (edges[s + 1] - edges[s]).astype(f32)
            count = jnp.where(sub == r * SEGS + s, size, count)
    match = top + jnp.log(total) - jnp.log(count)
    wide = score.shape[1]
    shape = (match.shape[1], wide)
    group = (
        lax.broadcasted_iota(jnp.int32, shape, 0) // query_tokens
        == lax.broadcasted_iota(jnp.int32, shape, 1)
    ).astype(f32)
    got = dot(match, group, 1, 0, HIGH)
    score[...] = got
    per = row_count * SEGS
    micros = rows // row_count
    for m in range(micros):
        part = got[m * per : (m + 1) * per]
        at = lax.broadcasted_iota(jnp.int32, (per, wide), 0) + meta[1]
        chosen = at == positives[m : m + 1, :]
        best = jnp.max(part, axis=0, keepdims=True)
        stats[m : m + 1, :] = best
        stats[micros + m : micros + m + 1, :] = jnp.sum(
            jnp.exp(part - best), axis=0, keepdims=True
        )
        stats[2 * micros + m : 2 * micros + m + 1, :] = jnp.sum(
            jnp.where(chosen, part, 0.0), axis=0, keepdims=True
        )


def merge_kernel(micros, first, second, out):
    one, two = first[...], second[...]
    best = jnp.maximum(one[:micros], two[:micros])
    out[:micros, :] = best
    out[micros : 2 * micros, :] = one[micros : 2 * micros] * jnp.exp(one[:micros] - best) + two[
        micros : 2 * micros
    ] * jnp.exp(two[:micros] - best)
    out[2 * micros : 3 * micros, :] = one[2 * micros : 3 * micros] + two[2 * micros : 3 * micros]


def upper_kernel(
    dims,
    meta,
    merged,
    score,
    stats,
    positives,
    queries,
    embed,
    proj,
    norm2,
    cols,
    gain2,
    shift2,
    w_proj,
    act,
    loss,
    d_proj,
    d_down,
    g_resid2,
    g_ffn,
    vec,
):
    rows, local, length, row_count, query_tokens = dims
    half = rows * SEGS
    micros = rows // row_count
    per = row_count * SEGS
    wide = score.shape[1]
    all_queries = merged.shape[1]
    shape = (wide, all_queries)
    group = (
        lax.broadcasted_iota(jnp.int32, shape, 1) // query_tokens
        == lax.broadcasted_iota(jnp.int32, shape, 0)
    ).astype(f32)
    parts = []
    for m in range(micros):
        best = stats[m : m + 1, :]
        total = stats[micros + m : micros + m + 1, :]
        loss[m : m + 1, :] = best + jnp.log(total) - stats[2 * micros + m : 2 * micros + m + 1, :]
        part = score[m * per : (m + 1) * per, :]
        at = lax.broadcasted_iota(jnp.int32, (per, wide), 0) + meta[1]
        chosen = (at == positives[m : m + 1, :]).astype(f32)
        parts.append(jnp.exp(part - best) / total - chosen)
    g_match = dot(jnp.concatenate(parts, axis=0), group, 1, 0, HIGH)
    factor = SHARP * g_match / merged[half:, :]
    base = meta[0]
    pieces = []
    for r in range(rows):
        m = r // row_count
        low = embed[r * local : (r + 1) * local, :]
        sharp = dot(low, queries[m], 1, 1) * SHARP
        seg = ident(base + lax.broadcasted_iota(jnp.int32, (local, 1), 0), meta, r, length)
        shift = jnp.zeros_like(sharp)
        scale = jnp.zeros_like(sharp)
        for s in range(SEGS):
            at = r * SEGS + s
            shift = jnp.where(seg == s, merged[at : at + 1, :], shift)
            scale = jnp.where(seg == s, factor[at : at + 1], scale)
        g_sim = (scale * jnp.exp(sharp - shift)).astype(bf16)
        pieces.append(dot(g_sim, queries[m], 1, 0))
    g_unit = jnp.concatenate(pieces, axis=0)
    out = proj[...]
    inv = lax.rsqrt(jnp.sum(out * out, axis=-1, keepdims=True) + NORM_EPS)
    unit = out * inv
    g_proj = ((g_unit - unit * jnp.sum(unit * g_unit, axis=-1, keepdims=True)) * inv).astype(bf16)
    n2 = norm2[...]
    hidden2_low = (n2 * gain2[...] + shift2[...]).astype(bf16)
    d_proj[...] = dot(hidden2_low, g_proj, 0, 0).astype(bf16)
    g_hidden = dot(g_proj, w_proj[...], 1, 1)
    vec[0:1, :] = jnp.sum(g_hidden * n2, axis=0, keepdims=True)
    vec[1:2, :] = jnp.sum(g_hidden, axis=0, keepdims=True)
    g_n = g_hidden * gain2[...]
    g_v = cols[:, 1:2] * (
        g_n
        - jnp.mean(g_n, axis=-1, keepdims=True)
        - n2 * jnp.mean(g_n * n2, axis=-1, keepdims=True)
    )
    g_resid2[...] = g_v
    low = g_v.astype(bf16)
    g_ffn[...] = low
    vec[2:3, :] = jnp.sum(low.astype(f32), axis=0, keepdims=True)
    step = 768
    for c in range(act.shape[1] // step):
        d_down[c * step : (c + 1) * step, :] = dot(
            act[:, c * step : (c + 1) * step], low, 0, 0
        ).astype(bf16)


def middle_kernel(
    g_ffn, g_resid2, w_down, w_up, slope, norm1, cols, gain1, shift1, d_up, g_resid1, vec, d_ubias
):
    low = g_ffn[...]
    n1 = norm1[...]
    hidden1_low = (n1 * gain1[...] + shift1[...]).astype(bf16)
    g_hidden = g_resid2[...]
    step = 768
    for c in range(w_up.shape[1] // step):
        cut = slice(c * step, (c + 1) * step)
        g_act = dot(low, w_down[cut, :], 1, 1)
        g_up = (g_act * slope[:, cut].astype(f32)).astype(bf16)
        d_ubias[:, cut] = jnp.sum(g_up.astype(f32), axis=0, keepdims=True)
        d_up[:, cut] = dot(hidden1_low, g_up, 0, 0).astype(bf16)
        g_hidden = g_hidden + dot(g_up, w_up[:, cut], 1, 1)
    vec[0:1, :] = jnp.sum(g_hidden * n1, axis=0, keepdims=True)
    vec[1:2, :] = jnp.sum(g_hidden, axis=0, keepdims=True)
    g_n = g_hidden * gain1[...]
    g_v = cols[:, 0:1] * (
        g_n
        - jnp.mean(g_n, axis=-1, keepdims=True)
        - n1 * jnp.mean(g_n * n1, axis=-1, keepdims=True)
    )
    g_resid1[...] = g_v
    vec[2:3, :] = jnp.sum(g_v.astype(bf16).astype(f32), axis=0, keepdims=True)


def attention_kernel(
    dims,
    meta,
    g_resid1,
    context,
    w_out,
    qkv,
    kv,
    lse,
    w_qkv,
    g_own,
    g_halo,
    g_query,
    g_kv,
    d_out,
    vec,
    g_ctx_scr,
    bias_scr,
):
    rows, local, far, window, length, width = dims
    pairs = width // 128
    low = g_resid1[...].astype(bf16)
    g_ctx_scr[...] = dot(low, w_out[...], 1, 1).astype(bf16)
    d_out[...] = dot(context[...], low, 0, 0).astype(bf16)
    even = lax.broadcasted_iota(jnp.int32, (local, 128), 1) < 64
    upper = lax.broadcasted_iota(jnp.int32, (128, local), 0) < 64
    for r in range(rows):
        bias_scr[...] = attention_bias(meta, r, local, far, window, length)
        own = slice(r * local, (r + 1) * local)
        win = slice(r * window, (r + 1) * window)
        for p in range(pairs):
            lanes = slice(p * 128, (p + 1) * 128)
            vlanes = slice(width + p * 128, width + (p + 1) * 128)
            q2 = pair_rows(qkv[own, lanes] * bf16(0.125), even)
            k2 = kv[win, lanes]
            v2 = kv[win, vlanes]
            gc2 = pair_rows(g_ctx_scr[own, lanes], even)
            bias = bias_scr[...]
            s = dot(k2, q2, 1, 1) + jnp.concatenate([bias, bias], axis=1)
            prob = jnp.exp(s - lse[r * pairs + p : r * pairs + p + 1, :])
            g_prob = dot(v2, gc2, 1, 1)
            weighted = prob * g_prob
            inner = jnp.sum(weighted, axis=0, keepdims=True)
            g_score = (weighted - prob * inner).astype(bf16)
            g_kv[win, vlanes] = dot(prob.astype(bf16), gc2, 1, 0).astype(bf16)
            g_kv[win, lanes] = dot(g_score, q2, 1, 0).astype(bf16)
            g_q = dot(k2, g_score, 0, 0)
            g_q = jnp.where(upper, g_q[:, :local], g_q[:, local:]) * 0.125
            g_query[own, lanes] = g_q.T.astype(bf16)
    vec[:, :width] = jnp.sum(g_query[...].astype(f32), axis=0, keepdims=True)
    vec[:, width:] = jnp.sum(g_kv[:, width:].astype(f32), axis=0, keepdims=True)
    back_q = dot(g_query[...], w_qkv[:, :width], 1, 1)
    for r in range(rows):
        own = slice(r * local, (r + 1) * local)
        back = dot(g_kv[r * window : (r + 1) * window, :], w_qkv[:, width:], 1, 1)
        g_own[own, :] = g_resid1[own, :] + back_q[own] + back[:local]
        g_halo[r * (window - local) : (r + 1) * (window - local), :] = back[local:].astype(bf16)


def weight_kernel(dims, x_own, prev, follow, far_prev, far_follow, g_query, g_kv, d_qkv):
    rows, local, far, window, width = dims
    w3 = 3 * width
    d_qkv[:, :width] = dot(x_own[...], g_query[...], 0, 0).astype(bf16)
    step = width // 2
    for c in range(4):
        cut = slice(c * step, (c + 1) * step)
        total = None
        offset = 0
        for piece, size in (
            (x_own, local),
            (prev, local),
            (follow, local),
            (far_prev, far),
            (far_follow, far),
        ):
            grads = jnp.concatenate(
                [
                    g_kv[r * window + offset : r * window + offset + size, cut]
                    for r in range(rows)
                ],
                axis=0,
            )
            part = dot(piece[...], grads, 0, 0)
            total = part if total is None else total + part
            offset += size
        d_qkv[:, width + c * step : width + (c + 1) * step] = total.astype(bf16)


def call(kernel, outs, ins, scratch=(), smem=1, name=None):
    return pl.pallas_call(
        kernel,
        out_shape=tuple(jax.ShapeDtypeStruct(shape, kind) for shape, kind in outs),
        in_specs=[SMEM] * smem + [VMEM] * (len(ins) - smem),
        out_specs=tuple([VMEM] * len(outs)),
        scratch_shapes=list(scratch),
        compiler_params=PARAMS,
        name=name,
    )(*ins)


def halve(grad, bit, dp_pos, dp_count):
    mine_at = (dp_pos // bit) % 2
    mine = lax.dynamic_index_in_dim(grad, mine_at, 1, keepdims=False)
    other = lax.dynamic_index_in_dim(grad, 1 - mine_at, 1, keepdims=False)
    recv = swap(other, "dp", bit, dp_count)
    return (mine.astype(f32) + recv.astype(f32)).astype(bf16)


def reduce_dp(grad, order, dp_pos, dp_count):
    tail = grad.shape[1:]
    left = sorted(bits_of(dp_count))
    for bit in order:
        low = len([b for b in left if b < bit])
        high = len(left) - low - 1
        g = grad.reshape((1 << high, 2, 1 << low) + tail)
        grad = halve(g, bit, dp_pos, dp_count)
        left.remove(bit)
    return grad.reshape(tail)


def reduce_seq(grad, seq_pos, seq_count):
    total = lax.dynamic_index_in_dim(grad, seq_pos, 0, keepdims=False).astype(f32)
    for step in range(1, seq_count):
        piece = lax.dynamic_index_in_dim(grad, (seq_pos + step) % seq_count, 0, keepdims=False)
        recv = lax.ppermute(piece, "seq", [(i, (i + step) % seq_count) for i in range(seq_count)])
        total = total + recv.astype(f32)
    return total


def body(
    hidden_in,
    segment_ids,
    query_emb,
    positives,
    w_qkv,
    query_bias,
    value_bias,
    w_out,
    out_bias,
    norm1_gain,
    norm1_bias,
    w_up,
    up_bias,
    w_down,
    down_bias,
    norm2_gain,
    norm2_bias,
    w_proj,
):
    micro_count, row_count, local_len, width = hidden_in.shape
    full_len = segment_ids.shape[2]
    embed_width = w_proj.shape[1]
    ff = w_up.shape[1]
    queries_local = query_emb.shape[1]
    query_tokens = query_emb.shape[2]
    seq_count = lax.axis_size("seq")
    dp_count = lax.axis_size("dp")
    seq_pos = lax.axis_index("seq")
    dp_pos = lax.axis_index("dp")
    rows = micro_count * row_count
    tokens = rows * local_len
    far = 64
    window = 3 * local_len + 2 * far
    assert local_len + far >= PASSAGE_MOST - 1 and seq_count == 4

    x_own = hidden_in.reshape(rows, local_len, width)
    follow = shifted(x_own, "seq", -1, seq_count)
    prev = shifted(x_own, "seq", 1, seq_count)
    far_follow = shifted(x_own[:, :far], "seq", -2, seq_count)
    far_prev = shifted(x_own[:, local_len - far :], "seq", 2, seq_count)
    pieces = [
        part.reshape(-1, width) for part in (prev, follow, far_prev, far_follow)
    ]
    x_flat = x_own.reshape(tokens, width)

    seg_full = segment_ids.reshape(rows, full_len)
    edges = jnp.sum(
        (seg_full[:, None, :] < jnp.arange(1, SEGS, dtype=jnp.int32)[None, :, None]).astype(
            jnp.int32
        ),
        axis=2,
    )
    meta = jnp.concatenate(
        [
            jnp.stack([seq_pos * local_len, dp_pos * row_count * SEGS]).astype(jnp.int32),
            edges.reshape(-1),
        ]
    )

    queries = query_emb.reshape(micro_count, queries_local * query_tokens, embed_width)
    for bit in bits_of(dp_count):
        recv = swap(queries, "dp", bit, dp_count)
        upper = (dp_pos // bit) % 2
        queries = jnp.where(
            upper == 0,
            jnp.concatenate([queries, recv], axis=1),
            jnp.concatenate([recv, queries], axis=1),
        )
    query_all = queries.shape[1]
    query_count = query_all // query_tokens
    wide = max(128, query_count)
    positives_wide = jnp.pad(
        positives, ((0, 0), (0, wide - query_count)), constant_values=-1
    )

    qkv_bias = jnp.concatenate([query_bias, jnp.zeros((width,), f32), value_bias])
    qkv = (jnp.dot(x_flat, w_qkv, preferred_element_type=f32) + qkv_bias).astype(bf16)

    def line(vector):
        return vector.reshape(1, -1)

    pairs = width // 128
    kv, context, lse, cols, norm1, act, slope, norm2, proj, embed, tops = call(
        functools.partial(
            forward_kernel, (rows, local_len, far, window, full_len, width, row_count)
        ),
        [
            ((rows * window, 2 * width), bf16),
            ((tokens, width), bf16),
            ((rows * pairs, 2 * local_len), f32),
            ((tokens, 128), f32),
            ((tokens, width), f32),
            ((tokens, ff), bf16),
            ((tokens, ff), bf16),
            ((tokens, width), f32),
            ((tokens, embed_width), f32),
            ((tokens, embed_width), bf16),
            ((2 * rows * SEGS, query_all), f32),
        ],
        [
            meta,
            x_flat,
            *pieces,
            qkv,
            w_qkv,
            line(value_bias),
            w_out,
            line(out_bias),
            line(norm1_gain),
            line(norm1_bias),
            w_up,
            line(up_bias),
            w_down,
            line(down_bias),
            line(norm2_gain),
            line(norm2_bias),
            w_proj,
            queries,
        ],
        [pltpu.VMEM((window, local_len), f32)],
        name="forward",
    )

    others = [swap(tops, "seq", bit, seq_count) for bit in (1, 2, 3)]
    stat_rows = 8
    merged, score, stats = call(
        functools.partial(score_kernel, (rows, full_len, row_count, query_tokens)),
        [
            ((2 * rows * SEGS, query_all), f32),
            ((rows * SEGS, wide), f32),
            ((stat_rows, wide), f32),
        ],
        [meta, tops, *others, positives_wide],
        name="score",
    )
    for bit in bits_of(dp_count):
        recv = swap(stats, "dp", bit, dp_count)
        (stats,) = call(
            functools.partial(merge_kernel, micro_count),
            [((stat_rows, wide), f32)],
            [stats, recv],
            smem=0,
            name="merge",
        )

    loss, d_proj, d_down, g_resid2, g_ffn, vec_c = call(
        functools.partial(upper_kernel, (rows, local_len, full_len, row_count, query_tokens)),
        [
            ((micro_count, wide), f32),
            ((width, embed_width), bf16),
            ((ff, width), bf16),
            ((tokens, width), f32),
            ((tokens, width), bf16),
            ((8, width), f32),
        ],
        [
            meta,
            merged,
            score,
            stats,
            positives_wide,
            queries,
            embed,
            proj,
            norm2,
            cols,
            line(norm2_gain),
            line(norm2_bias),
            w_proj,
            act,
        ],
        name="upper",
    )
    losses = lax.dynamic_slice_in_dim(loss, dp_pos * queries_local, queries_local, 1)

    d_up, g_resid1, vec_d, d_ubias = call(
        middle_kernel,
        [
            ((width, ff), bf16),
            ((tokens, width), f32),
            ((8, width), f32),
            ((1, ff), f32),
        ],
        [
            g_ffn,
            g_resid2,
            w_down,
            w_up,
            slope,
            norm1,
            cols,
            line(norm1_gain),
            line(norm1_bias),
        ],
        smem=0,
        name="middle",
    )

    halo = window - local_len
    g_own, g_halo, g_query, g_kv, d_out, vec_e = call(
        functools.partial(
            attention_kernel, (rows, local_len, far, window, full_len, width)
        ),
        [
            ((tokens, width), f32),
            ((rows * halo, width), bf16),
            ((tokens, width), bf16),
            ((rows * window, 2 * width), bf16),
            ((width, width), bf16),
            ((1, 2 * width), f32),
        ],
        [meta, g_resid1, context, w_out, qkv, kv, lse, w_qkv],
        [pltpu.VMEM((tokens, width), bf16), pltpu.VMEM((window, local_len), f32)],
        name="attention",
    )
    back = g_halo.reshape(rows, halo, width)
    to_prev = shifted(back[:, :local_len], "seq", -1, seq_count)
    to_follow = shifted(back[:, local_len : 2 * local_len], "seq", 1, seq_count)
    to_far_prev = shifted(back[:, 2 * local_len : 2 * local_len + far], "seq", -2, seq_count)
    to_far_follow = shifted(back[:, 2 * local_len + far :], "seq", 2, seq_count)
    grad_in = (
        g_own.reshape(rows, local_len, width)
        + to_prev.astype(f32)
        + to_follow.astype(f32)
        + jnp.pad(to_far_prev.astype(f32), ((0, 0), (local_len - far, 0), (0, 0)))
        + jnp.pad(to_far_follow.astype(f32), ((0, 0), (0, local_len - far), (0, 0)))
    )
    (d_qkv,) = call(
        functools.partial(weight_kernel, (rows, local_len, far, window, width)),
        [((width, 3 * width), bf16)],
        [x_flat, *pieces, g_query, g_kv],
        smem=0,
        name="weight",
    )

    devices = dp_count * seq_count
    lower_vec = jnp.concatenate([vec_e[0], vec_d[2], vec_d[0]])
    upper_vec = jnp.concatenate([vec_d[1], vec_c[2], vec_c[0], vec_c[1], d_ubias[0]])
    vec = jnp.concatenate(
        [lower_vec.reshape(devices, -1), upper_vec.reshape(devices, -1)], axis=1
    )
    bits = bits_of(dp_count)
    order_a = bits
    order_b = bits[:1] + bits[1:][::-1]

    def reduced(grad, cut):
        part = grad.reshape(dp_count, seq_count, grad.shape[0] // devices, -1)
        first = reduce_dp(part[..., :cut], order_a, dp_pos, dp_count)
        second = reduce_dp(part[..., cut:], order_b, dp_pos, dp_count)
        return reduce_seq(jnp.concatenate([first, second], axis=-1), seq_pos, seq_count)

    down_part = reduced(d_down, width // 2)
    up_part = reduced(d_up, ff // 2)
    vec_rows = vec.reshape(width, -1)
    vec_rows = jnp.pad(vec_rows, ((0, 0), (0, 128 - vec_rows.shape[1]))).astype(bf16)
    last = reduced(jnp.concatenate([d_qkv, d_out, d_proj, vec_rows], axis=1), 1664)
    at = 3 * width
    qkv_part = last[:, :at]
    out_part = last[:, at : at + width]
    proj_part = last[:, at + width : at + width + embed_width]
    vec_part = last[:, at + width + embed_width :][:, : vec.size // width].reshape(-1)
    lower_size = lower_vec.size // devices
    return (
        embed.reshape(micro_count, row_count, local_len, embed_width),
        losses,
        grad_in.reshape(micro_count, row_count, local_len, width),
        qkv_part.reshape(-1),
        out_part.reshape(-1),
        up_part.reshape(-1),
        down_part.reshape(-1),
        proj_part.reshape(-1),
        vec_part[:lower_size],
        vec_part[lower_size:],
    )


def solution(mesh):
    in_specs = (
        P(None, "dp", "seq", None),
        P(None, "dp", None),
        P(None, "dp", None, None),
    ) + (P(),) * 15
    out_specs = (
        P(None, "dp", "seq", None),
        P(None, "dp"),
        P(None, "dp", "seq", None),
    ) + (P(("dp", "seq")),) * 7
    return jax.shard_map(body, mesh=mesh, in_specs=in_specs, out_specs=out_specs, check_vma=False)
```

```python
import functools

import jax
import jax.numpy as jnp
from jax import lax
from jax.experimental import pallas as pl
from jax.experimental.pallas import tpu as pltpu
from jax.sharding import PartitionSpec as P

HEADS = 12
SEGS = 4
PASSAGE_MOST = 180

SHARP = 20.0
EDGES = 7
COST = 1e6
LN_EPS = 1e-12
NORM_EPS = 1e-12
MASKED = -1e30
HIGH = lax.Precision.HIGHEST
bf16 = jnp.bfloat16
f32 = jnp.float32
VMEM = pl.BlockSpec(memory_space=pltpu.VMEM)
HBM = pl.BlockSpec(memory_space=pl.ANY)
SMEM = pl.BlockSpec(memory_space=pltpu.SMEM)
PARAMS = pltpu.CompilerParams(vmem_limit_bytes=58 << 20)


def bits_of(count):
    return [1 << k for k in range(count.bit_length() - 1)]


def swap(value, axis, bit, count):
    return lax.ppermute(value, axis, [(i, i ^ bit) for i in range(count)])


def shifted(value, axis, step, count):
    return lax.ppermute(value, axis, [(i, i + step) for i in range(count) if 0 <= i + step < count])


def dot(left, right, left_dim, right_dim, precision=None):
    return lax.dot_general(
        left,
        right,
        (((left_dim,), (right_dim,)), ((), ())),
        precision=precision,
        preferred_element_type=f32,
    )


def ident(pos, meta, row, length):
    seg = jnp.zeros(pos.shape, jnp.int32)
    for s in range(SEGS - 1):
        seg = seg + (pos >= meta[EDGES + row * (SEGS - 1) + s]).astype(jnp.int32)
    return jnp.where((pos >= 0) & (pos < length), seg, -1)


def key_positions(meta, local, shape):
    w = lax.broadcasted_iota(jnp.int32, shape, 0)
    pos = meta[0] + w
    for piece in range(1, 4):
        pos = jnp.where(w >= piece * local, meta[1 + piece] + w - piece * local, pos)
    return pos


def pair_rows(block, even):
    zero = jnp.zeros_like(block)
    return jnp.concatenate([jnp.where(even, block, zero), jnp.where(even, zero, block)], axis=0)


def attention_bias(meta, row, local, window, length):
    key_seg = ident(key_positions(meta, local, (window, local)), meta, row, length)
    query_seg = ident(
        meta[0] + lax.broadcasted_iota(jnp.int32, (window, local), 1), meta, row, length
    )
    return jnp.where(key_seg == query_seg, 0.0, MASKED).astype(f32)


def copy_out(scr, outs, sems, first, core, columns, part=None):
    copies = []
    start, size = part or (0, scr.shape[0])
    if len(outs) == 1:
        rows = pl.ds(start, size)
        copies.append((scr.at[rows, :], outs[0].at[rows, columns]))
    else:
        high, block, _ = outs[0].shape
        for i in range(high):
            if not start <= 2 * i * block < start + size:
                continue
            for out, which in ((outs[0], 1 - core), (outs[1], core)):
                rows = pl.ds(pl.multiple_of((2 * i + which) * block, 16), block)
                copies.append((scr.at[rows, :], out.at[i, :, columns]))
    started = []
    for n, (source, target) in enumerate(copies):
        copy = pltpu.make_async_copy(source, target, sems.at[first + n])
        copy.start()
        started.append(copy)
    return started


def forward_kernel(
    dims,
    meta,
    x_own,
    side,
    middle,
    far_part,
    qkv,
    vectors,
    w_proj,
    queries,
    w_qkv_hbm,
    w_out_hbm,
    w_up_hbm,
    w_down_hbm,
    context_t,
    lse,
    cols,
    norm2,
    hidden2_t,
    proj,
    embed,
    parts,
    kv_hbm,
    x_t_hbm,
    norm1_hbm,
    hidden1_t_hbm,
    act_t_hbm,
    slope_hbm,
    bias_scr,
    context,
    w_kv,
    w_out,
    w_up,
    w_down,
    kv,
    x_t,
    norm1,
    hidden1_t,
    act_t,
    slope,
    sems,
):
    rows, local, far, window, length, width, row_count = dims
    value_bias = vectors[0 : 1, :]
    out_bias = vectors[1 : 2, :]
    gain1 = vectors[2 : 3, :]
    shift1 = vectors[3 : 4, :]
    down_bias = vectors[4 : 5, :]
    gain2 = vectors[5 : 6, :]
    shift2 = vectors[6 : 7, :]
    step = width
    chunks = w_up.shape[1] // step
    started = []

    def begin(source, target):
        copy = pltpu.make_async_copy(source, target, sems.at[len(started)])
        copy.start()
        started.append(copy)
        return copy

    kv_here = begin(w_qkv_hbm.at[:, pl.ds(width, 2 * width)], w_kv)
    out_here = begin(w_out_hbm, w_out)
    up_here, down_here = [], []
    for c in range(chunks):
        cut = slice(c * step, (c + 1) * step)
        up_here.append(begin(w_up_hbm.at[:, cut], w_up.at[:, cut]))
        down_here.append(begin(w_down_hbm.at[cut, :], w_down.at[cut, :]))
    leaving = []
    for r in range(rows):
        kv[r, :local, :] = qkv[r * local : (r + 1) * local, width:]
        x_t[r, :, :local] = x_own[r * local : (r + 1) * local, :].T
    offset = local
    kv_here.wait()
    for piece, size in ((side, local), (middle, local), (far_part, far)):
        got = dot(piece[...], w_kv[...], 1, 0)
        got_k = got[:, :width].astype(bf16)
        got_v = (got[:, width:] + value_bias).astype(bf16)
        for r in range(rows):
            mine = slice(r * size, (r + 1) * size)
            kv[r, offset : offset + size, :width] = got_k[mine]
            kv[r, offset : offset + size, width:] = got_v[mine]
            x_t[r, :, offset : offset + size] = piece[mine, :].T
        offset += size
    leaving.append(begin(kv, kv_hbm))
    leaving.append(begin(x_t, x_t_hbm))
    even = lax.broadcasted_iota(jnp.int32, (local, 128), 1) < 64
    upper = lax.broadcasted_iota(jnp.int32, (128, local), 0) < 64
    pairs = width // 128
    for r in range(rows):
        bias_scr[...] = attention_bias(meta, r, local, window, length)
        own = slice(r * local, (r + 1) * local)
        for p in range(pairs):
            lanes = slice(p * 128, (p + 1) * 128)
            q2 = pair_rows(qkv[own, lanes] * bf16(0.125), even)
            k2 = kv[r, :, lanes]
            v2 = kv[r, :, width + p * 128 : width + (p + 1) * 128]
            bias = bias_scr[...]
            s = dot(k2, q2, 1, 1) + jnp.concatenate([bias, bias], axis=1)
            top = jnp.max(s, axis=0, keepdims=True)
            e = jnp.exp(s - top)
            total = jnp.sum(e, axis=0, keepdims=True)
            lse[r * pairs + p : r * pairs + p + 1, :] = top + jnp.log(total)
            o = dot(v2, e.astype(bf16), 0, 0) * (1.0 / total)
            o = jnp.where(upper, o[:, :local], o[:, local:])
            context_t[lanes, own] = o.astype(bf16)
            context[own, lanes] = o.T.astype(bf16)
    out_here.wait()
    attended = dot(context[...], w_out[...], 1, 0) + out_bias
    resid = x_own[...].astype(f32) + attended
    centred = resid - jnp.mean(resid, axis=-1, keepdims=True)
    rstd1 = lax.rsqrt(jnp.mean(centred * centred, axis=-1, keepdims=True) + LN_EPS)
    n1 = centred * rstd1
    norm1[...] = n1
    leaving.append(begin(norm1, norm1_hbm))
    hidden1 = n1 * gain1 + shift1
    hidden1_low = hidden1.astype(bf16)
    hidden1_t[...] = hidden1_low.T
    leaving.append(begin(hidden1_t, hidden1_t_hbm))
    ffn = jnp.zeros(hidden1.shape, f32)
    for c in range(chunks):
        cut = slice(c * step, (c + 1) * step)
        up_here[c].wait()
        up = dot(hidden1_low, w_up[:, cut], 1, 0) + vectors[7 + c : 8 + c, :]
        cdf = 0.5 * (1.0 + lax.erf(up * (0.5**0.5)))
        act_low = (up * cdf).astype(bf16)
        act_t[cut, :] = act_low.T
        leaving.append(begin(act_t.at[cut, :], act_t_hbm.at[cut, :]))
        slope[:, cut] = (cdf + up * (jnp.exp(-0.5 * up * up) * 0.3989422804014327)).astype(bf16)
        leaving.append(begin(slope.at[:, cut], slope_hbm.at[:, cut]))
        down_here[c].wait()
        ffn = ffn + dot(act_low, w_down[cut, :], 1, 0)
    resid = hidden1 + ffn + down_bias
    centred = resid - jnp.mean(resid, axis=-1, keepdims=True)
    rstd2 = lax.rsqrt(jnp.mean(centred * centred, axis=-1, keepdims=True) + LN_EPS)
    n2 = centred * rstd2
    norm2[...] = n2
    lane = lax.broadcasted_iota(jnp.int32, cols.shape, 1)
    cols[...] = jnp.where(lane == 0, rstd1, rstd2)
    hidden2_low = (n2 * gain2 + shift2).astype(bf16)
    hidden2_t[...] = hidden2_low.T
    out = dot(hidden2_low, w_proj[...], 1, 0)
    proj[...] = out
    inv = lax.rsqrt(jnp.sum(out * out, axis=-1, keepdims=True) + NORM_EPS)
    low = (out * inv).astype(bf16)
    embed[...] = low
    base = meta[0]
    for r in range(rows):
        sharp = dot(low[r * local : (r + 1) * local], queries[r // row_count], 1, 1) * SHARP
        seg = ident(base + lax.broadcasted_iota(jnp.int32, (local, 1), 0), meta, r, length)
        tops = []
        shift = jnp.zeros_like(sharp)
        for s in range(SEGS):
            inside = seg == s
            top = jnp.max(jnp.where(inside, sharp, MASKED), axis=0, keepdims=True)
            tops.append(top)
            shift = jnp.where(inside, top, shift)
        e = jnp.exp(sharp - shift)
        for s in range(SEGS):
            total = jnp.sum(jnp.where(seg == s, e, 0.0), axis=0, keepdims=True)
            some = total > 0.0
            parts[r * SEGS + s : r * SEGS + s + 1, :] = jnp.where(
                some, tops[s] + jnp.log(jnp.where(some, total, 1.0)), MASKED
            )
    for copy in leaving:
        copy.wait()


def score_kernel(dims, meta, first, second, third, fourth, positives, merged, score, stats):
    rows, length, row_count, query_tokens = dims
    half = rows * SEGS
    parts = [ref[...] for ref in (first, second, third, fourth)]
    top = jnp.maximum(jnp.maximum(parts[0], parts[1]), jnp.maximum(parts[2], parts[3]))
    sums = [jnp.exp(part - top) for part in parts]
    whole = top + jnp.log((sums[0] + sums[1]) + (sums[2] + sums[3]))
    merged[...] = whole
    sub = lax.broadcasted_iota(jnp.int32, (half, 1), 0)
    count = jnp.zeros((half, 1), f32)
    for r in range(rows):
        edges = [0] + [meta[EDGES + r * (SEGS - 1) + s] for s in range(SEGS - 1)] + [length]
        for s in range(SEGS):
            size = (edges[s + 1] - edges[s]).astype(f32)
            count = jnp.where(sub == r * SEGS + s, size, count)
    match = whole - jnp.log(count)
    wide = score.shape[1]
    shape = (match.shape[1], wide)
    group = (
        lax.broadcasted_iota(jnp.int32, shape, 0) // query_tokens
        == lax.broadcasted_iota(jnp.int32, shape, 1)
    ).astype(f32)
    got = dot(match, group, 1, 0, HIGH)
    score[...] = got
    per = row_count * SEGS
    micros = rows // row_count
    stats[...] = jnp.zeros(stats.shape, f32)
    for m in range(micros):
        part = got[m * per : (m + 1) * per]
        at = lax.broadcasted_iota(jnp.int32, (per, wide), 0) + meta[5]
        chosen = at == positives[m : m + 1, :]
        best = jnp.max(part, axis=0, keepdims=True)
        stats[m : m + 1, :] = best + jnp.log(
            jnp.sum(jnp.exp(part - best), axis=0, keepdims=True)
        )
        stats[micros + m : micros + m + 1, :] = jnp.sum(
            jnp.where(chosen, part, 0.0), axis=0, keepdims=True
        )


def upper_kernel(
    dims,
    outs_down,
    meta,
    merged,
    score,
    stats,
    positives,
    queries,
    embed,
    proj,
    norm2,
    hidden2_t,
    cols,
    vectors,
    w_proj,
    act_t_hbm,
    loss,
    d_proj,
    g_resid2,
    vec,
    *rest,
):
    down_outs, (scr, act_t, sems) = rest[:outs_down], rest[outs_down:]
    gain2 = vectors[5:6, :]
    act_here = pltpu.make_async_copy(act_t_hbm, act_t, sems.at[sems.shape[0] - 1])
    act_here.start()
    rows, local, length, row_count, query_tokens = dims
    micros = rows // row_count
    per = row_count * SEGS
    wide = score.shape[1]
    all_queries = merged.shape[1]
    shape = (wide, all_queries)
    group = (
        lax.broadcasted_iota(jnp.int32, shape, 1) // query_tokens
        == lax.broadcasted_iota(jnp.int32, shape, 0)
    ).astype(f32)
    pieces = []
    for m in range(micros):
        whole = stats[m : m + 1, :]
        loss[m : m + 1, :] = whole - stats[micros + m : micros + m + 1, :]
        part = score[m * per : (m + 1) * per, :]
        at = lax.broadcasted_iota(jnp.int32, (per, wide), 0) + meta[5]
        chosen = (at == positives[m : m + 1, :]).astype(f32)
        pieces.append(jnp.exp(part - whole) - chosen)
    factor = SHARP * dot(jnp.concatenate(pieces, axis=0), group, 1, 0, HIGH)
    base = meta[0]
    pieces = []
    for r in range(rows):
        m = r // row_count
        low = embed[r * local : (r + 1) * local, :]
        sharp = dot(low, queries[m], 1, 1) * SHARP
        seg = ident(base + lax.broadcasted_iota(jnp.int32, (local, 1), 0), meta, r, length)
        shift = jnp.zeros_like(sharp)
        scale = jnp.zeros_like(sharp)
        for s in range(SEGS):
            at = r * SEGS + s
            shift = jnp.where(seg == s, merged[at : at + 1, :], shift)
            scale = jnp.where(seg == s, factor[at : at + 1], scale)
        g_sim = (scale * jnp.exp(sharp - shift)).astype(bf16)
        pieces.append(dot(g_sim, queries[m], 1, 0))
    g_unit = jnp.concatenate(pieces, axis=0)
    out = proj[...]
    inv = lax.rsqrt(jnp.sum(out * out, axis=-1, keepdims=True) + NORM_EPS)
    unit = out * inv
    g_proj = ((g_unit - unit * jnp.sum(unit * g_unit, axis=-1, keepdims=True)) * inv).astype(bf16)
    n2 = norm2[...]
    d_proj[...] = dot(hidden2_t[...], g_proj, 1, 0).astype(bf16)
    g_hidden = dot(g_proj, w_proj[...], 1, 1)
    vec[0:1, :] = jnp.sum(g_hidden * n2, axis=0, keepdims=True)
    vec[1:2, :] = jnp.sum(g_hidden, axis=0, keepdims=True)
    g_n = g_hidden * gain2
    g_v = cols[:, 1:2] * (
        g_n
        - jnp.mean(g_n, axis=-1, keepdims=True)
        - n2 * jnp.mean(g_n * n2, axis=-1, keepdims=True)
    )
    g_resid2[...] = g_v
    low = g_v.astype(bf16)
    vec[2:3, :] = jnp.sum(low.astype(f32), axis=0, keepdims=True)
    act_here.wait()
    step = 768
    copies = []
    for c in range(act_t.shape[0] // step):
        cut = slice(c * step, (c + 1) * step)
        scr[cut, :] = dot(act_t[cut, :], low, 1, 0).astype(bf16)
        copies += copy_out(
            scr, down_outs, sems, len(copies), meta[6], slice(0, scr.shape[1]), (c * step, step)
        )
    for copy in copies:
        copy.wait()


def gate_kernel(count, meta, g_resid2, hidden1_t, w_down_hbm, slope_hbm, d_ubias, g_up_hbm, *rest):
    outs, (scr, w_down, slope, g_up, sems) = rest[:count], rest[count:]
    step = 768
    chunks = w_down.shape[0] // step
    here = []
    for c in range(chunks):
        cut = slice(c * step, (c + 1) * step)
        here.append(pltpu.make_async_copy(w_down_hbm.at[cut, :], w_down.at[cut, :], sems.at[3 * c]))
        here.append(
            pltpu.make_async_copy(slope_hbm.at[:, cut], slope.at[:, cut], sems.at[3 * c + 1])
        )
    for copy in here:
        copy.start()
    low = g_resid2[...].astype(bf16)
    h_t = hidden1_t[...]
    copies = []
    first = 3 * chunks
    for c in range(chunks):
        cut = slice(c * step, (c + 1) * step)
        here[2 * c].wait()
        g_act = dot(low, w_down[cut, :], 1, 1)
        here[2 * c + 1].wait()
        got = (g_act * slope[:, cut].astype(f32)).astype(bf16)
        g_up[:, cut] = got
        leave = pltpu.make_async_copy(
            g_up.at[:, cut], g_up_hbm.at[:, cut], sems.at[3 * c + 2]
        )
        leave.start()
        d_ubias[:, cut] = jnp.sum(got.astype(f32), axis=0, keepdims=True)
        scr[c] = dot(h_t, got, 1, 0).astype(bf16)
        got = copy_out(scr.at[c], outs, sems, first, meta[6], cut)
        first += len(got)
        copies += got + [leave]
    for copy in copies:
        copy.wait()


def middle_kernel(
    ff,
    meta,
    g_resid2,
    norm1,
    cols,
    vectors,
    context_t,
    w_out,
    g_up_hbm,
    w_up_hbm,
    g_resid1,
    g_context,
    vec,
    d_out,
    g_up,
    w_up,
    sems,
):
    width = vectors.shape[1]
    gain1 = vectors[2:3, :]
    chunks = ff // width
    here = []
    for c in range(chunks):
        cut = slice(c * width, (c + 1) * width)
        here.append(pltpu.make_async_copy(g_up_hbm.at[:, cut], g_up.at[:, cut], sems.at[2 * c]))
        here.append(
            pltpu.make_async_copy(w_up_hbm.at[:, cut], w_up.at[:, cut], sems.at[2 * c + 1])
        )
    for copy in here:
        copy.start()
    n1 = norm1[...]
    g_hidden = g_resid2[...]
    for c in range(chunks):
        cut = slice(c * width, (c + 1) * width)
        here[2 * c].wait()
        here[2 * c + 1].wait()
        g_hidden = g_hidden + dot(g_up[:, cut], w_up[:, cut], 1, 1)
    vec[0:1, :] = jnp.sum(g_hidden * n1, axis=0, keepdims=True)
    vec[1:2, :] = jnp.sum(g_hidden, axis=0, keepdims=True)
    g_n = g_hidden * gain1
    g_v = cols[:, 0:1] * (
        g_n
        - jnp.mean(g_n, axis=-1, keepdims=True)
        - n1 * jnp.mean(g_n * n1, axis=-1, keepdims=True)
    )
    g_resid1[...] = g_v
    low = g_v.astype(bf16)
    vec[2:3, :] = jnp.sum(low.astype(f32), axis=0, keepdims=True)
    d_out[...] = dot(context_t[...], low, 1, 0).astype(bf16)
    g_context[...] = dot(low, w_out[...], 1, 1).astype(bf16)


def attention_kernel(
    dims,
    meta,
    g_context,
    qkv,
    kv,
    lse,
    g_query,
    g_kv,
    bias_scr,
):
    rows, local, window, length, width = dims
    pairs = width // 128
    even = lax.broadcasted_iota(jnp.int32, (local, 128), 1) < 64
    upper = lax.broadcasted_iota(jnp.int32, (128, local), 0) < 64
    for r in range(rows):
        bias_scr[...] = attention_bias(meta, r, local, window, length)
        own = slice(r * local, (r + 1) * local)
        for p in range(pairs):
            lanes = slice(p * 128, (p + 1) * 128)
            vlanes = slice(width + p * 128, width + (p + 1) * 128)
            q2 = pair_rows(qkv[own, lanes] * bf16(0.125), even)
            k2 = kv[r, :, lanes]
            v2 = kv[r, :, vlanes]
            gc2 = pair_rows(g_context[own, lanes], even)
            bias = bias_scr[...]
            s = dot(k2, q2, 1, 1) + jnp.concatenate([bias, bias], axis=1)
            prob = jnp.exp(s - lse[r * pairs + p : r * pairs + p + 1, :])
            g_prob = dot(v2, gc2, 1, 1)
            weighted = prob * g_prob
            inner = jnp.sum(weighted, axis=0, keepdims=True)
            g_score = (weighted - prob * inner).astype(bf16)
            g_kv[r, :, vlanes] = dot(prob.astype(bf16), gc2, 1, 0).astype(bf16)
            g_kv[r, :, lanes] = dot(g_score, q2, 1, 0).astype(bf16)
            g_q = dot(k2, g_score, 0, 0)
            g_q = jnp.where(upper, g_q[:, :local], g_q[:, local:]) * 0.125
            g_query[own, lanes] = g_q.T.astype(bf16)


def back_kernel(
    dims, g_resid1, g_query, g_kv, w_qkv, g_own, g_side, g_middle, g_far
):
    rows, local, far, window, width = dims
    w_kv = w_qkv[:, width:]
    for r in range(rows):
        own = slice(r * local, (r + 1) * local)
        back = dot(g_kv[r], w_kv, 1, 1)
        g_own[own, :] = (
            g_resid1[own, :] + dot(g_query[own, :], w_qkv[:, :width], 1, 1) + back[:local]
        )
        g_side[own, :] = back[local : 2 * local].astype(bf16)
        g_middle[own, :] = back[2 * local : 3 * local].astype(bf16)
        g_far[r * far : (r + 1) * far, :] = back[3 * local :].astype(bf16)


def weight_kernel(dims, meta, x_t, g_query, g_kv, vec_c, vec_d, d_ubias, d_out, d_proj, *rest):
    outs, (scr, low_scr, vec_scr, sems) = rest[:-4], rest[-4:]
    rows, local, width, devices = dims
    step = width
    ready = []
    at = 3 * width
    for source in (d_out, d_proj):
        columns = slice(at, at + source.shape[1])
        ready += copy_out(source, outs, sems, len(ready), meta[6], columns)
        at += source.shape[1]
    copies = ready
    for c in range(3):
        total = None
        for r in range(rows):
            if c == 0:
                part = dot(x_t[r, :, :local], g_query[r * local : (r + 1) * local, :], 1, 0)
            else:
                part = dot(x_t[r], g_kv[r, :, (c - 1) * width : c * width], 1, 0)
            total = part if total is None else total + part
        scr[c] = total.astype(bf16)
        copies += copy_out(
            scr.at[c], outs, sems, len(copies), meta[6], slice(c * step, (c + 1) * step)
        )
    d_qbias = jnp.sum(g_query[...].astype(f32), axis=0, keepdims=True)
    d_vbias = None
    for r in range(rows):
        part = jnp.sum(g_kv[r, :, width:].astype(f32), axis=0, keepdims=True)
        d_vbias = part if d_vbias is None else d_vbias + part
    lower = [d_qbias, d_vbias, vec_d[2:3, :], vec_d[0:1, :]]
    upper = [vec_d[1:2, :], vec_c[2:3, :], vec_c[0:1, :], vec_c[1:2, :]]
    upper += [
        d_ubias[:, c * width : (c + 1) * width] for c in range(d_ubias.shape[1] // width)
    ]
    block = width // devices
    some = 4 * width // devices
    vec_scr[...] = jnp.zeros(vec_scr.shape, f32)
    for device in range(devices):
        for row, vectors, start in (
            (0, lower, device * some),
            (1, upper, 2 * device * some),
            (2, upper, (2 * device + 1) * some),
        ):
            source = vectors[start // width]
            at = start % width
            vec_scr[device * block + row : device * block + row + 1, :some] = source[
                :, at : at + some
            ]
    low_scr[...] = vec_scr[...].astype(bf16)
    last = slice(outs[0].shape[-1] - 128, outs[0].shape[-1])
    copies += copy_out(low_scr, outs, sems, len(copies), meta[6], last)
    for copy in copies:
        copy.wait()


def call(kernel, outs, ins, scratch=(), smem=1, name=None, hbm_outs=0, hbm_ins=0, deps=(), aliases={}, us=1):
    deps = tuple(deps)
    count = len(ins)

    def run(*refs):
        kernel(*refs[:count], *refs[count + len(deps) :])

    return pl.pallas_call(
        run,
        out_shape=tuple(jax.ShapeDtypeStruct(shape, kind) for shape, kind in outs),
        in_specs=[SMEM] * smem
        + [VMEM] * (count - smem - hbm_ins)
        + [HBM] * (hbm_ins + len(deps)),
        out_specs=tuple([VMEM] * (len(outs) - hbm_outs) + [HBM] * hbm_outs),
        scratch_shapes=list(scratch),
        input_output_aliases=dict(aliases),
        cost_estimate=pl.CostEstimate(flops=int(us * COST), transcendentals=0, bytes_accessed=1),
        compiler_params=PARAMS,
        name=name,
    )(*ins, *deps)


def after(values, *tokens):
    return lax.optimization_barrier((values, tokens))[0]


class Chunk:
    def __init__(self, outs, dp_pos, seq_pos, dp_count, seq_count):
        self.dp_pos, self.seq_pos, self.dp_count, self.seq_count = (
            dp_pos,
            seq_pos,
            dp_count,
            seq_count,
        )
        if len(outs) == 2:
            self.other, self.mine = outs
        else:
            full = outs[0]
            parts = full.reshape(dp_count // 2, 2, full.shape[0] // dp_count, full.shape[1])
            core = dp_pos % 2
            self.other = lax.dynamic_index_in_dim(parts, 1 - core, 1, keepdims=False)
            self.mine = lax.dynamic_index_in_dim(parts, core, 1, keepdims=False)
        self.block = self.mine.shape[1]

    def core(self):
        self.recv = swap(self.other, "dp", 1, self.dp_count)
        return self.recv

    def ready(self, *tokens):
        mine, recv = after((self.mine, self.recv), *tokens)
        bits = bits_of(self.dp_count)[1:]
        columns = mine.shape[-1]
        half = columns // 256 * 128
        self.colours = [
            [[(mine, bits, 0), (recv, bits, 0)], bits, {}, half],
            [[(mine, bits, half), (recv, bits, half)], bits[::-1], {}, columns - half],
        ]

    def cut(self, term, fixed, columns, row, rows):
        value, bits, column = term
        high = sorted(bits, reverse=True)
        value = value.reshape((2,) * len(high) + (self.block, value.shape[-1]))
        start = [fixed.get(bit, 0) for bit in high] + [row, column]
        size = [1 if bit in fixed else 2 for bit in high] + [rows, columns]
        return lax.dynamic_slice(value, start, size).reshape(-1, rows, columns)

    def total_at(self, colour, fixed, row, rows):
        terms, _, _, columns = colour
        total = None
        for term in terms:
            part = self.cut(term, fixed, columns, row, rows).astype(f32)
            total = part if total is None else total + part
        return total

    def send(self):
        self.sent = []
        for colour in self.colours:
            _, order, fixed, _ = colour
            bit = order[0]
            at = (self.dp_pos // bit) % 2
            value = self.total_at(colour, {**fixed, bit: 1 - at}, 0, self.block).astype(bf16)
            self.sent.append((bit, value))
            colour[1] = order[1:]
            colour[2] = {**fixed, bit: at}
        return [value for _, value in self.sent]

    def go(self):
        self.got = [swap(value, "dp", bit, self.dp_count) for bit, value in self.sent]
        return self.got

    def take(self, *tokens):
        got = after(self.got, *tokens) if tokens else self.got
        for colour, recv in zip(self.colours, got):
            terms, order, _, _ = colour
            terms.append((recv, order, 0))

    def along_sends(self):
        while self.colours[0][1]:
            self.send()
            self.go()
            self.take()
        rows = self.block // self.seq_count

        def at(index):
            return jnp.concatenate(
                [self.total_at(c, c[2], index * rows, rows)[0] for c in self.colours], axis=-1
            )

        self.own = at(self.seq_pos)
        self.cells = [
            at(self.seq_pos ^ bit).astype(bf16) for bit in range(1, self.seq_count)
        ]
        return self.cells

    def along(self):
        self.got = [
            swap(cell, "seq", bit + 1, self.seq_count) for bit, cell in enumerate(self.cells)
        ]
        return self.got

    def total(self, *tokens):
        value = self.own
        for piece in after(self.got, *tokens) if tokens else self.got:
            value = value + piece.astype(f32)
        return value


def body(
    hidden_in,
    segment_ids,
    query_emb,
    positives,
    w_qkv,
    query_bias,
    value_bias,
    w_out,
    out_bias,
    norm1_gain,
    norm1_bias,
    w_up,
    up_bias,
    w_down,
    down_bias,
    norm2_gain,
    norm2_bias,
    w_proj,
):
    micro_count, row_count, local_len, width = hidden_in.shape
    full_len = segment_ids.shape[2]
    embed_width = w_proj.shape[1]
    ff = w_up.shape[1]
    queries_local = query_emb.shape[1]
    query_tokens = query_emb.shape[2]
    seq_count = lax.axis_size("seq")
    dp_count = lax.axis_size("dp")
    seq_pos = lax.axis_index("seq")
    dp_pos = lax.axis_index("dp")
    rows = micro_count * row_count
    tokens = rows * local_len
    far = 64
    window = 3 * local_len + far
    assert local_len + far >= PASSAGE_MOST - 1 and seq_count == 4

    x_own = hidden_in.reshape(rows, local_len, width)
    x_flat = x_own.reshape(tokens, width)
    low_half = seq_pos < 2
    inner = [(1, 2), (2, 1), (0, 0), (3, 3)]
    far_send = jnp.where(low_half, x_own[:, local_len - far :], x_own[:, :far])
    middle_x = lax.ppermute(x_flat, "seq", inner)
    far_x = swap(far_send.reshape(rows * far, width), "seq", 2, seq_count)
    side_x = swap(x_flat, "seq", 1, seq_count)
    pieces = [side_x, middle_x, far_x]

    seg_full = segment_ids.reshape(rows, full_len)
    edges = jnp.sum(
        (seg_full[:, None, :] < jnp.arange(1, SEGS, dtype=jnp.int32)[None, :, None]).astype(
            jnp.int32
        ),
        axis=2,
    )
    meta = jnp.concatenate(
        [
            jnp.stack(
                [
                    seq_pos * local_len,
                    0 * seq_pos,
                    (seq_pos ^ 1) * local_len,
                    jnp.where((seq_pos == 1) | (seq_pos == 2), 3 - seq_pos, -9) * local_len,
                    jnp.where(
                        low_half, (seq_pos + 2) * local_len, (seq_pos - 1) * local_len - far
                    ),
                    dp_pos * row_count * SEGS,
                    dp_pos % 2,
                ]
            ).astype(jnp.int32),
            edges.reshape(-1),
        ]
    )

    queries = query_emb.reshape(micro_count, queries_local * query_tokens, embed_width)
    for bit in bits_of(dp_count):
        recv = swap(queries, "dp", bit, dp_count)
        upper = (dp_pos // bit) % 2
        queries = jnp.where(
            upper == 0,
            jnp.concatenate([queries, recv], axis=1),
            jnp.concatenate([recv, queries], axis=1),
        )
    query_all = queries.shape[1]
    query_count = query_all // query_tokens
    wide = max(128, query_count)
    positives_wide = jnp.pad(
        positives, ((0, 0), (0, wide - query_count)), constant_values=-1
    )

    qkv_bias = jnp.concatenate([query_bias, jnp.zeros((width,), f32), value_bias])
    qkv = (jnp.dot(x_flat, w_qkv, preferred_element_type=f32) + qkv_bias).astype(bf16)

    vectors = jnp.concatenate(
        [value_bias, out_bias, norm1_gain, norm1_bias, down_bias, norm2_gain, norm2_bias, up_bias]
    ).reshape(-1, width)

    pairs = width // 128
    ff_chunks = ff // width
    forward = call(
        functools.partial(
            forward_kernel, (rows, local_len, far, window, full_len, width, row_count)
        ),
        [
            ((width, tokens), bf16),
            ((rows * pairs, 2 * local_len), f32),
            ((tokens, 128), f32),
            ((tokens, width), f32),
            ((width, tokens), bf16),
            ((tokens, embed_width), f32),
            ((tokens, embed_width), bf16),
            ((rows * SEGS, query_all), f32),
            ((rows, window, 2 * width), bf16),
            ((rows, width, window), bf16),
            ((tokens, width), f32),
            ((width, tokens), bf16),
            ((ff, tokens), bf16),
            ((tokens, ff), bf16),
        ],
        [
            meta,
            x_flat,
            *pieces,
            qkv,
            vectors,
            w_proj,
            queries,
            w_qkv,
            w_out,
            w_up,
            w_down,
        ],
        [
            pltpu.VMEM((window, local_len), f32),
            pltpu.VMEM((tokens, width), bf16),
            pltpu.VMEM((width, 2 * width), bf16),
            pltpu.VMEM((width, width), bf16),
            pltpu.VMEM((width, ff), bf16),
            pltpu.VMEM((ff, width), bf16),
            pltpu.VMEM((rows, window, 2 * width), bf16),
            pltpu.VMEM((rows, width, window), bf16),
            pltpu.VMEM((tokens, width), f32),
            pltpu.VMEM((width, tokens), bf16),
            pltpu.VMEM((ff, tokens), bf16),
            pltpu.VMEM((tokens, ff), bf16),
            pltpu.SemaphoreType.DMA((6 + 4 * ff_chunks,)),
        ],
        name="forward",
        hbm_ins=4,
        hbm_outs=6,
    )
    context_t, lse, cols, norm2, hidden2_t, proj, embed, parts = forward[:8]
    kv, x_t, norm1, hidden1_t, act_t, slope = forward[8:]

    others = [swap(parts, "seq", bit, seq_count) for bit in (1, 2, 3)]
    stat_rows = 8
    merged, score, stats = call(
        functools.partial(score_kernel, (rows, full_len, row_count, query_tokens)),
        [
            ((rows * SEGS, query_all), f32),
            ((rows * SEGS, wide), f32),
            ((stat_rows, wide), f32),
        ],
        [meta, parts, *others, positives_wide],
        name="score",
        us=2,
    )
    bits = bits_of(dp_count)
    groups = [bits[:1]] + [bits[k : k + 2] for k in range(1, len(bits), 2)]
    is_whole = lax.broadcasted_iota(jnp.int32, stats.shape, 0) < micro_count
    for group in groups:
        jumps = group if len(group) == 1 else [group[0], group[1], group[0] + group[1]]
        recv = [swap(stats, "dp", jump, dp_count) for jump in jumps]
        if len(recv) == 1:
            best = jnp.maximum(stats, recv[0])
            whole = jnp.exp(stats - best) + jnp.exp(recv[0] - best)
            hits = stats + recv[0]
        else:
            best = jnp.maximum(jnp.maximum(stats, recv[0]), jnp.maximum(recv[1], recv[2]))
            whole = (jnp.exp(stats - best) + jnp.exp(recv[0] - best)) + (
                jnp.exp(recv[1] - best) + jnp.exp(recv[2] - best)
            )
            hits = (stats + recv[0]) + (recv[1] + recv[2])
        stats = jnp.where(is_whole, best + jnp.log(whole), hits)

    devices = dp_count * seq_count

    def places(depth, columns):
        block = depth // dp_count
        if block % 16 == 0:
            return [((dp_count // 2, block, columns), bf16)] * 2
        return [((depth, columns), bf16)]

    def sems(outs, times=1):
        return pltpu.SemaphoreType.DMA((times * (dp_count if len(outs) == 2 else 1),))

    def chunk(outs):
        return Chunk(outs, dp_pos, seq_pos, dp_count, seq_count)

    down_places = places(ff, width)
    loss, d_proj, g_resid2, vec_c, *outs = call(
        functools.partial(
            upper_kernel,
            (rows, local_len, full_len, row_count, query_tokens),
            len(down_places),
        ),
        [
            ((micro_count, wide), f32),
            ((width, embed_width), bf16),
            ((tokens, width), f32),
            ((8, width), f32),
        ]
        + down_places,
        [
            meta,
            merged,
            score,
            stats,
            positives_wide,
            queries,
            embed,
            proj,
            norm2,
            hidden2_t,
            cols,
            vectors,
            w_proj,
            act_t,
        ],
        [
            pltpu.VMEM((ff, width), bf16),
            pltpu.VMEM((ff, tokens), bf16),
            pltpu.SemaphoreType.DMA((max(dp_count, ff_chunks) + 1,)),
        ],
        hbm_ins=1,
        name="upper",
        us=8,
        hbm_outs=len(down_places),
    )
    losses = lax.dynamic_slice_in_dim(loss, dp_pos * queries_local, queries_local, 1)
    down = chunk(outs)
    down.core()

    up_places = places(width, ff)
    d_ubias, g_up, *outs = call(
        functools.partial(gate_kernel, len(up_places)),
        [((1, ff), f32), ((tokens, ff), bf16)] + up_places,
        [meta, g_resid2, hidden1_t, w_down, slope],
        [
            pltpu.VMEM((ff_chunks, width, width), bf16),
            pltpu.VMEM((ff, width), bf16),
            pltpu.VMEM((tokens, ff), bf16),
            pltpu.VMEM((tokens, ff), bf16),
            pltpu.SemaphoreType.DMA((ff_chunks * (3 + dp_count),)),
        ],
        name="gate",
        us=8,
        hbm_ins=2,
        hbm_outs=1 + len(up_places),
    )
    up = chunk(outs)
    up.core()
    down.ready(g_up)
    sends = down.send()
    g_resid1, g_context, vec_d, d_out = call(
        functools.partial(middle_kernel, ff),
        [
            ((tokens, width), f32),
            ((tokens, width), bf16),
            ((8, width), f32),
            ((width, width), bf16),
        ],
        [meta, g_resid2, norm1, cols, vectors, context_t, w_out, g_up, w_up],
        [
            pltpu.VMEM((tokens, ff), bf16),
            pltpu.VMEM((width, ff), bf16),
            pltpu.SemaphoreType.DMA((2 * ff_chunks,)),
        ],
        name="middle",
        us=8,
        hbm_ins=2,
        deps=sends,
    )
    down.go()
    up.ready(g_resid1)
    sends = up.send()
    up.go()
    g_query, g_kv = call(
        functools.partial(attention_kernel, (rows, local_len, window, full_len, width)),
        [((tokens, width), bf16), ((rows, window, 2 * width), bf16)],
        [meta, g_context, qkv, kv, lse],
        [pltpu.VMEM((window, local_len), f32)],
        name="attention",
        us=9,
        deps=sends,
    )
    down.take(g_query)
    sends = down.send()
    down.go()
    last_places = places(width, 4 * width + embed_width + 128)
    outs = call(
        functools.partial(weight_kernel, (rows, local_len, width, devices)),
        last_places,
        [meta, x_t, g_query, g_kv, vec_c, vec_d, d_ubias, d_out, d_proj],
        [
            pltpu.VMEM((3, width, width), bf16),
            pltpu.VMEM((width, 128), bf16),
            pltpu.VMEM((width, 128), f32),
            pltpu.SemaphoreType.DMA((6 * dp_count,)),
        ],
        name="weight",
        us=7,
        hbm_outs=len(last_places),
        deps=sends,
    )
    last = chunk(outs)
    last.core()
    g_own, g_side, g_middle, g_far = call(
        functools.partial(back_kernel, (rows, local_len, far, window, width)),
        [
            ((tokens, width), f32),
            ((tokens, width), bf16),
            ((tokens, width), bf16),
            ((rows * far, width), bf16),
        ],
        [g_resid1, g_query, g_kv, w_qkv],
        smem=0,
        name="back",
        us=7,
        deps=outs,
    )
    from_middle = lax.ppermute(g_middle, "seq", inner)
    from_far = swap(g_far, "seq", 2, seq_count)
    from_side = swap(g_side, "seq", 1, seq_count)
    last.ready(g_own)
    sends = last.send()
    last.go()
    up.take(*sends)
    sends = up.send()
    up.go()
    down.take(*sends)
    sends = down.along_sends()
    down.along()
    g_own, from_side, from_middle, from_far = after(
        (g_own, from_side, from_middle, from_far), *sends
    )
    from_far = from_far.reshape(rows, far, width).astype(f32)
    pad = ((0, 0), (local_len - far, 0), (0, 0))
    flip = ((0, 0), (0, local_len - far), (0, 0))
    grad_in = (g_own + from_side.astype(f32) + from_middle.astype(f32)).reshape(
        rows, local_len, width
    ) + jnp.where(low_half, jnp.pad(from_far, pad), jnp.pad(from_far, flip))

    last.take(grad_in)
    sends = last.send()
    last.go()
    up.take(*sends)
    sends = up.along_sends()
    up.along()
    down_part = down.total(*sends)
    last.take(down_part)
    sends = last.along_sends()
    last.along()
    up_part = up.total(*sends)
    last_part = last.total(up_part)
    some = 4 * width // devices
    vec_at = 4 * width + embed_width
    vec_part = last_part[:3, vec_at : vec_at + some]
    return (
        embed.reshape(micro_count, row_count, local_len, embed_width),
        losses,
        grad_in.reshape(micro_count, row_count, local_len, width),
        last_part[:, : 3 * width].reshape(-1),
        last_part[:, 3 * width : 4 * width].reshape(-1),
        up_part.reshape(-1),
        down_part.reshape(-1),
        last_part[:, 4 * width : vec_at].reshape(-1),
        vec_part[0],
        vec_part[1:].reshape(-1),
    )


def solution(mesh):
    in_specs = (
        P(None, "dp", "seq", None),
        P(None, "dp", None),
        P(None, "dp", None, None),
    ) + (P(),) * 15
    out_specs = (
        P(None, "dp", "seq", None),
        P(None, "dp"),
        P(None, "dp", "seq", None),
    ) + (P(("dp", "seq")),) * 7
    return jax.shard_map(body, mesh=mesh, in_specs=in_specs, out_specs=out_specs, check_vma=False)
```

```python
import functools

import jax
import jax.numpy as jnp
from jax import lax
from jax.experimental import pallas as pl
from jax.experimental.pallas import tpu as pltpu
from jax.sharding import PartitionSpec as P

HEADS = 12
SEGS = 4
PASSAGE_MOST = 180

SHARP = 20.0
EDGES = 8
COST = 4e9
FOLD = 0.3
LN_EPS = 1e-12
NORM_EPS = 1e-12
MASKED = -1e30
HIGH = lax.Precision.HIGHEST
bf16 = jnp.bfloat16
f32 = jnp.float32
VMEM = pl.BlockSpec(memory_space=pltpu.VMEM)
HBM = pl.BlockSpec(memory_space=pltpu.HBM)
SMEM = pl.BlockSpec(memory_space=pltpu.SMEM)
PARAMS = pltpu.CompilerParams(vmem_limit_bytes=58 << 20)


def bits_of(count):
    return [1 << k for k in range(count.bit_length() - 1)]


def swap(value, axis, bit, count):
    return lax.ppermute(value, axis, [(i, i ^ bit) for i in range(count)])


def dot(left, right, left_dim, right_dim, precision=None):
    return lax.dot_general(
        left,
        right,
        (((left_dim,), (right_dim,)), ((), ())),
        precision=precision,
        preferred_element_type=f32,
    )


def ident(pos, meta, row, length):
    seg = jnp.zeros(pos.shape, jnp.int32)
    for s in range(SEGS - 1):
        seg = seg + (pos >= meta[EDGES + row * (SEGS - 1) + s]).astype(jnp.int32)
    return jnp.where((pos >= 0) & (pos < length), seg, -1)


def key_positions(meta, local, shape):
    w = lax.broadcasted_iota(jnp.int32, shape, 0)
    pos = meta[0] + w
    for piece in range(1, 4):
        pos = jnp.where(w >= piece * local, meta[1 + piece] + w - piece * local, pos)
    return pos


def pair_rows(block, even):
    zero = jnp.zeros_like(block)
    return jnp.concatenate([jnp.where(even, block, zero), jnp.where(even, zero, block)], axis=0)


def attention_bias(meta, row, local, window, length):
    key_seg = ident(key_positions(meta, local, (window, local)), meta, row, length)
    query_seg = ident(
        meta[0] + lax.broadcasted_iota(jnp.int32, (window, local), 1), meta, row, length
    )
    return jnp.where(key_seg == query_seg, 0.0, MASKED).astype(f32)


def copies_out(scr, outs, sems, first, core, columns, part=0, parts=1):
    size = scr.shape[0]
    if len(outs) == 1:
        pieces = [(scr, outs[0].at[pl.ds(part * size, size), columns])]
    else:
        high, block, _ = outs[0].shape
        pieces = []
        for k in range(high // parts):
            for out, which in ((outs[0], 1 - core), (outs[1], core)):
                rows = pl.ds(pl.multiple_of((2 * k + which) * block, 16), block)
                pieces.append((scr.at[rows, :], out.at[part * (high // parts) + k, :, columns]))
    return [
        pltpu.make_async_copy(source, target, sems.at[first + n])
        for n, (source, target) in enumerate(pieces)
    ]


def begin(copies):
    for copy in copies:
        copy.start()


def finish(copies):
    for copy in copies:
        copy.wait()


def forward_kernel(
    dims,
    meta,
    value_bias_in,
    out_bias_in,
    gain1_in,
    shift1_in,
    down_bias_in,
    gain2_in,
    shift2_in,
    query_bias_in,
    up_bias_in,
    w_proj,
    x_own_hbm,
    side_hbm,
    middle_hbm,
    far_hbm,
    queries_hbm,
    w_qkv_hbm,
    w_out_hbm,
    w_up_hbm,
    w_down_hbm,
    vectors,
    query,
    context_t,
    lse,
    cols,
    norm2,
    hidden2_t,
    proj,
    embed,
    parts,
    kv_hbm,
    x_t_hbm,
    norm1_hbm,
    hidden1_t_hbm,
    act_t_hbm,
    slope_hbm,
    bias_scr,
    context,
    x_own,
    side,
    middle,
    far_part,
    queries,
    w_qkv,
    w_out,
    w_up,
    w_down,
    kv,
    x_t,
    norm1,
    hidden1_t,
    act_t,
    slope,
    hidden_scr,
    ffn_scr,
    sems,
):
    rows, local, far, window, length, width, row_count = dims
    chunks = w_up.shape[0]
    kv_here = pltpu.make_async_copy(w_qkv_hbm, w_qkv, sems.at[0])
    out_here = pltpu.make_async_copy(w_out_hbm, w_out, sems.at[1])

    def up_here(c):
        cut = pl.ds(pl.multiple_of(c * width, 128), width)
        return pltpu.make_async_copy(w_up_hbm.at[:, cut], w_up.at[c], sems.at[2 + c])

    def down_here(c):
        cut = pl.ds(pl.multiple_of(c * width, 128), width)
        return pltpu.make_async_copy(
            w_down_hbm.at[cut, :], w_down.at[c], sems.at[2 + chunks + c]
        )

    base = 2 + 2 * chunks
    pieces_here = [
        pltpu.make_async_copy(source, target, sems.at[base + 4 + 2 * chunks + n])
        for n, (source, target) in enumerate(
            ((x_own_hbm, x_own), (side_hbm, side), (middle_hbm, middle), (far_hbm, far_part))
        )
    ]
    queries_here = pltpu.make_async_copy(
        queries_hbm, queries, sems.at[base + 8 + 2 * chunks]
    )
    begin([pieces_here[0], kv_here] + pieces_here[1:] + [out_here])
    for c in range(chunks):
        begin([up_here(c), down_here(c)])
    queries_here.start()
    for n, vector in enumerate(
        (
            value_bias_in,
            out_bias_in,
            gain1_in,
            shift1_in,
            down_bias_in,
            gain2_in,
            shift2_in,
        )
    ):
        vectors[n : n + 1, :] = vector[...].reshape(1, width)
    for c in range(chunks):
        vectors[7 + c : 8 + c, :] = up_bias_in[pl.ds(c * width, width)].reshape(1, width)
    vectors[7 + chunks : 8 + chunks, :] = query_bias_in[...].reshape(1, width)
    value_bias = vectors[0:1, :]
    kv_out = pltpu.make_async_copy(kv, kv_hbm, sems.at[base])
    x_out = pltpu.make_async_copy(x_t, x_t_hbm, sems.at[base + 1])
    norm_out = pltpu.make_async_copy(norm1, norm1_hbm, sems.at[base + 2])
    hidden_out = pltpu.make_async_copy(hidden1_t, hidden1_t_hbm, sems.at[base + 3])

    def act_out(c):
        return pltpu.make_async_copy(act_t.at[c], act_t_hbm.at[c], sems.at[base + 4 + c])

    def slope_out(c):
        return pltpu.make_async_copy(
            slope.at[c], slope_hbm.at[c], sems.at[base + 4 + chunks + c]
        )

    finish([pieces_here[0], kv_here])
    query[...] = (dot(x_own[...], w_qkv[:, :width], 1, 0) + vectors[7 + chunks : 8 + chunks, :]).astype(
        bf16
    )
    offset = 0
    for n, (piece, size) in enumerate(
        ((x_own, local), (side, local), (middle, local), (far_part, far))
    ):
        if n:
            pieces_here[n].wait()
        got = dot(piece[...], w_qkv[:, width:], 1, 0)
        got_k = got[:, :width].astype(bf16)
        got_v = (got[:, width:] + value_bias).astype(bf16)
        for r in range(rows):
            mine = slice(r * size, (r + 1) * size)
            kv[r, offset : offset + size, :width] = got_k[mine]
            kv[r, offset : offset + size, width:] = got_v[mine]
            x_t[r, :, offset : offset + size] = piece[mine, :].T
        offset += size
    begin([kv_out, x_out])
    even = lax.broadcasted_iota(jnp.int32, (local, 128), 1) < 64
    upper = lax.broadcasted_iota(jnp.int32, (128, local), 0) < 64
    pairs = width // 128

    def attend(r, carry):
        bias_scr[...] = attention_bias(meta, r, local, window, length)
        own = pl.ds(pl.multiple_of(r * local, 128), local)
        for p in range(pairs):
            lanes = slice(p * 128, (p + 1) * 128)
            q2 = pair_rows(query[own, lanes] * bf16(0.125), even)
            k2 = kv[r, :, lanes]
            v2 = kv[r, :, width + p * 128 : width + (p + 1) * 128]
            bias = bias_scr[...]
            s = dot(k2, q2, 1, 1) + jnp.concatenate([bias, bias], axis=1)
            top = jnp.max(s, axis=0, keepdims=True)
            e = jnp.exp(s - top)
            total = jnp.sum(e, axis=0, keepdims=True)
            lse[r, p : p + 1, :] = top + jnp.log(total)
            o = dot(v2, e.astype(bf16), 0, 0) * (1.0 / total)
            o = jnp.where(upper, o[:, :local], o[:, local:])
            context_t[lanes, own] = o.astype(bf16)
            context[own, lanes] = o.T.astype(bf16)
        return carry

    lax.fori_loop(0, rows, attend, 0)
    out_here.wait()
    attended = dot(context[...], w_out[...], 1, 0) + vectors[1:2, :]
    resid = x_own[...].astype(f32) + attended
    centred = resid - jnp.mean(resid, axis=-1, keepdims=True)
    rstd1 = lax.rsqrt(jnp.mean(centred * centred, axis=-1, keepdims=True) + LN_EPS)
    n1 = centred * rstd1
    norm1[...] = n1
    hidden1 = n1 * vectors[2:3, :] + vectors[3:4, :]
    hidden1_low = hidden1.astype(bf16)
    hidden1_t[...] = hidden1_low.T
    begin([norm_out, hidden_out])
    hidden_scr[...] = hidden1_low
    ffn_scr[...] = hidden1 + vectors[4:5, :]

    def feed(c, carry):
        up_here(c).wait()
        up = dot(hidden_scr[...], w_up[c], 1, 0) + vectors[pl.ds(7 + c, 1), :]
        cdf = 0.5 * (1.0 + lax.erf(up * (0.5**0.5)))
        act_low = (up * cdf).astype(bf16)
        act_t[c] = act_low.T
        slope[c] = (cdf + up * (jnp.exp(-0.5 * up * up) * 0.3989422804014327)).astype(bf16)
        begin([act_out(c), slope_out(c)])
        down_here(c).wait()
        ffn_scr[...] += dot(act_low, w_down[c], 1, 0)
        return carry

    lax.fori_loop(0, chunks, feed, 0)
    resid = ffn_scr[...]
    centred = resid - jnp.mean(resid, axis=-1, keepdims=True)
    rstd2 = lax.rsqrt(jnp.mean(centred * centred, axis=-1, keepdims=True) + LN_EPS)
    n2 = centred * rstd2
    norm2[...] = n2
    lane = lax.broadcasted_iota(jnp.int32, cols.shape, 1)
    cols[...] = jnp.where(lane == 0, rstd1, rstd2)
    hidden2_low = (n2 * vectors[5:6, :] + vectors[6:7, :]).astype(bf16)
    hidden2_t[...] = hidden2_low.T
    out = dot(hidden2_low, w_proj[...], 1, 0)
    proj[...] = out
    inv = lax.rsqrt(jnp.sum(out * out, axis=-1, keepdims=True) + NORM_EPS)
    embed[...] = (out * inv).astype(bf16)

    def match(r, carry):
        own = pl.ds(pl.multiple_of(r * local, 128), local)
        sharp = dot(embed[own, :], queries[r // row_count], 1, 1) * SHARP
        seg = ident(meta[0] + lax.broadcasted_iota(jnp.int32, (local, 1), 0), meta, r, length)
        tops = []
        shift = jnp.zeros_like(sharp)
        for s in range(SEGS):
            inside = seg == s
            top = jnp.max(jnp.where(inside, sharp, MASKED), axis=0, keepdims=True)
            tops.append(top)
            shift = jnp.where(inside, top, shift)
        e = jnp.exp(sharp - shift)
        for s in range(SEGS):
            total = jnp.sum(jnp.where(seg == s, e, 0.0), axis=0, keepdims=True)
            some = total > 0.0
            parts[pl.ds(r * SEGS + s, 1), :] = jnp.where(
                some, tops[s] + jnp.log(jnp.where(some, total, 1.0)), MASKED
            )
        return carry

    queries_here.wait()
    lax.fori_loop(0, rows, match, 0)
    finish([kv_out, x_out, norm_out, hidden_out])
    for c in range(chunks):
        finish([act_out(c), slope_out(c)])


def score_kernel(dims, meta, first, second, third, fourth, positives, merged, score, stats):
    rows, length, row_count, query_tokens = dims
    half = rows * SEGS
    parts = [ref[...] for ref in (first, second, third, fourth)]
    top = jnp.maximum(jnp.maximum(parts[0], parts[1]), jnp.maximum(parts[2], parts[3]))
    sums = [jnp.exp(part - top) for part in parts]
    whole = top + jnp.log((sums[0] + sums[1]) + (sums[2] + sums[3]))
    merged[...] = whole
    sub = lax.broadcasted_iota(jnp.int32, (half, 1), 0)
    count = jnp.zeros((half, 1), f32)
    for r in range(rows):
        edges = [0] + [meta[EDGES + r * (SEGS - 1) + s] for s in range(SEGS - 1)] + [length]
        for s in range(SEGS):
            size = (edges[s + 1] - edges[s]).astype(f32)
            count = jnp.where(sub == r * SEGS + s, size, count)
    match = whole - jnp.log(count)
    wide = score.shape[1]
    shape = (match.shape[1], wide)
    group = (
        lax.broadcasted_iota(jnp.int32, shape, 0) // query_tokens
        == lax.broadcasted_iota(jnp.int32, shape, 1)
    ).astype(f32)
    got = dot(match, group, 1, 0, HIGH)
    score[...] = got
    per = row_count * SEGS
    micros = rows // row_count
    stats[...] = jnp.zeros(stats.shape, f32)
    for m in range(micros):
        part = got[m * per : (m + 1) * per]
        at = lax.broadcasted_iota(jnp.int32, (per, wide), 0) + meta[5]
        chosen = at == positives[m : m + 1, :]
        best = jnp.max(part, axis=0, keepdims=True)
        stats[m : m + 1, :] = best + jnp.log(
            jnp.sum(jnp.exp(part - best), axis=0, keepdims=True)
        )
        stats[micros + m : micros + m + 1, :] = jnp.sum(
            jnp.where(chosen, part, 0.0), axis=0, keepdims=True
        )


def upper_kernel(
    dims,
    meta,
    merged,
    score,
    stats,
    positives,
    queries,
    embed,
    proj,
    norm2,
    hidden2_t,
    cols,
    vectors,
    w_proj,
    act_t_hbm,
    loss,
    d_proj,
    g_resid2,
    vec,
    *rest,
):
    outs, (scr, act_t, factor_scr, unit_scr, sems) = rest[:-5], rest[-5:]
    rows, local, length, row_count, query_tokens = dims
    chunks = act_t.shape[0]
    gain2 = vectors[5:6, :]
    act_here = pltpu.make_async_copy(act_t_hbm, act_t, sems.at[0])
    act_here.start()
    micros = rows // row_count
    per = row_count * SEGS
    wide = score.shape[1]
    all_queries = merged.shape[1]
    shape = (wide, all_queries)
    group = (
        lax.broadcasted_iota(jnp.int32, shape, 1) // query_tokens
        == lax.broadcasted_iota(jnp.int32, shape, 0)
    ).astype(f32)
    pieces = []
    for m in range(micros):
        whole = stats[m : m + 1, :]
        loss[m : m + 1, :] = whole - stats[micros + m : micros + m + 1, :]
        part = score[m * per : (m + 1) * per, :]
        at = lax.broadcasted_iota(jnp.int32, (per, wide), 0) + meta[5]
        chosen = (at == positives[m : m + 1, :]).astype(f32)
        pieces.append(jnp.exp(part - whole) - chosen)
    factor_scr[...] = SHARP * dot(jnp.concatenate(pieces, axis=0), group, 1, 0, HIGH)

    def pull(r, carry):
        own = pl.ds(pl.multiple_of(r * local, 128), local)
        m = r // row_count
        sharp = dot(embed[own, :], queries[m], 1, 1) * SHARP
        seg = ident(meta[0] + lax.broadcasted_iota(jnp.int32, (local, 1), 0), meta, r, length)
        shift = jnp.zeros_like(sharp)
        scale = jnp.zeros_like(sharp)
        for s in range(SEGS):
            at = pl.ds(r * SEGS + s, 1)
            shift = jnp.where(seg == s, merged[at, :], shift)
            scale = jnp.where(seg == s, factor_scr[at, :], scale)
        g_sim = (scale * jnp.exp(sharp - shift)).astype(bf16)
        unit_scr[own, :] = dot(g_sim, queries[m], 1, 0)
        return carry

    lax.fori_loop(0, rows, pull, 0)
    g_unit = unit_scr[...]
    out = proj[...]
    inv = lax.rsqrt(jnp.sum(out * out, axis=-1, keepdims=True) + NORM_EPS)
    unit = out * inv
    g_proj = ((g_unit - unit * jnp.sum(unit * g_unit, axis=-1, keepdims=True)) * inv).astype(bf16)
    n2 = norm2[...]
    d_proj[...] = dot(hidden2_t[...], g_proj, 1, 0).astype(bf16)
    g_hidden = dot(g_proj, w_proj[...], 1, 1)
    vec[0:1, :] = jnp.sum(g_hidden * n2, axis=0, keepdims=True)
    vec[1:2, :] = jnp.sum(g_hidden, axis=0, keepdims=True)
    g_n = g_hidden * gain2
    g_v = cols[:, 1:2] * (
        g_n
        - jnp.mean(g_n, axis=-1, keepdims=True)
        - n2 * jnp.mean(g_n * n2, axis=-1, keepdims=True)
    )
    g_resid2[...] = g_v
    low = g_v.astype(bf16)
    vec[2:3, :] = jnp.sum(low.astype(f32), axis=0, keepdims=True)
    act_here.wait()
    columns = slice(0, scr.shape[2])
    each = 2 * (outs[0].shape[0] // chunks) if len(outs) == 2 else 1

    def leaving(c):
        return copies_out(scr.at[c], outs, sems, 1 + c * each, meta[6], columns, c, chunks)

    for c in range(chunks):
        scr[c] = dot(act_t[c], low, 1, 0).astype(bf16)
        begin(leaving(c))
    for c in range(chunks):
        finish(leaving(c))


def lower_kernel(
    meta,
    g_resid2,
    hidden1_t,
    norm1,
    cols,
    vectors,
    context_t,
    w_out,
    d_proj,
    w_down_hbm,
    w_up_hbm,
    slope_hbm,
    d_ubias,
    g_resid1,
    g_context,
    vec,
    *rest,
):
    outs, (w_down, w_up, slope, hidden_scr, low_scr, scr, out_scr, sems) = rest[:-8], rest[-8:]
    chunks, width, _ = w_up.shape
    gain1 = vectors[2:3, :]
    each = 2 * outs[0].shape[0] if len(outs) == 2 else 1

    def here(c):
        cut = pl.ds(pl.multiple_of(c * width, 128), width)
        return [
            pltpu.make_async_copy(w_down_hbm.at[cut, :], w_down.at[c], sems.at[3 * c]),
            pltpu.make_async_copy(slope_hbm.at[c], slope.at[c], sems.at[3 * c + 1]),
            pltpu.make_async_copy(w_up_hbm.at[:, cut], w_up.at[c], sems.at[3 * c + 2]),
        ]

    def leaving(c):
        cut = pl.ds(pl.multiple_of(c * width, 128), width)
        return copies_out(scr.at[c], outs, sems, 3 * chunks + c * each, meta[6], cut)

    for c in range(chunks):
        begin(here(c))
    hidden_scr[...] = g_resid2[...]
    low_scr[...] = g_resid2[...].astype(bf16)

    def gate(c, carry):
        finish(here(c))
        g_act = dot(low_scr[...], w_down[c], 1, 1)
        g_up = (g_act * slope[c].astype(f32)).astype(bf16)
        d_ubias[c] = jnp.sum(g_up.astype(f32), axis=0, keepdims=True)
        scr[c] = dot(hidden1_t[...], g_up, 1, 0).astype(bf16)
        begin(leaving(c))
        hidden_scr[...] += dot(g_up, w_up[c], 1, 1)
        return carry

    lax.fori_loop(0, chunks, gate, 0)
    n1 = norm1[...]
    g_hidden = hidden_scr[...]
    vec[0:1, :] = jnp.sum(g_hidden * n1, axis=0, keepdims=True)
    vec[1:2, :] = jnp.sum(g_hidden, axis=0, keepdims=True)
    g_n = g_hidden * gain1
    g_v = cols[:, 0:1] * (
        g_n
        - jnp.mean(g_n, axis=-1, keepdims=True)
        - n1 * jnp.mean(g_n * n1, axis=-1, keepdims=True)
    )
    g_resid1[...] = g_v
    low = g_v.astype(bf16)
    vec[2:3, :] = jnp.sum(low.astype(f32), axis=0, keepdims=True)
    out_scr[:, :width] = dot(context_t[...], low, 1, 0).astype(bf16)
    out_scr[:, width:] = d_proj[...]
    columns = slice(chunks * width, chunks * width + out_scr.shape[1])
    last = copies_out(out_scr, outs, sems, (3 + each) * chunks, meta[6], columns)
    begin(last)
    g_context[...] = dot(low, w_out[...], 1, 1).astype(bf16)
    for c in range(chunks):
        finish(leaving(c))
    finish(last)


def attention_kernel(
    dims,
    meta,
    g_context,
    query,
    lse,
    vec_c,
    vec_d,
    d_ubias,
    g_resid1,
    kv_hbm,
    x_t_hbm,
    w_qkv_hbm,
    g_own,
    g_side,
    g_middle,
    g_far,
    *rest,
):
    outs, scratch = rest[:-10], rest[-10:]
    kv, x_t, g_query, g_kv, w_qkv, bias_scr, scr, low_scr, vec_scr, sems = scratch
    rows, local, far, window, length, width, devices = dims
    pairs = width // 128
    even = lax.broadcasted_iota(jnp.int32, (local, 128), 1) < 64
    upper = lax.broadcasted_iota(jnp.int32, (128, local), 0) < 64

    def kv_here(r):
        return pltpu.make_async_copy(kv_hbm.at[r], kv.at[r], sems.at[r])

    for r in range(rows):
        kv_here(r).start()
    x_here = pltpu.make_async_copy(x_t_hbm, x_t, sems.at[rows])
    w_here = pltpu.make_async_copy(w_qkv_hbm, w_qkv, sems.at[rows + 1])
    begin([x_here, w_here])

    def attend(r, carry):
        kv_here(r).wait()
        bias_scr[...] = attention_bias(meta, r, local, window, length)
        own = pl.ds(pl.multiple_of(r * local, 128), local)
        for p in range(pairs):
            lanes = slice(p * 128, (p + 1) * 128)
            vlanes = slice(width + p * 128, width + (p + 1) * 128)
            q2 = pair_rows(query[own, lanes] * bf16(0.125), even)
            k2 = kv[r, :, lanes]
            v2 = kv[r, :, vlanes]
            gc2 = pair_rows(g_context[own, lanes], even)
            bias = bias_scr[...]
            s = dot(k2, q2, 1, 1) + jnp.concatenate([bias, bias], axis=1)
            prob = jnp.exp(s - lse[r, p : p + 1, :])
            g_prob = dot(v2, gc2, 1, 1)
            weighted = prob * g_prob
            inner = jnp.sum(weighted, axis=0, keepdims=True)
            g_score = (weighted - prob * inner).astype(bf16)
            g_kv[r, :, vlanes] = dot(prob.astype(bf16), gc2, 1, 0).astype(bf16)
            g_kv[r, :, lanes] = dot(g_score, q2, 1, 0).astype(bf16)
            g_q = dot(k2, g_score, 0, 0)
            g_q = jnp.where(upper, g_q[:, :local], g_q[:, local:]) * 0.125
            g_query[own, lanes] = g_q.T.astype(bf16)
        return carry

    lax.fori_loop(0, rows, attend, 0)
    x_here.wait()
    each = 2 * outs[0].shape[0] if len(outs) == 2 else 1
    copies = []
    for c in range(3):
        total = None
        for r in range(rows):
            if c == 0:
                part = dot(x_t[r, :, :local], g_query[r * local : (r + 1) * local, :], 1, 0)
            else:
                part = dot(x_t[r], g_kv[r, :, (c - 1) * width : c * width], 1, 0)
            total = part if total is None else total + part
        scr[c] = total.astype(bf16)
        columns = slice(c * width, (c + 1) * width)
        got = copies_out(scr.at[c], outs, sems, rows + 2 + c * each, meta[6], columns)
        begin(got)
        copies += got
    d_qbias = jnp.sum(g_query[...].astype(f32), axis=0, keepdims=True)
    d_vbias = None
    for r in range(rows):
        part = jnp.sum(g_kv[r, :, width:].astype(f32), axis=0, keepdims=True)
        d_vbias = part if d_vbias is None else d_vbias + part
    lower = [d_qbias, d_vbias, vec_d[2:3, :], vec_d[0:1, :]]
    higher = [vec_d[1:2, :], vec_c[2:3, :], vec_c[0:1, :], vec_c[1:2, :]]
    higher += [d_ubias[c] for c in range(d_ubias.shape[0])]
    block = width // devices
    some = 4 * width // devices
    vec_scr[...] = jnp.zeros(vec_scr.shape, f32)
    for device in range(devices):
        for row, vectors, start in (
            (0, lower, device * some),
            (1, higher, 2 * device * some),
            (2, higher, (2 * device + 1) * some),
        ):
            source = vectors[start // width]
            at = start % width
            vec_scr[device * block + row : device * block + row + 1, :some] = source[
                :, at : at + some
            ]
    low_scr[...] = vec_scr[...].astype(bf16)
    columns = slice(3 * width, 3 * width + 128)
    got = copies_out(low_scr, outs, sems, rows + 2 + 3 * each, meta[6], columns)
    begin(got)
    w_here.wait()

    def back(r, carry):
        own = pl.ds(pl.multiple_of(r * local, 128), local)
        part = dot(g_kv[r], w_qkv[:, width:], 1, 1)
        g_own[own, :] = (
            g_resid1[own, :] + dot(g_query[own, :], w_qkv[:, :width], 1, 1) + part[:local]
        )
        g_side[own, :] = part[local : 2 * local].astype(bf16)
        g_middle[own, :] = part[2 * local : 3 * local].astype(bf16)
        g_far[pl.ds(pl.multiple_of(r * far, 64), far), :] = part[3 * local :].astype(bf16)
        return carry

    lax.fori_loop(0, rows, back, 0)
    finish(copies + got)


def nothing(meta):
    del meta


def job_index(meta, bits, fixed):
    index = []
    for bit in bits:
        if bit in fixed:
            axis, stride = bit
            at = (meta[1] if axis == "dp" else meta[7]) // stride % 2
            index.append(1 - at if fixed[bit] else at)
        else:
            index.append(slice(None))
    return tuple(index)


def call(
    kernel,
    outs,
    ins,
    scratch=(),
    name=None,
    hbm_outs=0,
    hbm_ins=0,
    deps=(),
    jobs=(),
    us=3,
):
    deps = tuple(deps)
    count = len(ins)
    job_ins, job_outs, job_scratch, job_scratch_out = [], [], [], []
    for job in jobs:
        columns = 0
        for terms, fixed, size in job:
            for value, bits, column in terms:
                free = len([bit for bit in bits if bit not in fixed])
                shape = (2,) * free + (value.shape[-2], size)
                job_ins.append(value)
                job_scratch.append(pltpu.VMEM(shape, bf16))
            columns += size
        job_outs.append((shape[:-1] + (columns,), bf16))
        job_scratch_out.append(pltpu.VMEM(shape[:-1] + (columns,), bf16))
    extra = [pltpu.SemaphoreType.DMA((len(job_ins) + len(jobs),))] if jobs else []
    out_count, scratch_count = len(outs), len(scratch)

    def run(*refs):
        refs = list(refs)

        def pop(number):
            got, refs[:] = refs[:number], refs[number:]
            return got

        mine = pop(count)
        sources = pop(len(job_ins))
        pop(len(deps))
        mine += pop(out_count)
        targets = pop(len(job_outs))
        mine += pop(scratch_count)
        buffers = pop(len(job_ins))
        results = pop(len(job_outs))
        copies = []
        n = 0
        for job in jobs:
            for terms, fixed, size in job:
                for value, bits, column in terms:
                    index = job_index(mine[0], bits, fixed) + (slice(None), pl.ds(column, size))
                    copies.append(
                        pltpu.make_async_copy(sources[n].at[index], buffers[n], refs[0].at[n])
                    )
                    n += 1
        begin(copies)
        kernel(*mine)
        n = 0
        leaving = []
        for job, target, final in zip(jobs, results, targets):
            column = 0
            for terms, fixed, size in job:
                finish(copies[n : n + len(terms)])
                lead = target.shape[:-2]
                for flat in range(2 ** len(lead)):
                    at = tuple((flat >> k) % 2 for k in range(len(lead)))
                    total = None
                    for buffer in buffers[n : n + len(terms)]:
                        part = buffer[at].astype(f32)
                        total = part if total is None else total + part
                    target[at + (slice(None), slice(column, column + size))] = total.astype(bf16)
                n += len(terms)
                column += size
            leaving.append(
                pltpu.make_async_copy(target, final, refs[0].at[len(job_ins) + len(leaving)])
            )
            leaving[-1].start()
        finish(leaving)

    return pl.pallas_call(
        run,
        out_shape=tuple(jax.ShapeDtypeStruct(s, k) for s, k in list(outs) + job_outs),
        in_specs=[SMEM]
        + [VMEM] * (count - 1 - hbm_ins)
        + [HBM] * (hbm_ins + len(job_ins) + len(deps)),
        out_specs=tuple(
            [VMEM] * (out_count - hbm_outs) + [HBM] * (hbm_outs + len(job_outs))
        ),
        scratch_shapes=list(scratch) + job_scratch + job_scratch_out + extra,
        cost_estimate=pl.CostEstimate(flops=int(us * COST), transcendentals=0, bytes_accessed=1),
        compiler_params=PARAMS,
        name=name,
    )(*ins, *job_ins, *deps)


def after(values, *tokens):
    return lax.optimization_barrier((values, tokens))[0]


class Chunk:
    def __init__(self, outs, where, counts):
        self.where, self.counts = where, counts
        if len(outs) == 2:
            self.other, self.mine = outs
        else:
            full = outs[0]
            dp_count = counts["dp"]
            parts = full.reshape(dp_count // 2, 2, full.shape[0] // dp_count, full.shape[1])
            core = where["dp"] % 2
            self.other = lax.dynamic_index_in_dim(parts, 1 - core, 1, keepdims=False)
            self.mine = lax.dynamic_index_in_dim(parts, core, 1, keepdims=False)
        self.bits = [("dp", bit) for bit in bits_of(counts["dp"])[:0:-1]]
        self.bits += [("seq", bit) for bit in bits_of(counts["seq"])[::-1]]
        self.rows = self.mine.shape[1] // counts["seq"]

    def core(self):
        recv = swap(self.other, "dp", 1, self.counts["dp"])
        columns = recv.shape[-1]
        half = columns // 256 * 128
        both = [self.shaped(value, self.bits) for value in (self.mine, recv)]
        self.groups = [
            {"terms": [(v, tuple(self.bits), at) for v in both], "fixed": {}, "columns": size}
            for at, size in ((0, half), (half, columns - half))
        ]
        order = [bit for bit in self.bits if bit[0] == "dp"]
        self.orders = list(zip(order[::-1], order))

    def shaped(self, value, bits):
        return value.reshape((2,) * len(bits) + (self.rows, value.shape[-1]))

    def total_at(self, group, flips):
        total = None
        for value, bits, column in group["terms"]:
            start, size = [], []
            for bit in bits:
                at = (self.where[bit[0]] // bit[1]) % 2
                start.append((1 - at if flips[bit] else at) if bit in flips else 0)
                size.append(1 if bit in flips else 2)
            part = lax.dynamic_slice(
                value, start + [0, column], size + [self.rows, group["columns"]]
            )
            free = [n for n in size if n > 1]
            part = part.reshape(free + [self.rows, group["columns"]]).astype(f32)
            total = part if total is None else total + part
        return total

    def jobs(self, bits, joint):
        parts = []
        for group, bit in zip(self.groups, bits):
            parts.append((list(group["terms"]), {**group["fixed"], bit: 1}, group["columns"]))
            group["fixed"][bit] = 0
        self.todo = list(bits[:1]) if joint else list(bits)
        jobs = [parts] if joint else [[part] for part in parts]
        if self.rows % 8 == 0:
            return jobs
        self.accept(
            [
                jnp.concatenate(
                    [
                        self.total_at({"terms": t, "columns": c}, flips)
                        for t, flips, c in job
                    ],
                    axis=-1,
                ).astype(bf16)
                for job in jobs
            ]
        )
        return []

    def across(self):
        return self.jobs(self.orders.pop(0), False)

    def along(self, index):
        return self.jobs([("seq", index)] * len(self.groups), True)

    def plain(self, jobs):
        return [
            jnp.concatenate(
                [self.total_at({"terms": t, "columns": c}, flips) for t, flips, c in job], axis=-1
            ).astype(bf16)
            for job in jobs
        ]

    def wait(self, *tokens):
        values = after([[t[0] for t in group["terms"]] for group in self.groups], *tokens)
        for group, got in zip(self.groups, values):
            group["terms"] = [(v, t[1], t[2]) for v, t in zip(got, group["terms"])]

    def accept(self, values):
        values = list(values)
        if not values:
            return
        self.sent = values
        got = [
            swap(value, bit[0], bit[1], self.counts[bit[0]])
            for value, bit in zip(values, self.todo)
        ]
        column = 0
        for n, group in enumerate(self.groups):
            recv = got[n] if len(got) > 1 else got[0]
            bits = tuple(bit for bit in self.bits if bit not in group["fixed"])
            group["terms"].append(
                (self.shaped(recv, bits), bits, 0 if len(got) > 1 else column)
            )
            column += group["columns"]

    def rest(self):
        while self.orders:
            self.accept(self.plain(self.across()))

    def straight(self):
        seq = [bit for bit in self.bits if bit[0] == "seq"]
        jobs = []
        for jump in range(1, self.counts["seq"]):
            flips = {bit: jump // bit[1] % 2 for bit in seq}
            jobs.append(
                [
                    (list(g["terms"]), {**g["fixed"], **flips}, g["columns"])
                    for g in self.groups
                ]
            )
        for group in self.groups:
            group["fixed"].update({bit: 0 for bit in seq})
        if self.rows % 8 == 0:
            return jobs
        self.accept_straight(
            [
                jnp.concatenate(
                    [self.total_at({"terms": t, "columns": c}, flips) for t, flips, c in job],
                    axis=-1,
                ).astype(bf16)
                for job in jobs
            ]
        )
        return []

    def accept_straight(self, values):
        values = list(values)
        if not values:
            return
        self.sent = values
        for jump, value in enumerate(values):
            got = swap(value, "seq", jump + 1, self.counts["seq"])
            column = 0
            for group in self.groups:
                group["terms"].append((self.shaped(got, ()), (), column))
                column += group["columns"]

    def total(self, *tokens):
        groups = None
        if tokens:
            values = [[term[0] for term in group["terms"]] for group in self.groups]
            groups = after(values, *tokens)
        parts = []
        for n, group in enumerate(self.groups):
            terms = group["terms"]
            if groups:
                terms = [(v, t[1], t[2]) for v, t in zip(groups[n], terms)]
            parts.append(
                self.total_at({"terms": terms, "columns": group["columns"]}, group["fixed"])
            )
        return jnp.concatenate(parts, axis=-1)


def body(
    hidden_in,
    segment_ids,
    query_emb,
    positives,
    w_qkv,
    query_bias,
    value_bias,
    w_out,
    out_bias,
    norm1_gain,
    norm1_bias,
    w_up,
    up_bias,
    w_down,
    down_bias,
    norm2_gain,
    norm2_bias,
    w_proj,
):
    micro_count, row_count, local_len, width = hidden_in.shape
    full_len = segment_ids.shape[2]
    embed_width = w_proj.shape[1]
    ff = w_up.shape[1]
    queries_local = query_emb.shape[1]
    query_tokens = query_emb.shape[2]
    seq_count = lax.axis_size("seq")
    dp_count = lax.axis_size("dp")
    seq_pos = lax.axis_index("seq")
    dp_pos = lax.axis_index("dp")
    rows = micro_count * row_count
    tokens = rows * local_len
    far = 64
    window = 3 * local_len + far
    assert local_len + far >= PASSAGE_MOST - 1 and seq_count == 4

    x_own = hidden_in.reshape(rows, local_len, width)
    x_flat = x_own.reshape(tokens, width)
    low_half = seq_pos < 2
    inner = [(1, 2), (2, 1), (0, 0), (3, 3)]
    far_send = jnp.where(low_half, x_own[:, local_len - far :], x_own[:, :far])
    middle_x = lax.ppermute(x_flat, "seq", inner)
    far_x = swap(far_send.reshape(rows * far, width), "seq", 2, seq_count)
    side_x = swap(x_flat, "seq", 1, seq_count)
    pieces = [side_x, middle_x, far_x]

    seg_full = segment_ids.reshape(rows, full_len)
    edges = jnp.sum(
        (seg_full[:, None, :] < jnp.arange(1, SEGS, dtype=jnp.int32)[None, :, None]).astype(
            jnp.int32
        ),
        axis=2,
    )
    meta = jnp.concatenate(
        [
            jnp.stack(
                [
                    seq_pos * local_len,
                    dp_pos,
                    (seq_pos ^ 1) * local_len,
                    jnp.where((seq_pos == 1) | (seq_pos == 2), 3 - seq_pos, -9) * local_len,
                    jnp.where(
                        low_half, (seq_pos + 2) * local_len, (seq_pos - 1) * local_len - far
                    ),
                    dp_pos * row_count * SEGS,
                    dp_pos % 2,
                    seq_pos,
                ]
            ).astype(jnp.int32),
            edges.reshape(-1),
        ]
    )

    queries = query_emb.reshape(micro_count, queries_local * query_tokens, embed_width)
    bits = bits_of(dp_count)
    strides = [bits[:1]] + [bits[k : k + 2] for k in range(1, len(bits), 2)]

    queries = lax.all_gather(queries, "dp", axis=1, tiled=True)
    query_all = queries.shape[1]
    query_count = query_all // query_tokens
    wide = max(128, query_count)
    positives_wide = jnp.pad(
        positives, ((0, 0), (0, wide - query_count)), constant_values=-1
    )

    pairs = width // 128
    chunks = ff // width
    forward = call(
        functools.partial(
            forward_kernel, (rows, local_len, far, window, full_len, width, row_count)
        ),
        [
            ((8 + chunks, width), f32),
            ((tokens, width), bf16),
            ((width, tokens), bf16),
            ((rows, pairs, 2 * local_len), f32),
            ((tokens, 128), f32),
            ((tokens, width), f32),
            ((width, tokens), bf16),
            ((tokens, embed_width), f32),
            ((tokens, embed_width), bf16),
            ((rows * SEGS, query_all), f32),
            ((rows, window, 2 * width), bf16),
            ((rows, width, window), bf16),
            ((tokens, width), f32),
            ((width, tokens), bf16),
            ((chunks, width, tokens), bf16),
            ((chunks, tokens, width), bf16),
        ],
        [
            meta,
            value_bias,
            out_bias,
            norm1_gain,
            norm1_bias,
            down_bias,
            norm2_gain,
            norm2_bias,
            query_bias,
            up_bias,
            w_proj,
            x_flat,
            *pieces,
            queries,
            w_qkv,
            w_out,
            w_up,
            w_down,
        ],
        [
            pltpu.VMEM((window, local_len), f32),
            pltpu.VMEM((tokens, width), bf16),
            pltpu.VMEM((tokens, width), bf16),
            pltpu.VMEM((tokens, width), bf16),
            pltpu.VMEM((tokens, width), bf16),
            pltpu.VMEM((rows * far, width), bf16),
            pltpu.VMEM(queries.shape, bf16),
            pltpu.VMEM((width, 3 * width), bf16),
            pltpu.VMEM((width, width), bf16),
            pltpu.VMEM((chunks, width, width), bf16),
            pltpu.VMEM((chunks, width, width), bf16),
            pltpu.VMEM((rows, window, 2 * width), bf16),
            pltpu.VMEM((rows, width, window), bf16),
            pltpu.VMEM((tokens, width), f32),
            pltpu.VMEM((width, tokens), bf16),
            pltpu.VMEM((chunks, width, tokens), bf16),
            pltpu.VMEM((chunks, tokens, width), bf16),
            pltpu.VMEM((tokens, width), bf16),
            pltpu.VMEM((tokens, width), f32),
            pltpu.SemaphoreType.DMA((11 + 4 * chunks,)),
        ],
        name="forward",
        us=20,
        hbm_ins=9,
        hbm_outs=6,
    )
    vectors, query, context_t, lse, cols, norm2, hidden2_t, proj, embed, parts = forward[:10]
    kv, x_t, norm1, hidden1_t, act_t, slope = forward[10:]

    others = [swap(parts, "seq", bit, seq_count) for bit in (1, 2, 3)]
    stat_rows = 8
    merged, score, stats = call(
        functools.partial(score_kernel, (rows, full_len, row_count, query_tokens)),
        [
            ((rows * SEGS, query_all), f32),
            ((rows * SEGS, wide), f32),
            ((stat_rows, wide), f32),
        ],
        [meta, parts, *others, positives_wide],
        name="score",
        us=2,
    )
    is_whole = lax.broadcasted_iota(jnp.int32, stats.shape, 0) < micro_count
    for group in strides:
        jumps = group if len(group) == 1 else [group[0], group[1], group[0] + group[1]]
        recv = [swap(stats, "dp", jump, dp_count) for jump in jumps]
        if len(recv) == 1:
            best = jnp.maximum(stats, recv[0])
            whole = jnp.exp(stats - best) + jnp.exp(recv[0] - best)
            hits = stats + recv[0]
        else:
            best = jnp.maximum(jnp.maximum(stats, recv[0]), jnp.maximum(recv[1], recv[2]))
            whole = (jnp.exp(stats - best) + jnp.exp(recv[0] - best)) + (
                jnp.exp(recv[1] - best) + jnp.exp(recv[2] - best)
            )
            hits = (stats + recv[0]) + (recv[1] + recv[2])
        stats = jnp.where(is_whole, best + jnp.log(whole), hits)

    devices = dp_count * seq_count

    def places(depth, columns):
        block = depth // dp_count
        if block % 16 == 0:
            return [((dp_count // 2, block, columns), bf16)] * 2
        return [((depth, columns), bf16)]

    where = {"dp": dp_pos, "seq": seq_pos}
    counts = {"dp": dp_count, "seq": seq_count}
    down_places = places(ff, width)
    loss, d_proj, g_resid2, vec_c, *outs = call(
        functools.partial(
            upper_kernel, (rows, local_len, full_len, row_count, query_tokens)
        ),
        [
            ((micro_count, wide), f32),
            ((width, embed_width), bf16),
            ((tokens, width), f32),
            ((8, width), f32),
        ]
        + down_places,
        [
            meta,
            merged,
            score,
            stats,
            positives_wide,
            queries,
            embed,
            proj,
            norm2,
            hidden2_t,
            cols,
            vectors,
            w_proj,
            act_t,
        ],
        [
            pltpu.VMEM((chunks, width, width), bf16),
            pltpu.VMEM((chunks, width, tokens), bf16),
            pltpu.VMEM((rows * SEGS, query_all), f32),
            pltpu.VMEM((tokens, embed_width), f32),
            pltpu.SemaphoreType.DMA((1 + max(dp_count, chunks),)),
        ],
        hbm_ins=1,
        name="upper",
        us=8,
        hbm_outs=len(down_places),
    )
    losses = lax.dynamic_slice_in_dim(loss, dp_pos * queries_local, queries_local, 1)
    down = Chunk(outs, where, counts)
    down.core()

    up_places = places(width, ff + width + embed_width)
    d_ubias, g_resid1, g_context, vec_d, *outs = call(
        lower_kernel,
        [
            ((chunks, 1, width), f32),
            ((tokens, width), f32),
            ((tokens, width), bf16),
            ((8, width), f32),
        ]
        + up_places,
        [
            meta,
            g_resid2,
            hidden1_t,
            norm1,
            cols,
            vectors,
            context_t,
            w_out,
            d_proj,
            w_down,
            w_up,
            slope,
        ],
        [
            pltpu.VMEM((chunks, width, width), bf16),
            pltpu.VMEM((chunks, width, width), bf16),
            pltpu.VMEM((chunks, tokens, width), bf16),
            pltpu.VMEM((tokens, width), f32),
            pltpu.VMEM((tokens, width), bf16),
            pltpu.VMEM((chunks, width, width), bf16),
            pltpu.VMEM((width, width + embed_width), bf16),
            pltpu.SemaphoreType.DMA(((3 + dp_count) * chunks + dp_count,)),
        ],
        name="lower",
        us=13,
        hbm_ins=3,
        hbm_outs=len(up_places),
    )
    up = Chunk(outs, where, counts)
    up.core()

    def fold(chunks_jobs, *tokens, us=FOLD):
        jobs = [job for _, got, _ in chunks_jobs for job in got]
        values = call(nothing, [], [meta], name="fold", deps=tokens, jobs=jobs, us=us) if jobs else []
        at = 0
        sent = []
        for chunk, got, accept in chunks_jobs:
            accept(values[at : at + len(got)])
            at += len(got)
            sent += chunk.sent
        return sent

    sends = fold([(down, down.across(), down.accept)], g_resid1, us=3)
    last_places = places(width, 3 * width + 128)
    sends = fold([(up, up.across(), up.accept)], *sends, us=3)
    g_own, g_side, g_middle, g_far, *outs = call(
        functools.partial(
            attention_kernel, (rows, local_len, far, window, full_len, width, devices)
        ),
        [
            ((tokens, width), f32),
            ((tokens, width), bf16),
            ((tokens, width), bf16),
            ((rows * far, width), bf16),
        ]
        + last_places,
        [meta, g_context, query, lse, vec_c, vec_d, d_ubias, g_resid1, kv, x_t, w_qkv],
        [
            pltpu.VMEM((rows, window, 2 * width), bf16),
            pltpu.VMEM((rows, width, window), bf16),
            pltpu.VMEM((tokens, width), bf16),
            pltpu.VMEM((rows, window, 2 * width), bf16),
            pltpu.VMEM((width, 3 * width), bf16),
            pltpu.VMEM((window, local_len), f32),
            pltpu.VMEM((3, width, width), bf16),
            pltpu.VMEM((width, 128), bf16),
            pltpu.VMEM((width, 128), f32),
            pltpu.SemaphoreType.DMA((rows + 2 + 4 * dp_count,)),
        ],
        name="attention",
        us=20,
        hbm_ins=3,
        hbm_outs=len(last_places),
        deps=sends,
    )
    last = Chunk(outs, where, counts)
    from_middle = lax.ppermute(g_middle, "seq", inner)
    down.wait(g_own)
    down.accept(down.plain(down.across()))
    up.wait(*down.sent)
    last.other = after(last.other, [term[0] for group in up.groups for term in group["terms"]])
    last.core()
    up.accept(up.plain(up.across()))
    fold([(last, last.across(), last.accept)], *up.sent)
    up.rest()
    down.rest()
    g_side, from_middle = after((g_side, from_middle))
    from_side = swap(g_side, "seq", 1, seq_count)
    down.wait(*last.sent)
    down.accept(down.plain(down.along(1)))
    up.wait(*down.sent)
    up.accept(up.plain(up.along(1)))
    down.wait(*up.sent)
    down.accept(down.plain(down.along(2)))
    last.wait(*down.sent)
    last.accept(last.plain(last.across()))
    last.rest()
    g_far, from_side = after((g_far, from_side))
    from_far = swap(g_far, "seq", 2, seq_count)
    up.wait(*last.sent)
    up.accept(up.plain(up.along(2)))
    sends = fold([(last, last.straight(), last.accept_straight)], *up.sent)
    g_own, from_side, from_middle, from_far = after(
        (g_own, from_side, from_middle, from_far), *sends
    )
    from_far = from_far.reshape(rows, far, width).astype(f32)
    pad = ((0, 0), (local_len - far, 0), (0, 0))
    flip = ((0, 0), (0, local_len - far), (0, 0))
    grad_in = (g_own + from_side.astype(f32) + from_middle.astype(f32)).reshape(
        rows, local_len, width
    ) + jnp.where(low_half, jnp.pad(from_far, pad), jnp.pad(from_far, flip))

    down_part = down.total(grad_in)
    up_part = up.total(down_part)
    last_part = last.total(up_part)
    some = 4 * width // devices
    vec_at = 3 * width
    vec_part = last_part[:3, vec_at : vec_at + some]
    return (
        embed.reshape(micro_count, row_count, local_len, embed_width),
        losses,
        grad_in.reshape(micro_count, row_count, local_len, width),
        last_part[:, : 3 * width].reshape(-1),
        up_part[:, ff : ff + width].reshape(-1),
        up_part[:, :ff].reshape(-1),
        down_part.reshape(-1),
        up_part[:, ff + width :].reshape(-1),
        vec_part[0],
        vec_part[1:].reshape(-1),
    )


def solution(mesh):
    in_specs = (
        P(None, "dp", "seq", None),
        P(None, "dp", None),
        P(None, "dp", None, None),
    ) + (P(),) * 15
    out_specs = (
        P(None, "dp", "seq", None),
        P(None, "dp"),
        P(None, "dp", "seq", None),
    ) + (P(("dp", "seq")),) * 7
    return jax.shard_map(body, mesh=mesh, in_specs=in_specs, out_specs=out_specs, check_vma=False)
```

```python
import functools

import jax
import jax.numpy as jnp
from jax import lax
from jax.experimental import pallas as pl
from jax.experimental.pallas import tpu as pltpu
from jax.sharding import PartitionSpec as P

HEADS = 12
SEGS = 4
PASSAGE_MOST = 180

SHARP = 20.0
EDGES = 8
COST = 4e9
FOLD = 0.3
ORDER = (
    "M", "A2", "C0", "B2", "m", "S", "C1", "A3", "s", "F", "B3", "A4", "C2", "B4", "C3", "f",
)
LN_EPS = 1e-12
NORM_EPS = 1e-12
MASKED = -1e30
HIGH = lax.Precision.HIGHEST
bf16 = jnp.bfloat16
f32 = jnp.float32
VMEM = pl.BlockSpec(memory_space=pltpu.VMEM)
HBM = pl.BlockSpec(memory_space=pltpu.HBM)
SMEM = pl.BlockSpec(memory_space=pltpu.SMEM)
PARAMS = pltpu.CompilerParams(vmem_limit_bytes=58 << 20)


def bits_of(count):
    return [1 << k for k in range(count.bit_length() - 1)]


def swap(value, axis, bit, count):
    return lax.ppermute(value, axis, [(i, i ^ bit) for i in range(count)])


def dot(left, right, left_dim, right_dim, precision=None):
    return lax.dot_general(
        left,
        right,
        (((left_dim,), (right_dim,)), ((), ())),
        precision=precision,
        preferred_element_type=f32,
    )


def ident(pos, meta, row, length):
    seg = jnp.zeros(pos.shape, jnp.int32)
    for s in range(SEGS - 1):
        seg = seg + (pos >= meta[EDGES + row * (SEGS - 1) + s]).astype(jnp.int32)
    return jnp.where((pos >= 0) & (pos < length), seg, -1)


def key_positions(meta, local, shape):
    w = lax.broadcasted_iota(jnp.int32, shape, 0)
    pos = meta[0] + w
    for piece in range(1, 4):
        pos = jnp.where(w >= piece * local, meta[1 + piece] + w - piece * local, pos)
    return pos


def pair_rows(block, even):
    zero = jnp.zeros_like(block)
    return jnp.concatenate([jnp.where(even, block, zero), jnp.where(even, zero, block)], axis=0)


def attention_bias(meta, row, local, window, length):
    key_seg = ident(key_positions(meta, local, (window, local)), meta, row, length)
    query_seg = ident(
        meta[0] + lax.broadcasted_iota(jnp.int32, (window, local), 1), meta, row, length
    )
    return jnp.where(key_seg == query_seg, 0.0, MASKED).astype(f32)


def copies_out(scr, outs, sems, first, core, columns, part=0, parts=1):
    size = scr.shape[0]
    if len(outs) == 1:
        pieces = [(scr, outs[0].at[pl.ds(part * size, size), columns])]
    else:
        high, block, _ = outs[0].shape
        pieces = []
        for k in range(high // parts):
            for out, which in ((outs[0], 1 - core), (outs[1], core)):
                rows = pl.ds(pl.multiple_of((2 * k + which) * block, 16), block)
                pieces.append((scr.at[rows, :], out.at[part * (high // parts) + k, :, columns]))
    return [
        pltpu.make_async_copy(source, target, sems.at[first + n])
        for n, (source, target) in enumerate(pieces)
    ]


def begin(copies):
    for copy in copies:
        copy.start()


def finish(copies):
    for copy in copies:
        copy.wait()


def forward_kernel(
    dims,
    meta,
    value_bias_in,
    out_bias_in,
    gain1_in,
    shift1_in,
    down_bias_in,
    gain2_in,
    shift2_in,
    query_bias_in,
    up_bias_in,
    w_proj,
    x_own_hbm,
    side_hbm,
    middle_hbm,
    far_hbm,
    queries_hbm,
    w_qkv_hbm,
    w_out_hbm,
    w_up_hbm,
    w_down_hbm,
    vectors,
    query,
    context_t,
    lse,
    cols,
    norm2,
    hidden2_t,
    proj,
    embed,
    parts,
    kv_hbm,
    x_t_hbm,
    norm1_hbm,
    hidden1_t_hbm,
    act_t_hbm,
    slope_hbm,
    bias_scr,
    context,
    x_own,
    side,
    middle,
    far_part,
    queries,
    w_qkv,
    w_out,
    w_up,
    w_down,
    kv,
    x_t,
    norm1,
    hidden1_t,
    act_t,
    slope,
    hidden_scr,
    ffn_scr,
    sems,
):
    rows, local, far, window, length, width, row_count = dims
    chunks = w_up.shape[0]
    kv_here = pltpu.make_async_copy(w_qkv_hbm, w_qkv, sems.at[0])
    out_here = pltpu.make_async_copy(w_out_hbm, w_out, sems.at[1])

    def up_here(c):
        cut = pl.ds(pl.multiple_of(c * width, 128), width)
        return pltpu.make_async_copy(w_up_hbm.at[:, cut], w_up.at[c], sems.at[2 + c])

    def down_here(c):
        cut = pl.ds(pl.multiple_of(c * width, 128), width)
        return pltpu.make_async_copy(
            w_down_hbm.at[cut, :], w_down.at[c], sems.at[2 + chunks + c]
        )

    base = 2 + 2 * chunks
    pieces_here = [
        pltpu.make_async_copy(source, target, sems.at[base + 4 + 2 * chunks + n])
        for n, (source, target) in enumerate(
            ((x_own_hbm, x_own), (side_hbm, side), (middle_hbm, middle), (far_hbm, far_part))
        )
    ]
    queries_here = pltpu.make_async_copy(
        queries_hbm, queries, sems.at[base + 8 + 2 * chunks]
    )
    begin([pieces_here[0], kv_here] + pieces_here[1:] + [out_here])
    for c in range(chunks):
        begin([up_here(c), down_here(c)])
    queries_here.start()
    for n, vector in enumerate(
        (
            value_bias_in,
            out_bias_in,
            gain1_in,
            shift1_in,
            down_bias_in,
            gain2_in,
            shift2_in,
        )
    ):
        vectors[n : n + 1, :] = vector[...].reshape(1, width)
    for c in range(chunks):
        vectors[7 + c : 8 + c, :] = up_bias_in[pl.ds(c * width, width)].reshape(1, width)
    vectors[7 + chunks : 8 + chunks, :] = query_bias_in[...].reshape(1, width)
    value_bias = vectors[0:1, :]
    kv_out = pltpu.make_async_copy(kv, kv_hbm, sems.at[base])
    x_out = pltpu.make_async_copy(x_t, x_t_hbm, sems.at[base + 1])
    norm_out = pltpu.make_async_copy(norm1, norm1_hbm, sems.at[base + 2])
    hidden_out = pltpu.make_async_copy(hidden1_t, hidden1_t_hbm, sems.at[base + 3])

    def act_out(c):
        return pltpu.make_async_copy(act_t.at[c], act_t_hbm.at[c], sems.at[base + 4 + c])

    def slope_out(c):
        return pltpu.make_async_copy(
            slope.at[c], slope_hbm.at[c], sems.at[base + 4 + chunks + c]
        )

    finish([pieces_here[0], kv_here])
    query[...] = (dot(x_own[...], w_qkv[:, :width], 1, 0) + vectors[7 + chunks : 8 + chunks, :]).astype(
        bf16
    )
    offset = 0
    for n, (piece, size) in enumerate(
        ((x_own, local), (side, local), (middle, local), (far_part, far))
    ):
        if n:
            pieces_here[n].wait()
        got = dot(piece[...], w_qkv[:, width:], 1, 0)
        got_k = got[:, :width].astype(bf16)
        got_v = (got[:, width:] + value_bias).astype(bf16)
        for r in range(rows):
            mine = slice(r * size, (r + 1) * size)
            kv[r, offset : offset + size, :width] = got_k[mine]
            kv[r, offset : offset + size, width:] = got_v[mine]
            x_t[r, :, offset : offset + size] = piece[mine, :].T
        offset += size
    begin([kv_out, x_out])
    even = lax.broadcasted_iota(jnp.int32, (local, 128), 1) < 64
    upper = lax.broadcasted_iota(jnp.int32, (128, local), 0) < 64
    pairs = width // 128

    def attend(r, carry):
        bias_scr[...] = attention_bias(meta, r, local, window, length)
        own = pl.ds(pl.multiple_of(r * local, 128), local)
        for p in range(pairs):
            lanes = slice(p * 128, (p + 1) * 128)
            q2 = pair_rows(query[own, lanes] * bf16(0.125), even)
            k2 = kv[r, :, lanes]
            v2 = kv[r, :, width + p * 128 : width + (p + 1) * 128]
            bias = bias_scr[...]
            s = dot(k2, q2, 1, 1) + jnp.concatenate([bias, bias], axis=1)
            top = jnp.max(s, axis=0, keepdims=True)
            e = jnp.exp(s - top)
            total = jnp.sum(e, axis=0, keepdims=True)
            lse[r, p : p + 1, :] = top + jnp.log(total)
            o = dot(v2, e.astype(bf16), 0, 0) * (1.0 / total)
            o = jnp.where(upper, o[:, :local], o[:, local:])
            context_t[lanes, own] = o.astype(bf16)
            context[own, lanes] = o.T.astype(bf16)
        return carry

    lax.fori_loop(0, rows, attend, 0)
    out_here.wait()
    attended = dot(context[...], w_out[...], 1, 0) + vectors[1:2, :]
    resid = x_own[...].astype(f32) + attended
    centred = resid - jnp.mean(resid, axis=-1, keepdims=True)
    rstd1 = lax.rsqrt(jnp.mean(centred * centred, axis=-1, keepdims=True) + LN_EPS)
    n1 = centred * rstd1
    norm1[...] = n1
    hidden1 = n1 * vectors[2:3, :] + vectors[3:4, :]
    hidden1_low = hidden1.astype(bf16)
    hidden1_t[...] = hidden1_low.T
    begin([norm_out, hidden_out])
    hidden_scr[...] = hidden1_low
    ffn_scr[...] = hidden1 + vectors[4:5, :]

    def feed(c, carry):
        up_here(c).wait()
        up = dot(hidden_scr[...], w_up[c], 1, 0) + vectors[pl.ds(7 + c, 1), :]
        cdf = 0.5 * (1.0 + lax.erf(up * (0.5**0.5)))
        act_low = (up * cdf).astype(bf16)
        act_t[c] = act_low.T
        slope[c] = (cdf + up * (jnp.exp(-0.5 * up * up) * 0.3989422804014327)).astype(bf16)
        begin([act_out(c), slope_out(c)])
        down_here(c).wait()
        ffn_scr[...] += dot(act_low, w_down[c], 1, 0)
        return carry

    lax.fori_loop(0, chunks, feed, 0)
    resid = ffn_scr[...]
    centred = resid - jnp.mean(resid, axis=-1, keepdims=True)
    rstd2 = lax.rsqrt(jnp.mean(centred * centred, axis=-1, keepdims=True) + LN_EPS)
    n2 = centred * rstd2
    norm2[...] = n2
    lane = lax.broadcasted_iota(jnp.int32, cols.shape, 1)
    cols[...] = jnp.where(lane == 0, rstd1, rstd2)
    hidden2_low = (n2 * vectors[5:6, :] + vectors[6:7, :]).astype(bf16)
    hidden2_t[...] = hidden2_low.T
    out = dot(hidden2_low, w_proj[...], 1, 0)
    proj[...] = out
    inv = lax.rsqrt(jnp.sum(out * out, axis=-1, keepdims=True) + NORM_EPS)
    embed[...] = (out * inv).astype(bf16)

    def match(r, carry):
        own = pl.ds(pl.multiple_of(r * local, 128), local)
        sharp = dot(embed[own, :], queries[r // row_count], 1, 1) * SHARP
        seg = ident(meta[0] + lax.broadcasted_iota(jnp.int32, (local, 1), 0), meta, r, length)
        tops = []
        shift = jnp.zeros_like(sharp)
        for s in range(SEGS):
            inside = seg == s
            top = jnp.max(jnp.where(inside, sharp, MASKED), axis=0, keepdims=True)
            tops.append(top)
            shift = jnp.where(inside, top, shift)
        e = jnp.exp(sharp - shift)
        for s in range(SEGS):
            total = jnp.sum(jnp.where(seg == s, e, 0.0), axis=0, keepdims=True)
            some = total > 0.0
            parts[pl.ds(r * SEGS + s, 1), :] = jnp.where(
                some, tops[s] + jnp.log(jnp.where(some, total, 1.0)), MASKED
            )
        return carry

    queries_here.wait()
    lax.fori_loop(0, rows, match, 0)
    finish([kv_out, x_out, norm_out, hidden_out])
    for c in range(chunks):
        finish([act_out(c), slope_out(c)])


def score_kernel(dims, meta, first, second, third, fourth, positives, merged, score, stats):
    rows, length, row_count, query_tokens = dims
    half = rows * SEGS
    parts = [ref[...] for ref in (first, second, third, fourth)]
    top = jnp.maximum(jnp.maximum(parts[0], parts[1]), jnp.maximum(parts[2], parts[3]))
    sums = [jnp.exp(part - top) for part in parts]
    whole = top + jnp.log((sums[0] + sums[1]) + (sums[2] + sums[3]))
    merged[...] = whole
    sub = lax.broadcasted_iota(jnp.int32, (half, 1), 0)
    count = jnp.zeros((half, 1), f32)
    for r in range(rows):
        edges = [0] + [meta[EDGES + r * (SEGS - 1) + s] for s in range(SEGS - 1)] + [length]
        for s in range(SEGS):
            size = (edges[s + 1] - edges[s]).astype(f32)
            count = jnp.where(sub == r * SEGS + s, size, count)
    match = whole - jnp.log(count)
    wide = score.shape[1]
    shape = (match.shape[1], wide)
    group = (
        lax.broadcasted_iota(jnp.int32, shape, 0) // query_tokens
        == lax.broadcasted_iota(jnp.int32, shape, 1)
    ).astype(f32)
    got = dot(match, group, 1, 0, HIGH)
    score[...] = got
    per = row_count * SEGS
    micros = rows // row_count
    stats[...] = jnp.zeros(stats.shape, f32)
    for m in range(micros):
        part = got[m * per : (m + 1) * per]
        at = lax.broadcasted_iota(jnp.int32, (per, wide), 0) + meta[5]
        chosen = at == positives[m : m + 1, :]
        best = jnp.max(part, axis=0, keepdims=True)
        stats[m : m + 1, :] = best + jnp.log(
            jnp.sum(jnp.exp(part - best), axis=0, keepdims=True)
        )
        stats[micros + m : micros + m + 1, :] = jnp.sum(
            jnp.where(chosen, part, 0.0), axis=0, keepdims=True
        )


def upper_kernel(
    dims,
    meta,
    merged,
    score,
    stats,
    positives,
    queries,
    embed,
    proj,
    norm2,
    hidden2_t,
    cols,
    vectors,
    w_proj,
    act_t_hbm,
    loss,
    d_proj,
    g_resid2,
    vec,
    *rest,
):
    outs, (scr, act_t, factor_scr, unit_scr, sems) = rest[:-5], rest[-5:]
    rows, local, length, row_count, query_tokens = dims
    chunks = act_t.shape[0]
    gain2 = vectors[5:6, :]
    act_here = pltpu.make_async_copy(act_t_hbm, act_t, sems.at[0])
    act_here.start()
    micros = rows // row_count
    per = row_count * SEGS
    wide = score.shape[1]
    all_queries = merged.shape[1]
    shape = (wide, all_queries)
    group = (
        lax.broadcasted_iota(jnp.int32, shape, 1) // query_tokens
        == lax.broadcasted_iota(jnp.int32, shape, 0)
    ).astype(f32)
    pieces = []
    for m in range(micros):
        whole = stats[m : m + 1, :]
        loss[m : m + 1, :] = whole - stats[micros + m : micros + m + 1, :]
        part = score[m * per : (m + 1) * per, :]
        at = lax.broadcasted_iota(jnp.int32, (per, wide), 0) + meta[5]
        chosen = (at == positives[m : m + 1, :]).astype(f32)
        pieces.append(jnp.exp(part - whole) - chosen)
    factor_scr[...] = SHARP * dot(jnp.concatenate(pieces, axis=0), group, 1, 0, HIGH)

    def pull(r, carry):
        own = pl.ds(pl.multiple_of(r * local, 128), local)
        m = r // row_count
        sharp = dot(embed[own, :], queries[m], 1, 1) * SHARP
        seg = ident(meta[0] + lax.broadcasted_iota(jnp.int32, (local, 1), 0), meta, r, length)
        shift = jnp.zeros_like(sharp)
        scale = jnp.zeros_like(sharp)
        for s in range(SEGS):
            at = pl.ds(r * SEGS + s, 1)
            shift = jnp.where(seg == s, merged[at, :], shift)
            scale = jnp.where(seg == s, factor_scr[at, :], scale)
        g_sim = (scale * jnp.exp(sharp - shift)).astype(bf16)
        unit_scr[own, :] = dot(g_sim, queries[m], 1, 0)
        return carry

    lax.fori_loop(0, rows, pull, 0)
    g_unit = unit_scr[...]
    out = proj[...]
    inv = lax.rsqrt(jnp.sum(out * out, axis=-1, keepdims=True) + NORM_EPS)
    unit = out * inv
    g_proj = ((g_unit - unit * jnp.sum(unit * g_unit, axis=-1, keepdims=True)) * inv).astype(bf16)
    n2 = norm2[...]
    d_proj[...] = dot(hidden2_t[...], g_proj, 1, 0).astype(bf16)
    g_hidden = dot(g_proj, w_proj[...], 1, 1)
    vec[0:1, :] = jnp.sum(g_hidden * n2, axis=0, keepdims=True)
    vec[1:2, :] = jnp.sum(g_hidden, axis=0, keepdims=True)
    g_n = g_hidden * gain2
    g_v = cols[:, 1:2] * (
        g_n
        - jnp.mean(g_n, axis=-1, keepdims=True)
        - n2 * jnp.mean(g_n * n2, axis=-1, keepdims=True)
    )
    g_resid2[...] = g_v
    low = g_v.astype(bf16)
    vec[2:3, :] = jnp.sum(low.astype(f32), axis=0, keepdims=True)
    act_here.wait()
    columns = slice(0, scr.shape[2])
    each = 2 * (outs[0].shape[0] // chunks) if len(outs) == 2 else 1

    def leaving(c):
        return copies_out(scr.at[c], outs, sems, 1 + c * each, meta[6], columns, c, chunks)

    for c in range(chunks):
        scr[c] = dot(act_t[c], low, 1, 0).astype(bf16)
        begin(leaving(c))
    for c in range(chunks):
        finish(leaving(c))


def lower_kernel(
    meta,
    g_resid2,
    hidden1_t,
    norm1,
    cols,
    vectors,
    context_t,
    w_out,
    d_proj,
    w_down_hbm,
    w_up_hbm,
    slope_hbm,
    d_ubias,
    g_resid1,
    g_context,
    vec,
    *rest,
):
    outs, (w_down, w_up, slope, hidden_scr, low_scr, scr, out_scr, sems) = rest[:-8], rest[-8:]
    chunks, width, _ = w_up.shape
    gain1 = vectors[2:3, :]
    each = 2 * outs[0].shape[0] if len(outs) == 2 else 1

    def here(c):
        cut = pl.ds(pl.multiple_of(c * width, 128), width)
        return [
            pltpu.make_async_copy(w_down_hbm.at[cut, :], w_down.at[c], sems.at[3 * c]),
            pltpu.make_async_copy(slope_hbm.at[c], slope.at[c], sems.at[3 * c + 1]),
            pltpu.make_async_copy(w_up_hbm.at[:, cut], w_up.at[c], sems.at[3 * c + 2]),
        ]

    def leaving(c):
        cut = pl.ds(pl.multiple_of(c * width, 128), width)
        return copies_out(scr.at[c], outs, sems, 3 * chunks + c * each, meta[6], cut)

    for c in range(chunks):
        begin(here(c))
    hidden_scr[...] = g_resid2[...]
    low_scr[...] = g_resid2[...].astype(bf16)

    def gate(c, carry):
        finish(here(c))
        g_act = dot(low_scr[...], w_down[c], 1, 1)
        g_up = (g_act * slope[c].astype(f32)).astype(bf16)
        d_ubias[c] = jnp.sum(g_up.astype(f32), axis=0, keepdims=True)
        scr[c] = dot(hidden1_t[...], g_up, 1, 0).astype(bf16)
        begin(leaving(c))
        hidden_scr[...] += dot(g_up, w_up[c], 1, 1)
        return carry

    lax.fori_loop(0, chunks, gate, 0)
    n1 = norm1[...]
    g_hidden = hidden_scr[...]
    vec[0:1, :] = jnp.sum(g_hidden * n1, axis=0, keepdims=True)
    vec[1:2, :] = jnp.sum(g_hidden, axis=0, keepdims=True)
    g_n = g_hidden * gain1
    g_v = cols[:, 0:1] * (
        g_n
        - jnp.mean(g_n, axis=-1, keepdims=True)
        - n1 * jnp.mean(g_n * n1, axis=-1, keepdims=True)
    )
    g_resid1[...] = g_v
    low = g_v.astype(bf16)
    vec[2:3, :] = jnp.sum(low.astype(f32), axis=0, keepdims=True)
    out_scr[:, :width] = dot(context_t[...], low, 1, 0).astype(bf16)
    out_scr[:, width:] = d_proj[...]
    columns = slice(chunks * width, chunks * width + out_scr.shape[1])
    last = copies_out(out_scr, outs, sems, (3 + each) * chunks, meta[6], columns)
    begin(last)
    g_context[...] = dot(low, w_out[...], 1, 1).astype(bf16)
    for c in range(chunks):
        finish(leaving(c))
    finish(last)


def attention_kernel(
    dims,
    meta,
    g_context,
    query,
    lse,
    vec_c,
    vec_d,
    d_ubias,
    g_resid1,
    kv_hbm,
    x_t_hbm,
    w_qkv_hbm,
    g_own,
    g_side,
    g_middle,
    g_far,
    *rest,
):
    outs, scratch = rest[:-10], rest[-10:]
    kv, x_t, g_query, g_kv, w_qkv, bias_scr, scr, low_scr, vec_scr, sems = scratch
    rows, local, far, window, length, width, devices = dims
    pairs = width // 128
    even = lax.broadcasted_iota(jnp.int32, (local, 128), 1) < 64
    upper = lax.broadcasted_iota(jnp.int32, (128, local), 0) < 64

    def kv_here(r):
        return pltpu.make_async_copy(kv_hbm.at[r], kv.at[r], sems.at[r])

    for r in range(rows):
        kv_here(r).start()
    x_here = pltpu.make_async_copy(x_t_hbm, x_t, sems.at[rows])
    w_here = pltpu.make_async_copy(w_qkv_hbm, w_qkv, sems.at[rows + 1])
    begin([x_here, w_here])

    def attend(r, carry):
        kv_here(r).wait()
        bias_scr[...] = attention_bias(meta, r, local, window, length)
        own = pl.ds(pl.multiple_of(r * local, 128), local)
        for p in range(pairs):
            lanes = slice(p * 128, (p + 1) * 128)
            vlanes = slice(width + p * 128, width + (p + 1) * 128)
            q2 = pair_rows(query[own, lanes] * bf16(0.125), even)
            k2 = kv[r, :, lanes]
            v2 = kv[r, :, vlanes]
            gc2 = pair_rows(g_context[own, lanes], even)
            bias = bias_scr[...]
            s = dot(k2, q2, 1, 1) + jnp.concatenate([bias, bias], axis=1)
            prob = jnp.exp(s - lse[r, p : p + 1, :])
            g_prob = dot(v2, gc2, 1, 1)
            weighted = prob * g_prob
            inner = jnp.sum(weighted, axis=0, keepdims=True)
            g_score = (weighted - prob * inner).astype(bf16)
            g_kv[r, :, vlanes] = dot(prob.astype(bf16), gc2, 1, 0).astype(bf16)
            g_kv[r, :, lanes] = dot(g_score, q2, 1, 0).astype(bf16)
            g_q = dot(k2, g_score, 0, 0)
            g_q = jnp.where(upper, g_q[:, :local], g_q[:, local:]) * 0.125
            g_query[own, lanes] = g_q.T.astype(bf16)
        return carry

    lax.fori_loop(0, rows, attend, 0)
    x_here.wait()
    each = 2 * outs[0].shape[0] if len(outs) == 2 else 1
    copies = []
    for c in range(3):
        total = None
        for r in range(rows):
            if c == 0:
                part = dot(x_t[r, :, :local], g_query[r * local : (r + 1) * local, :], 1, 0)
            else:
                part = dot(x_t[r], g_kv[r, :, (c - 1) * width : c * width], 1, 0)
            total = part if total is None else total + part
        scr[c] = total.astype(bf16)
        columns = slice(c * width, (c + 1) * width)
        got = copies_out(scr.at[c], outs, sems, rows + 2 + c * each, meta[6], columns)
        begin(got)
        copies += got
    d_qbias = jnp.sum(g_query[...].astype(f32), axis=0, keepdims=True)
    d_vbias = None
    for r in range(rows):
        part = jnp.sum(g_kv[r, :, width:].astype(f32), axis=0, keepdims=True)
        d_vbias = part if d_vbias is None else d_vbias + part
    lower = [d_qbias, d_vbias, vec_d[2:3, :], vec_d[0:1, :]]
    higher = [vec_d[1:2, :], vec_c[2:3, :], vec_c[0:1, :], vec_c[1:2, :]]
    higher += [d_ubias[c] for c in range(d_ubias.shape[0])]
    block = width // devices
    some = 4 * width // devices
    vec_scr[...] = jnp.zeros(vec_scr.shape, f32)
    for device in range(devices):
        for row, vectors, start in (
            (0, lower, device * some),
            (1, higher, 2 * device * some),
            (2, higher, (2 * device + 1) * some),
        ):
            source = vectors[start // width]
            at = start % width
            vec_scr[device * block + row : device * block + row + 1, :some] = source[
                :, at : at + some
            ]
    low_scr[...] = vec_scr[...].astype(bf16)
    columns = slice(3 * width, 3 * width + 128)
    got = copies_out(low_scr, outs, sems, rows + 2 + 3 * each, meta[6], columns)
    begin(got)
    w_here.wait()

    def back(r, carry):
        own = pl.ds(pl.multiple_of(r * local, 128), local)
        part = dot(g_kv[r], w_qkv[:, width:], 1, 1)
        g_own[own, :] = (
            g_resid1[own, :] + dot(g_query[own, :], w_qkv[:, :width], 1, 1) + part[:local]
        )
        g_side[own, :] = part[local : 2 * local].astype(bf16)
        g_middle[own, :] = part[2 * local : 3 * local].astype(bf16)
        g_far[pl.ds(pl.multiple_of(r * far, 64), far), :] = part[3 * local :].astype(bf16)
        return carry

    lax.fori_loop(0, rows, back, 0)
    finish(copies + got)


def nothing(meta):
    del meta


def job_index(meta, bits, fixed):
    index = []
    for bit in bits:
        if bit in fixed:
            axis, stride = bit
            at = (meta[1] if axis == "dp" else meta[7]) // stride % 2
            index.append(1 - at if fixed[bit] else at)
        else:
            index.append(slice(None))
    return tuple(index)


def call(
    kernel,
    outs,
    ins,
    scratch=(),
    name=None,
    hbm_outs=0,
    hbm_ins=0,
    deps=(),
    jobs=(),
    us=3,
):
    deps = tuple(deps)
    count = len(ins)
    job_ins, job_outs, job_scratch, job_scratch_out = [], [], [], []
    for job in jobs:
        columns = 0
        for terms, fixed, size in job:
            for value, bits, column in terms:
                free = len([bit for bit in bits if bit not in fixed])
                shape = (2,) * free + (value.shape[-2], size)
                job_ins.append(value)
                job_scratch.append(pltpu.VMEM(shape, bf16))
            columns += size
        job_outs.append((shape[:-1] + (columns,), bf16))
        job_scratch_out.append(pltpu.VMEM(shape[:-1] + (columns,), bf16))
    extra = [pltpu.SemaphoreType.DMA((len(job_ins) + len(jobs),))] if jobs else []
    out_count, scratch_count = len(outs), len(scratch)

    def run(*refs):
        refs = list(refs)

        def pop(number):
            got, refs[:] = refs[:number], refs[number:]
            return got

        mine = pop(count)
        sources = pop(len(job_ins))
        pop(len(deps))
        mine += pop(out_count)
        targets = pop(len(job_outs))
        mine += pop(scratch_count)
        buffers = pop(len(job_ins))
        results = pop(len(job_outs))
        copies = []
        n = 0
        for job in jobs:
            for terms, fixed, size in job:
                for value, bits, column in terms:
                    index = job_index(mine[0], bits, fixed) + (slice(None), pl.ds(column, size))
                    copies.append(
                        pltpu.make_async_copy(sources[n].at[index], buffers[n], refs[0].at[n])
                    )
                    n += 1
        begin(copies)
        kernel(*mine)
        n = 0
        leaving = []
        for job, target, final in zip(jobs, results, targets):
            column = 0
            for terms, fixed, size in job:
                finish(copies[n : n + len(terms)])
                lead = target.shape[:-2]
                for flat in range(2 ** len(lead)):
                    at = tuple((flat >> k) % 2 for k in range(len(lead)))
                    total = None
                    for buffer in buffers[n : n + len(terms)]:
                        part = buffer[at].astype(f32)
                        total = part if total is None else total + part
                    target[at + (slice(None), slice(column, column + size))] = total.astype(bf16)
                n += len(terms)
                column += size
            leaving.append(
                pltpu.make_async_copy(target, final, refs[0].at[len(job_ins) + len(leaving)])
            )
            leaving[-1].start()
        finish(leaving)

    return pl.pallas_call(
        run,
        out_shape=tuple(jax.ShapeDtypeStruct(s, k) for s, k in list(outs) + job_outs),
        in_specs=[SMEM]
        + [VMEM] * (count - 1 - hbm_ins)
        + [HBM] * (hbm_ins + len(job_ins) + len(deps)),
        out_specs=tuple(
            [VMEM] * (out_count - hbm_outs) + [HBM] * (hbm_outs + len(job_outs))
        ),
        scratch_shapes=list(scratch) + job_scratch + job_scratch_out + extra,
        cost_estimate=pl.CostEstimate(flops=int(us * COST), transcendentals=0, bytes_accessed=1),
        compiler_params=PARAMS,
        name=name,
    )(*ins, *job_ins, *deps)


def after(values, *tokens):
    return lax.optimization_barrier((values, tokens))[0]


class Chunk:
    def __init__(self, outs, where, counts):
        self.where, self.counts = where, counts
        if len(outs) == 2:
            self.other, self.mine = outs
        else:
            full = outs[0]
            dp_count = counts["dp"]
            parts = full.reshape(dp_count // 2, 2, full.shape[0] // dp_count, full.shape[1])
            core = where["dp"] % 2
            self.other = lax.dynamic_index_in_dim(parts, 1 - core, 1, keepdims=False)
            self.mine = lax.dynamic_index_in_dim(parts, core, 1, keepdims=False)
        self.bits = [("dp", bit) for bit in bits_of(counts["dp"])[:0:-1]]
        self.bits += [("seq", bit) for bit in bits_of(counts["seq"])[::-1]]
        self.rows = self.mine.shape[1] // counts["seq"]

    def core(self):
        recv = self.recv = swap(self.other, "dp", 1, self.counts["dp"])
        columns = recv.shape[-1]
        half = columns // 256 * 128
        both = [self.shaped(value, self.bits) for value in (self.mine, recv)]
        self.groups = [
            {"terms": [(v, tuple(self.bits), at) for v in both], "fixed": {}, "columns": size}
            for at, size in ((0, half), (half, columns - half))
        ]
        order = [bit for bit in self.bits if bit[0] == "dp"]
        self.orders = list(zip(order[::-1], order))

    def shaped(self, value, bits):
        return value.reshape((2,) * len(bits) + (self.rows, value.shape[-1]))

    def total_at(self, group, flips):
        total = None
        for value, bits, column in group["terms"]:
            start, size = [], []
            for bit in bits:
                at = (self.where[bit[0]] // bit[1]) % 2
                start.append((1 - at if flips[bit] else at) if bit in flips else 0)
                size.append(1 if bit in flips else 2)
            part = lax.dynamic_slice(
                value, start + [0, column], size + [self.rows, group["columns"]]
            )
            free = [n for n in size if n > 1]
            part = part.reshape(free + [self.rows, group["columns"]]).astype(f32)
            total = part if total is None else total + part
        return total

    def jobs(self, bits, joint):
        parts = []
        for group, bit in zip(self.groups, bits):
            parts.append((list(group["terms"]), {**group["fixed"], bit: 1}, group["columns"]))
            group["fixed"][bit] = 0
        self.todo = list(bits[:1]) if joint else list(bits)
        jobs = [parts] if joint else [[part] for part in parts]
        if self.rows % 8 == 0:
            return jobs
        self.accept(
            [
                jnp.concatenate(
                    [
                        self.total_at({"terms": t, "columns": c}, flips)
                        for t, flips, c in job
                    ],
                    axis=-1,
                ).astype(bf16)
                for job in jobs
            ]
        )
        return []

    def across(self):
        return self.jobs(self.orders.pop(0), False)

    def along(self, index):
        return self.jobs([("seq", index)] * len(self.groups), True)

    def plain(self, jobs):
        return [
            jnp.concatenate(
                [self.total_at({"terms": t, "columns": c}, flips) for t, flips, c in job], axis=-1
            ).astype(bf16)
            for job in jobs
        ]

    def wait(self, *tokens):
        values = after([[t[0] for t in group["terms"]] for group in self.groups], *tokens)
        for group, got in zip(self.groups, values):
            group["terms"] = [(v, t[1], t[2]) for v, t in zip(got, group["terms"])]

    def accept(self, values):
        values = list(values)
        if not values:
            return
        self.sent = values
        got = [
            swap(value.reshape(-1, value.shape[-1]), bit[0], bit[1], self.counts[bit[0]])
            for value, bit in zip(values, self.todo)
        ]
        column = 0
        for n, group in enumerate(self.groups):
            recv = got[n] if len(got) > 1 else got[0]
            bits = tuple(bit for bit in self.bits if bit not in group["fixed"])
            group["terms"].append(
                (self.shaped(recv, bits), bits, 0 if len(got) > 1 else column)
            )
            column += group["columns"]

    def rest(self):
        while self.orders:
            self.accept(self.plain(self.across()))

    def straight(self):
        seq = [bit for bit in self.bits if bit[0] == "seq"]
        jobs = []
        for jump in range(1, self.counts["seq"]):
            flips = {bit: jump // bit[1] % 2 for bit in seq}
            jobs.append(
                [
                    (list(g["terms"]), {**g["fixed"], **flips}, g["columns"])
                    for g in self.groups
                ]
            )
        for group in self.groups:
            group["fixed"].update({bit: 0 for bit in seq})
        if self.rows % 8 == 0:
            return jobs
        self.accept_straight(
            [
                jnp.concatenate(
                    [self.total_at({"terms": t, "columns": c}, flips) for t, flips, c in job],
                    axis=-1,
                ).astype(bf16)
                for job in jobs
            ]
        )
        return []

    def accept_straight(self, values):
        values = list(values)
        if not values:
            return
        self.sent = values
        for jump, value in enumerate(values):
            got = swap(value, "seq", jump + 1, self.counts["seq"])
            column = 0
            for group in self.groups:
                group["terms"].append((self.shaped(got, ()), (), column))
                column += group["columns"]

    def total(self, *tokens):
        groups = None
        if tokens:
            values = [[term[0] for term in group["terms"]] for group in self.groups]
            groups = after(values, *tokens)
        parts = []
        for n, group in enumerate(self.groups):
            terms = group["terms"]
            if groups:
                terms = [(v, t[1], t[2]) for v, t in zip(groups[n], terms)]
            parts.append(
                self.total_at({"terms": terms, "columns": group["columns"]}, group["fixed"])
            )
        return jnp.concatenate(parts, axis=-1)


def body(
    hidden_in,
    segment_ids,
    query_emb,
    positives,
    w_qkv,
    query_bias,
    value_bias,
    w_out,
    out_bias,
    norm1_gain,
    norm1_bias,
    w_up,
    up_bias,
    w_down,
    down_bias,
    norm2_gain,
    norm2_bias,
    w_proj,
):
    micro_count, row_count, local_len, width = hidden_in.shape
    full_len = segment_ids.shape[2]
    embed_width = w_proj.shape[1]
    ff = w_up.shape[1]
    queries_local = query_emb.shape[1]
    query_tokens = query_emb.shape[2]
    seq_count = lax.axis_size("seq")
    dp_count = lax.axis_size("dp")
    seq_pos = lax.axis_index("seq")
    dp_pos = lax.axis_index("dp")
    rows = micro_count * row_count
    tokens = rows * local_len
    far = 64
    window = 3 * local_len + far
    assert local_len + far >= PASSAGE_MOST - 1 and seq_count == 4

    x_own = hidden_in.reshape(rows, local_len, width)
    x_flat = x_own.reshape(tokens, width)
    low_half = seq_pos < 2
    inner = [(1, 2), (2, 1), (0, 0), (3, 3)]
    far_send = jnp.where(low_half, x_own[:, local_len - far :], x_own[:, :far])
    middle_x = lax.ppermute(x_flat, "seq", inner)
    far_x = swap(far_send.reshape(rows * far, width), "seq", 2, seq_count)
    side_x = swap(x_flat, "seq", 1, seq_count)
    pieces = [side_x, middle_x, far_x]

    seg_full = segment_ids.reshape(rows, full_len)
    edges = jnp.sum(
        (seg_full[:, None, :] < jnp.arange(1, SEGS, dtype=jnp.int32)[None, :, None]).astype(
            jnp.int32
        ),
        axis=2,
    )
    meta = jnp.concatenate(
        [
            jnp.stack(
                [
                    seq_pos * local_len,
                    dp_pos,
                    (seq_pos ^ 1) * local_len,
                    jnp.where((seq_pos == 1) | (seq_pos == 2), 3 - seq_pos, -9) * local_len,
                    jnp.where(
                        low_half, (seq_pos + 2) * local_len, (seq_pos - 1) * local_len - far
                    ),
                    dp_pos * row_count * SEGS,
                    dp_pos % 2,
                    seq_pos,
                ]
            ).astype(jnp.int32),
            edges.reshape(-1),
        ]
    )

    queries = query_emb.reshape(micro_count, queries_local * query_tokens, embed_width)
    bits = bits_of(dp_count)
    strides = [bits[:1]] + [bits[k : k + 2] for k in range(1, len(bits), 2)]

    queries = lax.all_gather(queries, "dp", axis=1, tiled=True)
    query_all = queries.shape[1]
    query_count = query_all // query_tokens
    wide = max(128, query_count)
    positives_wide = jnp.pad(
        positives, ((0, 0), (0, wide - query_count)), constant_values=-1
    )

    pairs = width // 128
    chunks = ff // width
    forward = call(
        functools.partial(
            forward_kernel, (rows, local_len, far, window, full_len, width, row_count)
        ),
        [
            ((8 + chunks, width), f32),
            ((tokens, width), bf16),
            ((width, tokens), bf16),
            ((rows, pairs, 2 * local_len), f32),
            ((tokens, 128), f32),
            ((tokens, width), f32),
            ((width, tokens), bf16),
            ((tokens, embed_width), f32),
            ((tokens, embed_width), bf16),
            ((rows * SEGS, query_all), f32),
            ((rows, window, 2 * width), bf16),
            ((rows, width, window), bf16),
            ((tokens, width), f32),
            ((width, tokens), bf16),
            ((chunks, width, tokens), bf16),
            ((chunks, tokens, width), bf16),
        ],
        [
            meta,
            value_bias,
            out_bias,
            norm1_gain,
            norm1_bias,
            down_bias,
            norm2_gain,
            norm2_bias,
            query_bias,
            up_bias,
            w_proj,
            x_flat,
            *pieces,
            queries,
            w_qkv,
            w_out,
            w_up,
            w_down,
        ],
        [
            pltpu.VMEM((window, local_len), f32),
            pltpu.VMEM((tokens, width), bf16),
            pltpu.VMEM((tokens, width), bf16),
            pltpu.VMEM((tokens, width), bf16),
            pltpu.VMEM((tokens, width), bf16),
            pltpu.VMEM((rows * far, width), bf16),
            pltpu.VMEM(queries.shape, bf16),
            pltpu.VMEM((width, 3 * width), bf16),
            pltpu.VMEM((width, width), bf16),
            pltpu.VMEM((chunks, width, width), bf16),
            pltpu.VMEM((chunks, width, width), bf16),
            pltpu.VMEM((rows, window, 2 * width), bf16),
            pltpu.VMEM((rows, width, window), bf16),
            pltpu.VMEM((tokens, width), f32),
            pltpu.VMEM((width, tokens), bf16),
            pltpu.VMEM((chunks, width, tokens), bf16),
            pltpu.VMEM((chunks, tokens, width), bf16),
            pltpu.VMEM((tokens, width), bf16),
            pltpu.VMEM((tokens, width), f32),
            pltpu.SemaphoreType.DMA((11 + 4 * chunks,)),
        ],
        name="forward",
        us=20,
        hbm_ins=9,
        hbm_outs=6,
    )
    vectors, query, context_t, lse, cols, norm2, hidden2_t, proj, embed, parts = forward[:10]
    kv, x_t, norm1, hidden1_t, act_t, slope = forward[10:]

    others = [swap(parts, "seq", bit, seq_count) for bit in (1, 2, 3)]
    stat_rows = 8
    merged, score, stats = call(
        functools.partial(score_kernel, (rows, full_len, row_count, query_tokens)),
        [
            ((rows * SEGS, query_all), f32),
            ((rows * SEGS, wide), f32),
            ((stat_rows, wide), f32),
        ],
        [meta, parts, *others, positives_wide],
        name="score",
        us=2,
    )
    is_whole = lax.broadcasted_iota(jnp.int32, stats.shape, 0) < micro_count
    for group in strides:
        jumps = group if len(group) == 1 else [group[0], group[1], group[0] + group[1]]
        recv = [swap(stats, "dp", jump, dp_count) for jump in jumps]
        if len(recv) == 1:
            best = jnp.maximum(stats, recv[0])
            whole = jnp.exp(stats - best) + jnp.exp(recv[0] - best)
            hits = stats + recv[0]
        else:
            best = jnp.maximum(jnp.maximum(stats, recv[0]), jnp.maximum(recv[1], recv[2]))
            whole = (jnp.exp(stats - best) + jnp.exp(recv[0] - best)) + (
                jnp.exp(recv[1] - best) + jnp.exp(recv[2] - best)
            )
            hits = (stats + recv[0]) + (recv[1] + recv[2])
        stats = jnp.where(is_whole, best + jnp.log(whole), hits)

    devices = dp_count * seq_count

    def places(depth, columns):
        block = depth // dp_count
        if block % 16 == 0:
            return [((dp_count // 2, block, columns), bf16)] * 2
        return [((depth, columns), bf16)]

    where = {"dp": dp_pos, "seq": seq_pos}
    counts = {"dp": dp_count, "seq": seq_count}
    down_places = places(ff, width)
    loss, d_proj, g_resid2, vec_c, *outs = call(
        functools.partial(
            upper_kernel, (rows, local_len, full_len, row_count, query_tokens)
        ),
        [
            ((micro_count, wide), f32),
            ((width, embed_width), bf16),
            ((tokens, width), f32),
            ((8, width), f32),
        ]
        + down_places,
        [
            meta,
            merged,
            score,
            stats,
            positives_wide,
            queries,
            embed,
            proj,
            norm2,
            hidden2_t,
            cols,
            vectors,
            w_proj,
            act_t,
        ],
        [
            pltpu.VMEM((chunks, width, width), bf16),
            pltpu.VMEM((chunks, width, tokens), bf16),
            pltpu.VMEM((rows * SEGS, query_all), f32),
            pltpu.VMEM((tokens, embed_width), f32),
            pltpu.SemaphoreType.DMA((1 + max(dp_count, chunks),)),
        ],
        hbm_ins=1,
        name="upper",
        us=8,
        hbm_outs=len(down_places),
    )
    losses = lax.dynamic_slice_in_dim(loss, dp_pos * queries_local, queries_local, 1)
    down = Chunk(outs, where, counts)
    down.core()

    up_places = places(width, ff + width + embed_width)
    d_ubias, g_resid1, g_context, vec_d, *outs = call(
        lower_kernel,
        [
            ((chunks, 1, width), f32),
            ((tokens, width), f32),
            ((tokens, width), bf16),
            ((8, width), f32),
        ]
        + up_places,
        [
            meta,
            g_resid2,
            hidden1_t,
            norm1,
            cols,
            vectors,
            context_t,
            w_out,
            d_proj,
            w_down,
            w_up,
            slope,
        ],
        [
            pltpu.VMEM((chunks, width, width), bf16),
            pltpu.VMEM((chunks, width, width), bf16),
            pltpu.VMEM((chunks, tokens, width), bf16),
            pltpu.VMEM((tokens, width), f32),
            pltpu.VMEM((tokens, width), bf16),
            pltpu.VMEM((chunks, width, width), bf16),
            pltpu.VMEM((width, width + embed_width), bf16),
            pltpu.SemaphoreType.DMA(((3 + dp_count) * chunks + dp_count,)),
        ],
        name="lower",
        us=13,
        hbm_ins=3,
        hbm_outs=len(up_places),
    )
    up = Chunk(outs, where, counts)
    up.core()

    def fold(chunks_jobs, *tokens, us=FOLD):
        jobs = [job for _, got, _ in chunks_jobs for job in got]
        values = call(nothing, [], [meta], name="fold", deps=tokens, jobs=jobs, us=us) if jobs else []
        at = 0
        sent = []
        for chunk, got, accept in chunks_jobs:
            accept(values[at : at + len(got)])
            at += len(got)
            sent += chunk.sent
        return sent

    sends = fold([(down, down.across(), down.accept)], g_resid1, us=3)
    last_places = places(width, 3 * width + 128)
    sends = fold([(up, up.across(), up.accept)], *sends, us=3)
    g_own, g_side, g_middle, g_far, *outs = call(
        functools.partial(
            attention_kernel, (rows, local_len, far, window, full_len, width, devices)
        ),
        [
            ((tokens, width), f32),
            ((tokens, width), bf16),
            ((tokens, width), bf16),
            ((rows * far, width), bf16),
        ]
        + last_places,
        [meta, g_context, query, lse, vec_c, vec_d, d_ubias, g_resid1, kv, x_t, w_qkv],
        [
            pltpu.VMEM((rows, window, 2 * width), bf16),
            pltpu.VMEM((rows, width, window), bf16),
            pltpu.VMEM((tokens, width), bf16),
            pltpu.VMEM((rows, window, 2 * width), bf16),
            pltpu.VMEM((width, 3 * width), bf16),
            pltpu.VMEM((window, local_len), f32),
            pltpu.VMEM((3, width, width), bf16),
            pltpu.VMEM((width, 128), bf16),
            pltpu.VMEM((width, 128), f32),
            pltpu.SemaphoreType.DMA((rows + 2 + 4 * dp_count,)),
        ],
        name="attention",
        us=20,
        hbm_ins=3,
        hbm_outs=len(last_places),
        deps=sends,
    )
    last = Chunk(outs, where, counts)
    received = [term[0] for group in up.groups for term in group["terms"]]
    halo = {}
    token = [g_own]
    for step in ORDER:
        if step in ("m", "s", "f"):
            token = token + [halo[step.upper()]]
        elif step == "M":
            halo[step] = lax.ppermute(after(g_middle, token), "seq", inner)
        elif step == "S":
            halo[step] = swap(after(g_side, token), "seq", 1, seq_count)
        elif step == "F":
            halo[step] = swap(after(g_far, token), "seq", 2, seq_count)
        elif step == "C0":
            last.other = after(last.other, token, received)
            last.core()
        elif step == "c0":
            token = token + [last.recv]
        elif step == "C1":
            token = fold([(last, last.across(), last.accept)], *token)
        elif step == "C3":
            last.rest()
            token = fold([(last, last.straight(), last.accept_straight)], *token)
        else:
            chunk = {"A": down, "B": up, "C": last}[step[0]]
            chunk.wait(*token)
            if step[1] == "2":
                jobs = chunk.across()
            else:
                chunk.rest()
                jobs = chunk.along(1 if step[1] == "3" else 2)
            chunk.accept(chunk.plain(jobs))
            token = list(chunk.sent)
    g_own, from_side, from_middle, from_far = after(
        (g_own, halo["S"], halo["M"], halo["F"]), *token
    )
    from_far = from_far.reshape(rows, far, width).astype(f32)
    pad = ((0, 0), (local_len - far, 0), (0, 0))
    flip = ((0, 0), (0, local_len - far), (0, 0))
    grad_in = (g_own + from_side.astype(f32) + from_middle.astype(f32)).reshape(
        rows, local_len, width
    ) + jnp.where(low_half, jnp.pad(from_far, pad), jnp.pad(from_far, flip))

    down_part = down.total(grad_in)
    up_part = up.total(down_part)
    last_part = last.total(up_part)
    some = 4 * width // devices
    vec_at = 3 * width
    vec_part = last_part[:3, vec_at : vec_at + some]
    return (
        embed.reshape(micro_count, row_count, local_len, embed_width),
        losses,
        grad_in.reshape(micro_count, row_count, local_len, width),
        last_part[:, : 3 * width].reshape(-1),
        up_part[:, ff : ff + width].reshape(-1),
        up_part[:, :ff].reshape(-1),
        down_part.reshape(-1),
        up_part[:, ff + width :].reshape(-1),
        vec_part[0],
        vec_part[1:].reshape(-1),
    )


def solution(mesh):
    in_specs = (
        P(None, "dp", "seq", None),
        P(None, "dp", None),
        P(None, "dp", None, None),
    ) + (P(),) * 15
    out_specs = (
        P(None, "dp", "seq", None),
        P(None, "dp"),
        P(None, "dp", "seq", None),
    ) + (P(("dp", "seq")),) * 7
    return jax.shard_map(body, mesh=mesh, in_specs=in_specs, out_specs=out_specs, check_vma=False)
```

```python
import functools

import jax
import jax.numpy as jnp
from jax import lax
from jax.experimental import pallas as pl
from jax.experimental.pallas import tpu as pltpu
from jax.sharding import PartitionSpec as P

HEADS = 12
SEGS = 4
PASSAGE_MOST = 180

SHARP = 20.0
EDGES = 8
COST = 4e9
FOLD = 0.3
ORDER = (
    "M", "A2", "C0", "B2", "m", "S", "C1", "A3", "s", "F", "B3", "A4", "C2", "B4", "C3", "f",
)
LN_EPS = 1e-12
NORM_EPS = 1e-12
MASKED = -1e30
HIGH = lax.Precision.HIGHEST
bf16 = jnp.bfloat16
f32 = jnp.float32
VMEM = pl.BlockSpec(memory_space=pltpu.VMEM)
HBM = pl.BlockSpec(memory_space=pltpu.HBM)
SMEM = pl.BlockSpec(memory_space=pltpu.SMEM)
PARAMS = pltpu.CompilerParams(vmem_limit_bytes=58 << 20)


def bits_of(count):
    return [1 << k for k in range(count.bit_length() - 1)]


def swap(value, axis, bit, count):
    return lax.ppermute(value, axis, [(i, i ^ bit) for i in range(count)])


def dot(left, right, left_dim, right_dim, precision=None):
    return lax.dot_general(
        left,
        right,
        (((left_dim,), (right_dim,)), ((), ())),
        precision=precision,
        preferred_element_type=f32,
    )


def ident(pos, meta, row, length):
    seg = jnp.zeros(pos.shape, jnp.int32)
    for s in range(SEGS - 1):
        seg = seg + (pos >= meta[EDGES + row * (SEGS - 1) + s]).astype(jnp.int32)
    return jnp.where((pos >= 0) & (pos < length), seg, -1)


def key_positions(meta, local, shape):
    w = lax.broadcasted_iota(jnp.int32, shape, 0)
    pos = meta[0] + w
    for piece in range(1, 4):
        pos = jnp.where(w >= piece * local, meta[1 + piece] + w - piece * local, pos)
    return pos


def pair_rows(block, even):
    zero = jnp.zeros_like(block)
    return jnp.concatenate([jnp.where(even, block, zero), jnp.where(even, zero, block)], axis=0)


def attention_bias(meta, row, local, window, length):
    key_seg = ident(key_positions(meta, local, (window, local)), meta, row, length)
    query_seg = ident(
        meta[0] + lax.broadcasted_iota(jnp.int32, (window, local), 1), meta, row, length
    )
    return jnp.where(key_seg == query_seg, 0.0, MASKED).astype(f32)


def copies_out(scr, outs, sems, first, core, columns, part=0, parts=1):
    size = scr.shape[0]
    if len(outs) == 1:
        pieces = [(scr, outs[0].at[pl.ds(part * size, size), columns])]
    else:
        high, block, _ = outs[0].shape
        pieces = []
        for k in range(high // parts):
            for out, which in ((outs[0], 1 - core), (outs[1], core)):
                rows = pl.ds(pl.multiple_of((2 * k + which) * block, 16), block)
                pieces.append((scr.at[rows, :], out.at[part * (high // parts) + k, :, columns]))
    return [
        pltpu.make_async_copy(source, target, sems.at[first + n])
        for n, (source, target) in enumerate(pieces)
    ]


def begin(copies):
    for copy in copies:
        copy.start()


def finish(copies):
    for copy in copies:
        copy.wait()


def own_kernel(dims, meta, query_bias, value_bias, x_own, w_qkv, query, kv, x_t):
    rows, local, width = dims
    x = x_own[...]
    got = dot(x, w_qkv[...], 1, 0)
    query[...] = (got[:, :width] + query_bias[...].reshape(1, width)).astype(bf16)
    keys = got[:, width : 2 * width].astype(bf16)
    values = (got[:, 2 * width :] + value_bias[...].reshape(1, width)).astype(bf16)
    for r in range(rows):
        mine = slice(r * local, (r + 1) * local)
        kv[r, :, :width] = keys[mine]
        kv[r, :, width:] = values[mine]
        x_t[r] = x[mine].T


def forward_kernel(
    dims,
    meta,
    value_bias_in,
    out_bias_in,
    gain1_in,
    shift1_in,
    down_bias_in,
    gain2_in,
    shift2_in,
    up_bias_in,
    w_proj,
    query,
    x_own_hbm,
    side_hbm,
    middle_hbm,
    far_hbm,
    kv_own_hbm,
    x_t_own_hbm,
    queries_hbm,
    w_qkv_hbm,
    w_out_hbm,
    w_up_hbm,
    w_down_hbm,
    vectors,
    context_t,
    lse,
    cols,
    norm2,
    hidden2_t,
    proj,
    embed,
    parts,
    kv_hbm,
    x_t_hbm,
    norm1_hbm,
    hidden1_t_hbm,
    act_t_hbm,
    slope_hbm,
    bias_scr,
    context,
    x_own,
    side,
    middle,
    far_part,
    queries,
    w_qkv,
    w_out,
    w_up,
    w_down,
    kv,
    x_t,
    norm1,
    hidden1_t,
    act_t,
    slope,
    hidden_scr,
    ffn_scr,
    sems,
):
    rows, local, far, window, length, width, row_count = dims
    chunks = w_up.shape[0]
    cut_kv = pl.ds(width, 2 * width)
    kv_here = pltpu.make_async_copy(
        w_qkv_hbm.at[:, cut_kv], w_qkv.at[:, cut_kv], sems.at[0]
    )
    out_here = pltpu.make_async_copy(w_out_hbm, w_out, sems.at[1])

    def up_here(c):
        cut = pl.ds(pl.multiple_of(c * width, 128), width)
        return pltpu.make_async_copy(w_up_hbm.at[:, cut], w_up.at[c], sems.at[2 + c])

    def down_here(c):
        cut = pl.ds(pl.multiple_of(c * width, 128), width)
        return pltpu.make_async_copy(
            w_down_hbm.at[cut, :], w_down.at[c], sems.at[2 + chunks + c]
        )

    base = 2 + 2 * chunks
    pieces_here = [
        pltpu.make_async_copy(source, target, sems.at[base + 4 + 2 * chunks + n])
        for n, (source, target) in enumerate(
            ((x_own_hbm, x_own), (side_hbm, side), (middle_hbm, middle), (far_hbm, far_part))
        )
    ]
    queries_here = pltpu.make_async_copy(
        queries_hbm, queries, sems.at[base + 8 + 2 * chunks]
    )
    own = pl.ds(0, local)
    own_here = [
        pltpu.make_async_copy(
            kv_own_hbm, kv.at[:, own, :], sems.at[base + 9 + 2 * chunks]
        ),
        pltpu.make_async_copy(
            x_t_own_hbm, x_t.at[:, :, own], sems.at[base + 10 + 2 * chunks]
        ),
    ]
    begin([kv_here] + pieces_here[1:] + own_here + [pieces_here[0], out_here])
    for c in range(chunks):
        begin([up_here(c), down_here(c)])
    queries_here.start()
    for n, vector in enumerate(
        (
            value_bias_in,
            out_bias_in,
            gain1_in,
            shift1_in,
            down_bias_in,
            gain2_in,
            shift2_in,
        )
    ):
        vectors[n : n + 1, :] = vector[...].reshape(1, width)
    for c in range(chunks):
        vectors[7 + c : 8 + c, :] = up_bias_in[pl.ds(c * width, width)].reshape(1, width)
    value_bias = vectors[0:1, :]
    kv_out = pltpu.make_async_copy(kv, kv_hbm, sems.at[base])
    x_out = pltpu.make_async_copy(x_t, x_t_hbm, sems.at[base + 1])
    norm_out = pltpu.make_async_copy(norm1, norm1_hbm, sems.at[base + 2])
    hidden_out = pltpu.make_async_copy(hidden1_t, hidden1_t_hbm, sems.at[base + 3])

    def act_out(c):
        return pltpu.make_async_copy(act_t.at[c], act_t_hbm.at[c], sems.at[base + 4 + c])

    def slope_out(c):
        return pltpu.make_async_copy(
            slope.at[c], slope_hbm.at[c], sems.at[base + 4 + chunks + c]
        )

    kv_here.wait()
    offset = local
    for n, (piece, size) in enumerate(((side, local), (middle, local), (far_part, far))):
        pieces_here[n + 1].wait()
        got = dot(piece[...], w_qkv[:, width:], 1, 0)
        got_k = got[:, :width].astype(bf16)
        got_v = (got[:, width:] + value_bias).astype(bf16)
        for r in range(rows):
            mine = slice(r * size, (r + 1) * size)
            kv[r, offset : offset + size, :width] = got_k[mine]
            kv[r, offset : offset + size, width:] = got_v[mine]
            x_t[r, :, offset : offset + size] = piece[mine, :].T
        offset += size
    finish(own_here + pieces_here[:1])
    begin([kv_out, x_out])
    even = lax.broadcasted_iota(jnp.int32, (local, 128), 1) < 64
    upper = lax.broadcasted_iota(jnp.int32, (128, local), 0) < 64
    pairs = width // 128

    def attend(r, carry):
        bias_scr[...] = attention_bias(meta, r, local, window, length)
        own = pl.ds(pl.multiple_of(r * local, 128), local)
        for p in range(pairs):
            lanes = slice(p * 128, (p + 1) * 128)
            q2 = pair_rows(query[own, lanes] * bf16(0.125), even)
            k2 = kv[r, :, lanes]
            v2 = kv[r, :, width + p * 128 : width + (p + 1) * 128]
            bias = bias_scr[...]
            s = dot(k2, q2, 1, 1) + jnp.concatenate([bias, bias], axis=1)
            top = jnp.max(s, axis=0, keepdims=True)
            e = jnp.exp(s - top)
            total = jnp.sum(e, axis=0, keepdims=True)
            lse[r, p : p + 1, :] = top + jnp.log(total)
            o = dot(v2, e.astype(bf16), 0, 0) * (1.0 / total)
            o = jnp.where(upper, o[:, :local], o[:, local:])
            context_t[lanes, own] = o.astype(bf16)
            context[own, lanes] = o.T.astype(bf16)
        return carry

    lax.fori_loop(0, rows, attend, 0)
    out_here.wait()
    attended = dot(context[...], w_out[...], 1, 0) + vectors[1:2, :]
    resid = x_own[...].astype(f32) + attended
    centred = resid - jnp.mean(resid, axis=-1, keepdims=True)
    rstd1 = lax.rsqrt(jnp.mean(centred * centred, axis=-1, keepdims=True) + LN_EPS)
    n1 = centred * rstd1
    norm1[...] = n1
    hidden1 = n1 * vectors[2:3, :] + vectors[3:4, :]
    hidden1_low = hidden1.astype(bf16)
    hidden1_t[...] = hidden1_low.T
    begin([norm_out, hidden_out])
    hidden_scr[...] = hidden1_low
    ffn_scr[...] = hidden1 + vectors[4:5, :]

    def feed(c, carry):
        up_here(c).wait()
        up = dot(hidden_scr[...], w_up[c], 1, 0) + vectors[pl.ds(7 + c, 1), :]
        cdf = 0.5 * (1.0 + lax.erf(up * (0.5**0.5)))
        act_low = (up * cdf).astype(bf16)
        act_t[c] = act_low.T
        slope[c] = (cdf + up * (jnp.exp(-0.5 * up * up) * 0.3989422804014327)).astype(bf16)
        begin([act_out(c), slope_out(c)])
        down_here(c).wait()
        ffn_scr[...] += dot(act_low, w_down[c], 1, 0)
        return carry

    lax.fori_loop(0, chunks, feed, 0)
    resid = ffn_scr[...]
    centred = resid - jnp.mean(resid, axis=-1, keepdims=True)
    rstd2 = lax.rsqrt(jnp.mean(centred * centred, axis=-1, keepdims=True) + LN_EPS)
    n2 = centred * rstd2
    norm2[...] = n2
    lane = lax.broadcasted_iota(jnp.int32, cols.shape, 1)
    cols[...] = jnp.where(lane == 0, rstd1, rstd2)
    hidden2_low = (n2 * vectors[5:6, :] + vectors[6:7, :]).astype(bf16)
    hidden2_t[...] = hidden2_low.T
    out = dot(hidden2_low, w_proj[...], 1, 0)
    proj[...] = out
    inv = lax.rsqrt(jnp.sum(out * out, axis=-1, keepdims=True) + NORM_EPS)
    embed[...] = (out * inv).astype(bf16)

    def match(r, carry):
        own = pl.ds(pl.multiple_of(r * local, 128), local)
        sharp = dot(embed[own, :], queries[r // row_count], 1, 1) * SHARP
        seg = ident(meta[0] + lax.broadcasted_iota(jnp.int32, (local, 1), 0), meta, r, length)
        tops = []
        shift = jnp.zeros_like(sharp)
        for s in range(SEGS):
            inside = seg == s
            top = jnp.max(jnp.where(inside, sharp, MASKED), axis=0, keepdims=True)
            tops.append(top)
            shift = jnp.where(inside, top, shift)
        e = jnp.exp(sharp - shift)
        for s in range(SEGS):
            total = jnp.sum(jnp.where(seg == s, e, 0.0), axis=0, keepdims=True)
            some = total > 0.0
            parts[pl.ds(r * SEGS + s, 1), :] = jnp.where(
                some, tops[s] + jnp.log(jnp.where(some, total, 1.0)), MASKED
            )
        return carry

    queries_here.wait()
    lax.fori_loop(0, rows, match, 0)
    finish([kv_out, x_out, norm_out, hidden_out])
    for c in range(chunks):
        finish([act_out(c), slope_out(c)])


def score_kernel(dims, meta, first, second, third, fourth, positives, merged, score, stats):
    rows, length, row_count, query_tokens = dims
    half = rows * SEGS
    parts = [ref[...] for ref in (first, second, third, fourth)]
    top = jnp.maximum(jnp.maximum(parts[0], parts[1]), jnp.maximum(parts[2], parts[3]))
    sums = [jnp.exp(part - top) for part in parts]
    whole = top + jnp.log((sums[0] + sums[1]) + (sums[2] + sums[3]))
    merged[...] = whole
    sub = lax.broadcasted_iota(jnp.int32, (half, 1), 0)
    count = jnp.zeros((half, 1), f32)
    for r in range(rows):
        edges = [0] + [meta[EDGES + r * (SEGS - 1) + s] for s in range(SEGS - 1)] + [length]
        for s in range(SEGS):
            size = (edges[s + 1] - edges[s]).astype(f32)
            count = jnp.where(sub == r * SEGS + s, size, count)
    match = whole - jnp.log(count)
    wide = score.shape[1]
    shape = (match.shape[1], wide)
    group = (
        lax.broadcasted_iota(jnp.int32, shape, 0) // query_tokens
        == lax.broadcasted_iota(jnp.int32, shape, 1)
    ).astype(f32)
    got = dot(match, group, 1, 0, HIGH)
    score[...] = got
    per = row_count * SEGS
    micros = rows // row_count
    stats[...] = jnp.zeros(stats.shape, f32)
    for m in range(micros):
        part = got[m * per : (m + 1) * per]
        at = lax.broadcasted_iota(jnp.int32, (per, wide), 0) + meta[5]
        chosen = at == positives[m : m + 1, :]
        best = jnp.max(part, axis=0, keepdims=True)
        stats[m : m + 1, :] = best + jnp.log(
            jnp.sum(jnp.exp(part - best), axis=0, keepdims=True)
        )
        stats[micros + m : micros + m + 1, :] = jnp.sum(
            jnp.where(chosen, part, 0.0), axis=0, keepdims=True
        )


def upper_kernel(
    dims,
    meta,
    merged,
    score,
    stats,
    positives,
    queries,
    embed,
    proj,
    norm2,
    hidden2_t,
    cols,
    vectors,
    w_proj,
    act_t_hbm,
    loss,
    d_proj,
    g_resid2,
    vec,
    *rest,
):
    outs, (scr, act_t, factor_scr, unit_scr, sems) = rest[:-5], rest[-5:]
    rows, local, length, row_count, query_tokens = dims
    chunks = act_t.shape[0]
    gain2 = vectors[5:6, :]
    act_here = pltpu.make_async_copy(act_t_hbm, act_t, sems.at[0])
    act_here.start()
    micros = rows // row_count
    per = row_count * SEGS
    wide = score.shape[1]
    all_queries = merged.shape[1]
    shape = (wide, all_queries)
    group = (
        lax.broadcasted_iota(jnp.int32, shape, 1) // query_tokens
        == lax.broadcasted_iota(jnp.int32, shape, 0)
    ).astype(f32)
    pieces = []
    for m in range(micros):
        whole = stats[m : m + 1, :]
        loss[m : m + 1, :] = whole - stats[micros + m : micros + m + 1, :]
        part = score[m * per : (m + 1) * per, :]
        at = lax.broadcasted_iota(jnp.int32, (per, wide), 0) + meta[5]
        chosen = (at == positives[m : m + 1, :]).astype(f32)
        pieces.append(jnp.exp(part - whole) - chosen)
    factor_scr[...] = SHARP * dot(jnp.concatenate(pieces, axis=0), group, 1, 0, HIGH)

    def pull(r, carry):
        own = pl.ds(pl.multiple_of(r * local, 128), local)
        m = r // row_count
        sharp = dot(embed[own, :], queries[m], 1, 1) * SHARP
        seg = ident(meta[0] + lax.broadcasted_iota(jnp.int32, (local, 1), 0), meta, r, length)
        shift = jnp.zeros_like(sharp)
        scale = jnp.zeros_like(sharp)
        for s in range(SEGS):
            at = pl.ds(r * SEGS + s, 1)
            shift = jnp.where(seg == s, merged[at, :], shift)
            scale = jnp.where(seg == s, factor_scr[at, :], scale)
        g_sim = (scale * jnp.exp(sharp - shift)).astype(bf16)
        unit_scr[own, :] = dot(g_sim, queries[m], 1, 0)
        return carry

    lax.fori_loop(0, rows, pull, 0)
    g_unit = unit_scr[...]
    out = proj[...]
    inv = lax.rsqrt(jnp.sum(out * out, axis=-1, keepdims=True) + NORM_EPS)
    unit = out * inv
    g_proj = ((g_unit - unit * jnp.sum(unit * g_unit, axis=-1, keepdims=True)) * inv).astype(bf16)
    n2 = norm2[...]
    d_proj[...] = dot(hidden2_t[...], g_proj, 1, 0).astype(bf16)
    g_hidden = dot(g_proj, w_proj[...], 1, 1)
    vec[0:1, :] = jnp.sum(g_hidden * n2, axis=0, keepdims=True)
    vec[1:2, :] = jnp.sum(g_hidden, axis=0, keepdims=True)
    g_n = g_hidden * gain2
    g_v = cols[:, 1:2] * (
        g_n
        - jnp.mean(g_n, axis=-1, keepdims=True)
        - n2 * jnp.mean(g_n * n2, axis=-1, keepdims=True)
    )
    g_resid2[...] = g_v
    low = g_v.astype(bf16)
    vec[2:3, :] = jnp.sum(low.astype(f32), axis=0, keepdims=True)
    act_here.wait()
    columns = slice(0, scr.shape[2])
    each = 2 * (outs[0].shape[0] // chunks) if len(outs) == 2 else 1

    def leaving(c):
        return copies_out(scr.at[c], outs, sems, 1 + c * each, meta[6], columns, c, chunks)

    for c in range(chunks):
        scr[c] = dot(act_t[c], low, 1, 0).astype(bf16)
        begin(leaving(c))
    for c in range(chunks):
        finish(leaving(c))


def lower_kernel(
    meta,
    g_resid2,
    hidden1_t,
    norm1,
    cols,
    vectors,
    context_t,
    w_out,
    d_proj,
    w_down_hbm,
    w_up_hbm,
    slope_hbm,
    d_ubias,
    g_resid1,
    g_context,
    vec,
    *rest,
):
    outs, (w_down, w_up, slope, hidden_scr, low_scr, scr, out_scr, sems) = rest[:-8], rest[-8:]
    chunks, width, _ = w_up.shape
    gain1 = vectors[2:3, :]
    each = 2 * outs[0].shape[0] if len(outs) == 2 else 1

    def here(c):
        cut = pl.ds(pl.multiple_of(c * width, 128), width)
        return [
            pltpu.make_async_copy(w_down_hbm.at[cut, :], w_down.at[c], sems.at[3 * c]),
            pltpu.make_async_copy(slope_hbm.at[c], slope.at[c], sems.at[3 * c + 1]),
            pltpu.make_async_copy(w_up_hbm.at[:, cut], w_up.at[c], sems.at[3 * c + 2]),
        ]

    def leaving(c):
        cut = pl.ds(pl.multiple_of(c * width, 128), width)
        return copies_out(scr.at[c], outs, sems, 3 * chunks + c * each, meta[6], cut)

    for c in range(chunks):
        begin(here(c))
    hidden_scr[...] = g_resid2[...]
    low_scr[...] = g_resid2[...].astype(bf16)

    def gate(c, carry):
        finish(here(c))
        g_act = dot(low_scr[...], w_down[c], 1, 1)
        g_up = (g_act * slope[c].astype(f32)).astype(bf16)
        d_ubias[c] = jnp.sum(g_up.astype(f32), axis=0, keepdims=True)
        scr[c] = dot(hidden1_t[...], g_up, 1, 0).astype(bf16)
        begin(leaving(c))
        hidden_scr[...] += dot(g_up, w_up[c], 1, 1)
        return carry

    lax.fori_loop(0, chunks, gate, 0)
    n1 = norm1[...]
    g_hidden = hidden_scr[...]
    vec[0:1, :] = jnp.sum(g_hidden * n1, axis=0, keepdims=True)
    vec[1:2, :] = jnp.sum(g_hidden, axis=0, keepdims=True)
    g_n = g_hidden * gain1
    g_v = cols[:, 0:1] * (
        g_n
        - jnp.mean(g_n, axis=-1, keepdims=True)
        - n1 * jnp.mean(g_n * n1, axis=-1, keepdims=True)
    )
    g_resid1[...] = g_v
    low = g_v.astype(bf16)
    vec[2:3, :] = jnp.sum(low.astype(f32), axis=0, keepdims=True)
    out_scr[:, :width] = dot(context_t[...], low, 1, 0).astype(bf16)
    out_scr[:, width:] = d_proj[...]
    columns = slice(chunks * width, chunks * width + out_scr.shape[1])
    last = copies_out(out_scr, outs, sems, (3 + each) * chunks, meta[6], columns)
    begin(last)
    g_context[...] = dot(low, w_out[...], 1, 1).astype(bf16)
    for c in range(chunks):
        finish(leaving(c))
    finish(last)


def attention_kernel(
    dims,
    meta,
    g_context,
    query,
    lse,
    vec_c,
    vec_d,
    d_ubias,
    g_resid1,
    kv_hbm,
    x_t_hbm,
    w_qkv_hbm,
    g_own,
    g_side,
    g_middle,
    g_far,
    *rest,
):
    outs, scratch = rest[:-10], rest[-10:]
    kv, x_t, g_query, g_kv, w_qkv, bias_scr, scr, low_scr, vec_scr, sems = scratch
    rows, local, far, window, length, width, devices = dims
    pairs = width // 128
    even = lax.broadcasted_iota(jnp.int32, (local, 128), 1) < 64
    upper = lax.broadcasted_iota(jnp.int32, (128, local), 0) < 64

    def kv_here(r):
        return pltpu.make_async_copy(kv_hbm.at[r], kv.at[r], sems.at[r])

    for r in range(rows):
        kv_here(r).start()
    x_here = pltpu.make_async_copy(x_t_hbm, x_t, sems.at[rows])
    w_here = pltpu.make_async_copy(w_qkv_hbm, w_qkv, sems.at[rows + 1])
    begin([x_here, w_here])

    def attend(r, carry):
        kv_here(r).wait()
        bias_scr[...] = attention_bias(meta, r, local, window, length)
        own = pl.ds(pl.multiple_of(r * local, 128), local)
        for p in range(pairs):
            lanes = slice(p * 128, (p + 1) * 128)
            vlanes = slice(width + p * 128, width + (p + 1) * 128)
            q2 = pair_rows(query[own, lanes] * bf16(0.125), even)
            k2 = kv[r, :, lanes]
            v2 = kv[r, :, vlanes]
            gc2 = pair_rows(g_context[own, lanes], even)
            bias = bias_scr[...]
            s = dot(k2, q2, 1, 1) + jnp.concatenate([bias, bias], axis=1)
            prob = jnp.exp(s - lse[r, p : p + 1, :])
            g_prob = dot(v2, gc2, 1, 1)
            weighted = prob * g_prob
            inner = jnp.sum(weighted, axis=0, keepdims=True)
            g_score = (weighted - prob * inner).astype(bf16)
            g_kv[r, :, vlanes] = dot(prob.astype(bf16), gc2, 1, 0).astype(bf16)
            g_kv[r, :, lanes] = dot(g_score, q2, 1, 0).astype(bf16)
            g_q = dot(k2, g_score, 0, 0)
            g_q = jnp.where(upper, g_q[:, :local], g_q[:, local:]) * 0.125
            g_query[own, lanes] = g_q.T.astype(bf16)
        return carry

    lax.fori_loop(0, rows, attend, 0)
    x_here.wait()
    each = 2 * outs[0].shape[0] if len(outs) == 2 else 1
    copies = []
    for c in range(3):
        total = None
        for r in range(rows):
            if c == 0:
                part = dot(x_t[r, :, :local], g_query[r * local : (r + 1) * local, :], 1, 0)
            else:
                part = dot(x_t[r], g_kv[r, :, (c - 1) * width : c * width], 1, 0)
            total = part if total is None else total + part
        scr[c] = total.astype(bf16)
        columns = slice(c * width, (c + 1) * width)
        got = copies_out(scr.at[c], outs, sems, rows + 2 + c * each, meta[6], columns)
        begin(got)
        copies += got
    d_qbias = jnp.sum(g_query[...].astype(f32), axis=0, keepdims=True)
    d_vbias = None
    for r in range(rows):
        part = jnp.sum(g_kv[r, :, width:].astype(f32), axis=0, keepdims=True)
        d_vbias = part if d_vbias is None else d_vbias + part
    lower = [d_qbias, d_vbias, vec_d[2:3, :], vec_d[0:1, :]]
    higher = [vec_d[1:2, :], vec_c[2:3, :], vec_c[0:1, :], vec_c[1:2, :]]
    higher += [d_ubias[c] for c in range(d_ubias.shape[0])]
    block = width // devices
    some = 4 * width // devices
    vec_scr[...] = jnp.zeros(vec_scr.shape, f32)
    for device in range(devices):
        for row, vectors, start in (
            (0, lower, device * some),
            (1, higher, 2 * device * some),
            (2, higher, (2 * device + 1) * some),
        ):
            source = vectors[start // width]
            at = start % width
            vec_scr[device * block + row : device * block + row + 1, :some] = source[
                :, at : at + some
            ]
    low_scr[...] = vec_scr[...].astype(bf16)
    columns = slice(3 * width, 3 * width + 128)
    got = copies_out(low_scr, outs, sems, rows + 2 + 3 * each, meta[6], columns)
    begin(got)
    w_here.wait()

    def back(r, carry):
        own = pl.ds(pl.multiple_of(r * local, 128), local)
        part = dot(g_kv[r], w_qkv[:, width:], 1, 1)
        g_own[own, :] = (
            g_resid1[own, :] + dot(g_query[own, :], w_qkv[:, :width], 1, 1) + part[:local]
        )
        g_side[own, :] = part[local : 2 * local].astype(bf16)
        g_middle[own, :] = part[2 * local : 3 * local].astype(bf16)
        g_far[pl.ds(pl.multiple_of(r * far, 64), far), :] = part[3 * local :].astype(bf16)
        return carry

    lax.fori_loop(0, rows, back, 0)
    finish(copies + got)


def nothing(meta):
    del meta


def job_index(meta, bits, fixed):
    index = []
    for bit in bits:
        if bit in fixed:
            axis, stride = bit
            at = (meta[1] if axis == "dp" else meta[7]) // stride % 2
            index.append(1 - at if fixed[bit] else at)
        else:
            index.append(slice(None))
    return tuple(index)


def call(
    kernel,
    outs,
    ins,
    scratch=(),
    name=None,
    hbm_outs=0,
    hbm_ins=0,
    deps=(),
    jobs=(),
    us=3,
):
    deps = tuple(deps)
    count = len(ins)
    job_ins, job_outs, job_scratch, job_scratch_out = [], [], [], []
    for job in jobs:
        columns = 0
        for terms, fixed, size in job:
            for value, bits, column in terms:
                free = len([bit for bit in bits if bit not in fixed])
                shape = (2,) * free + (value.shape[-2], size)
                job_ins.append(value)
                job_scratch.append(pltpu.VMEM(shape, bf16))
            columns += size
        job_outs.append((shape[:-1] + (columns,), bf16))
        job_scratch_out.append(pltpu.VMEM(shape[:-1] + (columns,), bf16))
    extra = [pltpu.SemaphoreType.DMA((len(job_ins) + len(jobs),))] if jobs else []
    out_count, scratch_count = len(outs), len(scratch)

    def run(*refs):
        refs = list(refs)

        def pop(number):
            got, refs[:] = refs[:number], refs[number:]
            return got

        mine = pop(count)
        sources = pop(len(job_ins))
        pop(len(deps))
        mine += pop(out_count)
        targets = pop(len(job_outs))
        mine += pop(scratch_count)
        buffers = pop(len(job_ins))
        results = pop(len(job_outs))
        copies = []
        n = 0
        for job in jobs:
            for terms, fixed, size in job:
                for value, bits, column in terms:
                    index = job_index(mine[0], bits, fixed) + (slice(None), pl.ds(column, size))
                    copies.append(
                        pltpu.make_async_copy(sources[n].at[index], buffers[n], refs[0].at[n])
                    )
                    n += 1
        begin(copies)
        kernel(*mine)
        n = 0
        leaving = []
        for job, target, final in zip(jobs, results, targets):
            column = 0
            for terms, fixed, size in job:
                finish(copies[n : n + len(terms)])
                lead = target.shape[:-2]
                for flat in range(2 ** len(lead)):
                    at = tuple((flat >> k) % 2 for k in range(len(lead)))
                    total = None
                    for buffer in buffers[n : n + len(terms)]:
                        part = buffer[at].astype(f32)
                        total = part if total is None else total + part
                    target[at + (slice(None), slice(column, column + size))] = total.astype(bf16)
                n += len(terms)
                column += size
            leaving.append(
                pltpu.make_async_copy(target, final, refs[0].at[len(job_ins) + len(leaving)])
            )
            leaving[-1].start()
        finish(leaving)

    return pl.pallas_call(
        run,
        out_shape=tuple(jax.ShapeDtypeStruct(s, k) for s, k in list(outs) + job_outs),
        in_specs=[SMEM]
        + [VMEM] * (count - 1 - hbm_ins)
        + [HBM] * (hbm_ins + len(job_ins) + len(deps)),
        out_specs=tuple(
            [VMEM] * (out_count - hbm_outs) + [HBM] * (hbm_outs + len(job_outs))
        ),
        scratch_shapes=list(scratch) + job_scratch + job_scratch_out + extra,
        cost_estimate=pl.CostEstimate(flops=int(us * COST), transcendentals=0, bytes_accessed=1),
        compiler_params=PARAMS,
        name=name,
    )(*ins, *job_ins, *deps)


def after(values, *tokens):
    return lax.optimization_barrier((values, tokens))[0]


class Chunk:
    def __init__(self, outs, where, counts):
        self.where, self.counts = where, counts
        if len(outs) == 2:
            self.other, self.mine = outs
        else:
            full = outs[0]
            dp_count = counts["dp"]
            parts = full.reshape(dp_count // 2, 2, full.shape[0] // dp_count, full.shape[1])
            core = where["dp"] % 2
            self.other = lax.dynamic_index_in_dim(parts, 1 - core, 1, keepdims=False)
            self.mine = lax.dynamic_index_in_dim(parts, core, 1, keepdims=False)
        self.bits = [("dp", bit) for bit in bits_of(counts["dp"])[:0:-1]]
        self.bits += [("seq", bit) for bit in bits_of(counts["seq"])[::-1]]
        self.rows = self.mine.shape[1] // counts["seq"]

    def core(self):
        recv = self.recv = swap(self.other, "dp", 1, self.counts["dp"])
        columns = recv.shape[-1]
        half = columns // 256 * 128
        both = [self.shaped(value, self.bits) for value in (self.mine, recv)]
        self.groups = [
            {"terms": [(v, tuple(self.bits), at) for v in both], "fixed": {}, "columns": size}
            for at, size in ((0, half), (half, columns - half))
        ]
        order = [bit for bit in self.bits if bit[0] == "dp"]
        self.orders = list(zip(order[::-1], order))

    def shaped(self, value, bits):
        return value.reshape((2,) * len(bits) + (self.rows, value.shape[-1]))

    def total_at(self, group, flips):
        total = None
        for value, bits, column in group["terms"]:
            start, size = [], []
            for bit in bits:
                at = (self.where[bit[0]] // bit[1]) % 2
                start.append((1 - at if flips[bit] else at) if bit in flips else 0)
                size.append(1 if bit in flips else 2)
            part = lax.dynamic_slice(
                value, start + [0, column], size + [self.rows, group["columns"]]
            )
            free = [n for n in size if n > 1]
            part = part.reshape(free + [self.rows, group["columns"]]).astype(f32)
            total = part if total is None else total + part
        return total

    def jobs(self, bits, joint):
        parts = []
        for group, bit in zip(self.groups, bits):
            parts.append((list(group["terms"]), {**group["fixed"], bit: 1}, group["columns"]))
            group["fixed"][bit] = 0
        self.todo = list(bits[:1]) if joint else list(bits)
        jobs = [parts] if joint else [[part] for part in parts]
        if self.rows % 8 == 0:
            return jobs
        self.accept(
            [
                jnp.concatenate(
                    [
                        self.total_at({"terms": t, "columns": c}, flips)
                        for t, flips, c in job
                    ],
                    axis=-1,
                ).astype(bf16)
                for job in jobs
            ]
        )
        return []

    def across(self):
        return self.jobs(self.orders.pop(0), False)

    def along(self, index):
        return self.jobs([("seq", index)] * len(self.groups), True)

    def plain(self, jobs):
        return [
            jnp.concatenate(
                [self.total_at({"terms": t, "columns": c}, flips) for t, flips, c in job], axis=-1
            ).astype(bf16)
            for job in jobs
        ]

    def wait(self, *tokens):
        values = after([[t[0] for t in group["terms"]] for group in self.groups], *tokens)
        for group, got in zip(self.groups, values):
            group["terms"] = [(v, t[1], t[2]) for v, t in zip(got, group["terms"])]

    def accept(self, values):
        values = list(values)
        if not values:
            return
        self.sent = values
        got = [
            swap(value.reshape(-1, value.shape[-1]), bit[0], bit[1], self.counts[bit[0]])
            for value, bit in zip(values, self.todo)
        ]
        column = 0
        for n, group in enumerate(self.groups):
            recv = got[n] if len(got) > 1 else got[0]
            bits = tuple(bit for bit in self.bits if bit not in group["fixed"])
            group["terms"].append(
                (self.shaped(recv, bits), bits, 0 if len(got) > 1 else column)
            )
            column += group["columns"]

    def rest(self):
        while self.orders:
            self.accept(self.plain(self.across()))

    def straight(self):
        seq = [bit for bit in self.bits if bit[0] == "seq"]
        jobs = []
        for jump in range(1, self.counts["seq"]):
            flips = {bit: jump // bit[1] % 2 for bit in seq}
            jobs.append(
                [
                    (list(g["terms"]), {**g["fixed"], **flips}, g["columns"])
                    for g in self.groups
                ]
            )
        for group in self.groups:
            group["fixed"].update({bit: 0 for bit in seq})
        if self.rows % 8 == 0:
            return jobs
        self.accept_straight(
            [
                jnp.concatenate(
                    [self.total_at({"terms": t, "columns": c}, flips) for t, flips, c in job],
                    axis=-1,
                ).astype(bf16)
                for job in jobs
            ]
        )
        return []

    def accept_straight(self, values):
        values = list(values)
        if not values:
            return
        self.sent = values
        for jump, value in enumerate(values):
            got = swap(value, "seq", jump + 1, self.counts["seq"])
            column = 0
            for group in self.groups:
                group["terms"].append((self.shaped(got, ()), (), column))
                column += group["columns"]

    def total(self, *tokens):
        groups = None
        if tokens:
            values = [[term[0] for term in group["terms"]] for group in self.groups]
            groups = after(values, *tokens)
        parts = []
        for n, group in enumerate(self.groups):
            terms = group["terms"]
            if groups:
                terms = [(v, t[1], t[2]) for v, t in zip(groups[n], terms)]
            parts.append(
                self.total_at({"terms": terms, "columns": group["columns"]}, group["fixed"])
            )
        return jnp.concatenate(parts, axis=-1)


def body(
    hidden_in,
    segment_ids,
    query_emb,
    positives,
    w_qkv,
    query_bias,
    value_bias,
    w_out,
    out_bias,
    norm1_gain,
    norm1_bias,
    w_up,
    up_bias,
    w_down,
    down_bias,
    norm2_gain,
    norm2_bias,
    w_proj,
):
    micro_count, row_count, local_len, width = hidden_in.shape
    full_len = segment_ids.shape[2]
    embed_width = w_proj.shape[1]
    ff = w_up.shape[1]
    queries_local = query_emb.shape[1]
    query_tokens = query_emb.shape[2]
    seq_count = lax.axis_size("seq")
    dp_count = lax.axis_size("dp")
    seq_pos = lax.axis_index("seq")
    dp_pos = lax.axis_index("dp")
    rows = micro_count * row_count
    tokens = rows * local_len
    far = 64
    window = 3 * local_len + far
    assert local_len + far >= PASSAGE_MOST - 1 and seq_count == 4

    x_own = hidden_in.reshape(rows, local_len, width)
    x_flat = x_own.reshape(tokens, width)
    low_half = seq_pos < 2
    inner = [(1, 2), (2, 1), (0, 0), (3, 3)]
    far_send = jnp.where(low_half, x_own[:, local_len - far :], x_own[:, :far])
    middle_x = lax.ppermute(x_flat, "seq", inner)
    far_x = swap(far_send.reshape(rows * far, width), "seq", 2, seq_count)
    side_x = swap(x_flat, "seq", 1, seq_count)
    pieces = [side_x, middle_x, far_x]

    seg_full = segment_ids.reshape(rows, full_len)
    edges = jnp.sum(
        (seg_full[:, None, :] < jnp.arange(1, SEGS, dtype=jnp.int32)[None, :, None]).astype(
            jnp.int32
        ),
        axis=2,
    )
    meta = jnp.concatenate(
        [
            jnp.stack(
                [
                    seq_pos * local_len,
                    dp_pos,
                    (seq_pos ^ 1) * local_len,
                    jnp.where((seq_pos == 1) | (seq_pos == 2), 3 - seq_pos, -9) * local_len,
                    jnp.where(
                        low_half, (seq_pos + 2) * local_len, (seq_pos - 1) * local_len - far
                    ),
                    dp_pos * row_count * SEGS,
                    dp_pos % 2,
                    seq_pos,
                ]
            ).astype(jnp.int32),
            edges.reshape(-1),
        ]
    )

    queries = query_emb.reshape(micro_count, queries_local * query_tokens, embed_width)
    bits = bits_of(dp_count)
    strides = [bits[:1]] + [bits[k : k + 2] for k in range(1, len(bits), 2)]

    queries = lax.all_gather(queries, "dp", axis=1, tiled=True)
    query_all = queries.shape[1]
    query_count = query_all // query_tokens
    wide = max(128, query_count)
    positives_wide = jnp.pad(
        positives, ((0, 0), (0, wide - query_count)), constant_values=-1
    )

    pairs = width // 128
    chunks = ff // width
    query, kv_own, x_t_own = call(
        functools.partial(own_kernel, (rows, local_len, width)),
        [
            ((tokens, width), bf16),
            ((rows, local_len, 2 * width), bf16),
            ((rows, width, local_len), bf16),
        ],
        [meta, query_bias, value_bias, x_flat, w_qkv],
        name="own",
        us=3,
    )
    forward = call(
        functools.partial(
            forward_kernel, (rows, local_len, far, window, full_len, width, row_count)
        ),
        [
            ((7 + chunks, width), f32),
            ((width, tokens), bf16),
            ((rows, pairs, 2 * local_len), f32),
            ((tokens, 128), f32),
            ((tokens, width), f32),
            ((width, tokens), bf16),
            ((tokens, embed_width), f32),
            ((tokens, embed_width), bf16),
            ((rows * SEGS, query_all), f32),
            ((rows, window, 2 * width), bf16),
            ((rows, width, window), bf16),
            ((tokens, width), f32),
            ((width, tokens), bf16),
            ((chunks, width, tokens), bf16),
            ((chunks, tokens, width), bf16),
        ],
        [
            meta,
            value_bias,
            out_bias,
            norm1_gain,
            norm1_bias,
            down_bias,
            norm2_gain,
            norm2_bias,
            up_bias,
            w_proj,
            query,
            x_flat,
            *pieces,
            kv_own,
            x_t_own,
            queries,
            w_qkv,
            w_out,
            w_up,
            w_down,
        ],
        [
            pltpu.VMEM((window, local_len), f32),
            pltpu.VMEM((tokens, width), bf16),
            pltpu.VMEM((tokens, width), bf16),
            pltpu.VMEM((tokens, width), bf16),
            pltpu.VMEM((tokens, width), bf16),
            pltpu.VMEM((rows * far, width), bf16),
            pltpu.VMEM(queries.shape, bf16),
            pltpu.VMEM((width, 3 * width), bf16),
            pltpu.VMEM((width, width), bf16),
            pltpu.VMEM((chunks, width, width), bf16),
            pltpu.VMEM((chunks, width, width), bf16),
            pltpu.VMEM((rows, window, 2 * width), bf16),
            pltpu.VMEM((rows, width, window), bf16),
            pltpu.VMEM((tokens, width), f32),
            pltpu.VMEM((width, tokens), bf16),
            pltpu.VMEM((chunks, width, tokens), bf16),
            pltpu.VMEM((chunks, tokens, width), bf16),
            pltpu.VMEM((tokens, width), bf16),
            pltpu.VMEM((tokens, width), f32),
            pltpu.SemaphoreType.DMA((13 + 4 * chunks,)),
        ],
        name="forward",
        us=20,
        hbm_ins=11,
        hbm_outs=6,
    )
    vectors, context_t, lse, cols, norm2, hidden2_t, proj, embed, parts = forward[:9]
    kv, x_t, norm1, hidden1_t, act_t, slope = forward[9:]

    others = [swap(parts, "seq", bit, seq_count) for bit in (1, 2, 3)]
    stat_rows = 8
    merged, score, stats = call(
        functools.partial(score_kernel, (rows, full_len, row_count, query_tokens)),
        [
            ((rows * SEGS, query_all), f32),
            ((rows * SEGS, wide), f32),
            ((stat_rows, wide), f32),
        ],
        [meta, parts, *others, positives_wide],
        name="score",
        us=2,
    )
    is_whole = lax.broadcasted_iota(jnp.int32, stats.shape, 0) < micro_count
    for group in strides:
        jumps = group if len(group) == 1 else [group[0], group[1], group[0] + group[1]]
        recv = [swap(stats, "dp", jump, dp_count) for jump in jumps]
        if len(recv) == 1:
            best = jnp.maximum(stats, recv[0])
            whole = jnp.exp(stats - best) + jnp.exp(recv[0] - best)
            hits = stats + recv[0]
        else:
            best = jnp.maximum(jnp.maximum(stats, recv[0]), jnp.maximum(recv[1], recv[2]))
            whole = (jnp.exp(stats - best) + jnp.exp(recv[0] - best)) + (
                jnp.exp(recv[1] - best) + jnp.exp(recv[2] - best)
            )
            hits = (stats + recv[0]) + (recv[1] + recv[2])
        stats = jnp.where(is_whole, best + jnp.log(whole), hits)

    devices = dp_count * seq_count

    def places(depth, columns):
        block = depth // dp_count
        if block % 16 == 0:
            return [((dp_count // 2, block, columns), bf16)] * 2
        return [((depth, columns), bf16)]

    where = {"dp": dp_pos, "seq": seq_pos}
    counts = {"dp": dp_count, "seq": seq_count}
    down_places = places(ff, width)
    loss, d_proj, g_resid2, vec_c, *outs = call(
        functools.partial(
            upper_kernel, (rows, local_len, full_len, row_count, query_tokens)
        ),
        [
            ((micro_count, wide), f32),
            ((width, embed_width), bf16),
            ((tokens, width), f32),
            ((8, width), f32),
        ]
        + down_places,
        [
            meta,
            merged,
            score,
            stats,
            positives_wide,
            queries,
            embed,
            proj,
            norm2,
            hidden2_t,
            cols,
            vectors,
            w_proj,
            act_t,
        ],
        [
            pltpu.VMEM((chunks, width, width), bf16),
            pltpu.VMEM((chunks, width, tokens), bf16),
            pltpu.VMEM((rows * SEGS, query_all), f32),
            pltpu.VMEM((tokens, embed_width), f32),
            pltpu.SemaphoreType.DMA((1 + max(dp_count, chunks),)),
        ],
        hbm_ins=1,
        name="upper",
        us=8,
        hbm_outs=len(down_places),
    )
    losses = lax.dynamic_slice_in_dim(loss, dp_pos * queries_local, queries_local, 1)
    down = Chunk(outs, where, counts)
    down.core()

    up_places = places(width, ff + width + embed_width)
    d_ubias, g_resid1, g_context, vec_d, *outs = call(
        lower_kernel,
        [
            ((chunks, 1, width), f32),
            ((tokens, width), f32),
            ((tokens, width), bf16),
            ((8, width), f32),
        ]
        + up_places,
        [
            meta,
            g_resid2,
            hidden1_t,
            norm1,
            cols,
            vectors,
            context_t,
            w_out,
            d_proj,
            w_down,
            w_up,
            slope,
        ],
        [
            pltpu.VMEM((chunks, width, width), bf16),
            pltpu.VMEM((chunks, width, width), bf16),
            pltpu.VMEM((chunks, tokens, width), bf16),
            pltpu.VMEM((tokens, width), f32),
            pltpu.VMEM((tokens, width), bf16),
            pltpu.VMEM((chunks, width, width), bf16),
            pltpu.VMEM((width, width + embed_width), bf16),
            pltpu.SemaphoreType.DMA(((3 + dp_count) * chunks + dp_count,)),
        ],
        name="lower",
        us=13,
        hbm_ins=3,
        hbm_outs=len(up_places),
    )
    up = Chunk(outs, where, counts)
    up.core()

    def fold(chunks_jobs, *tokens, us=FOLD):
        jobs = [job for _, got, _ in chunks_jobs for job in got]
        values = call(nothing, [], [meta], name="fold", deps=tokens, jobs=jobs, us=us) if jobs else []
        at = 0
        sent = []
        for chunk, got, accept in chunks_jobs:
            accept(values[at : at + len(got)])
            at += len(got)
            sent += chunk.sent
        return sent

    sends = fold([(down, down.across(), down.accept)], g_resid1, us=3)
    last_places = places(width, 3 * width + 128)
    sends = fold([(up, up.across(), up.accept)], *sends, us=3)
    g_own, g_side, g_middle, g_far, *outs = call(
        functools.partial(
            attention_kernel, (rows, local_len, far, window, full_len, width, devices)
        ),
        [
            ((tokens, width), f32),
            ((tokens, width), bf16),
            ((tokens, width), bf16),
            ((rows * far, width), bf16),
        ]
        + last_places,
        [meta, g_context, query, lse, vec_c, vec_d, d_ubias, g_resid1, kv, x_t, w_qkv],
        [
            pltpu.VMEM((rows, window, 2 * width), bf16),
            pltpu.VMEM((rows, width, window), bf16),
            pltpu.VMEM((tokens, width), bf16),
            pltpu.VMEM((rows, window, 2 * width), bf16),
            pltpu.VMEM((width, 3 * width), bf16),
            pltpu.VMEM((window, local_len), f32),
            pltpu.VMEM((3, width, width), bf16),
            pltpu.VMEM((width, 128), bf16),
            pltpu.VMEM((width, 128), f32),
            pltpu.SemaphoreType.DMA((rows + 2 + 4 * dp_count,)),
        ],
        name="attention",
        us=20,
        hbm_ins=3,
        hbm_outs=len(last_places),
        deps=sends,
    )
    last = Chunk(outs, where, counts)
    received = [term[0] for group in up.groups for term in group["terms"]]
    halo = {}
    token = [g_own]
    for step in ORDER:
        if step in ("m", "s", "f"):
            token = token + [halo[step.upper()]]
        elif step == "M":
            halo[step] = lax.ppermute(after(g_middle, token), "seq", inner)
        elif step == "S":
            halo[step] = swap(after(g_side, token), "seq", 1, seq_count)
        elif step == "F":
            halo[step] = swap(after(g_far, token), "seq", 2, seq_count)
        elif step == "C0":
            last.other = after(last.other, token, received)
            last.core()
        elif step == "c0":
            token = token + [last.recv]
        elif step == "C1":
            token = fold([(last, last.across(), last.accept)], *token)
        elif step == "C3":
            last.rest()
            token = fold([(last, last.straight(), last.accept_straight)], *token)
        else:
            chunk = {"A": down, "B": up, "C": last}[step[0]]
            if not step[2:]:
                chunk.wait(*token)
            if step[1] == "2":
                jobs = chunk.across()
            else:
                chunk.rest()
                jobs = chunk.along(1 if step[1] == "3" else 2)
            if step[2:] and jobs:
                token = list(call(nothing, [], [meta], name="fold", deps=token, jobs=jobs, us=FOLD))
                chunk.accept(token)
            else:
                chunk.accept(chunk.plain(jobs))
                token = list(chunk.sent)
    g_own, from_side, from_middle, from_far = after(
        (g_own, halo["S"], halo["M"], halo["F"]), *token
    )
    from_far = from_far.reshape(rows, far, width).astype(f32)
    pad = ((0, 0), (local_len - far, 0), (0, 0))
    flip = ((0, 0), (0, local_len - far), (0, 0))
    grad_in = (g_own + from_side.astype(f32) + from_middle.astype(f32)).reshape(
        rows, local_len, width
    ) + jnp.where(low_half, jnp.pad(from_far, pad), jnp.pad(from_far, flip))

    down_part = down.total(grad_in)
    up_part = up.total(down_part)
    last_part = last.total(up_part)
    some = 4 * width // devices
    vec_at = 3 * width
    vec_part = last_part[:3, vec_at : vec_at + some]
    return (
        embed.reshape(micro_count, row_count, local_len, embed_width),
        losses,
        grad_in.reshape(micro_count, row_count, local_len, width),
        last_part[:, : 3 * width].reshape(-1),
        up_part[:, ff : ff + width].reshape(-1),
        up_part[:, :ff].reshape(-1),
        down_part.reshape(-1),
        up_part[:, ff + width :].reshape(-1),
        vec_part[0],
        vec_part[1:].reshape(-1),
    )


def solution(mesh):
    in_specs = (
        P(None, "dp", "seq", None),
        P(None, "dp", None),
        P(None, "dp", None, None),
    ) + (P(),) * 15
    out_specs = (
        P(None, "dp", "seq", None),
        P(None, "dp"),
        P(None, "dp", "seq", None),
    ) + (P(("dp", "seq")),) * 7
    return jax.shard_map(body, mesh=mesh, in_specs=in_specs, out_specs=out_specs, check_vma=False)
```

```python
import functools

import jax
import jax.numpy as jnp
from jax import lax
from jax.experimental import pallas as pl
from jax.experimental.pallas import tpu as pltpu
from jax.sharding import PartitionSpec as P

HEADS = 12
SEGS = 4
PASSAGE_MOST = 180

SHARP = 20.0
EDGES = 8
COST = 4e9
FOLD = 0.3
ORDER = (
    "M", "A2", "C0", "B2", "m", "S", "C1", "A3", "s", "F", "B3", "A4", "C2", "B4", "C3", "f",
)
LN_EPS = 1e-12
NORM_EPS = 1e-12
MASKED = -1e30
HIGH = lax.Precision.HIGHEST
bf16 = jnp.bfloat16
f32 = jnp.float32
VMEM = pl.BlockSpec(memory_space=pltpu.VMEM)
HBM = pl.BlockSpec(memory_space=pltpu.HBM)
SMEM = pl.BlockSpec(memory_space=pltpu.SMEM)
PARAMS = pltpu.CompilerParams(vmem_limit_bytes=58 << 20)


def bits_of(count):
    return [1 << k for k in range(count.bit_length() - 1)]


def swap(value, axis, bit, count):
    return lax.ppermute(value, axis, [(i, i ^ bit) for i in range(count)])


def dot(left, right, left_dim, right_dim, precision=None):
    return lax.dot_general(
        left,
        right,
        (((left_dim,), (right_dim,)), ((), ())),
        precision=precision,
        preferred_element_type=f32,
    )


def ident(pos, meta, row, length):
    seg = jnp.zeros(pos.shape, jnp.int32)
    for s in range(SEGS - 1):
        seg = seg + (pos >= meta[EDGES + row * (SEGS - 1) + s]).astype(jnp.int32)
    return jnp.where((pos >= 0) & (pos < length), seg, -1)


def key_positions(meta, local, shape):
    w = lax.broadcasted_iota(jnp.int32, shape, 0)
    pos = meta[0] + w
    for piece in range(1, 4):
        pos = jnp.where(w >= piece * local, meta[1 + piece] + w - piece * local, pos)
    return pos


def pair_rows(block, even):
    zero = jnp.zeros_like(block)
    return jnp.concatenate([jnp.where(even, block, zero), jnp.where(even, zero, block)], axis=0)


def attention_bias(meta, row, local, window, length):
    key_seg = ident(key_positions(meta, local, (window, local)), meta, row, length)
    query_seg = ident(
        meta[0] + lax.broadcasted_iota(jnp.int32, (window, local), 1), meta, row, length
    )
    return jnp.where(key_seg == query_seg, 0.0, MASKED).astype(f32)


def copies_out(scr, outs, sems, first, core, columns, part=0, parts=1):
    size = scr.shape[0]
    if len(outs) == 1:
        pieces = [(scr, outs[0].at[pl.ds(part * size, size), columns])]
    else:
        high, block, _ = outs[0].shape
        pieces = []
        for k in range(high // parts):
            for out, which in ((outs[0], 1 - core), (outs[1], core)):
                rows = pl.ds(pl.multiple_of((2 * k + which) * block, 16), block)
                pieces.append((scr.at[rows, :], out.at[part * (high // parts) + k, :, columns]))
    return [
        pltpu.make_async_copy(source, target, sems.at[first + n])
        for n, (source, target) in enumerate(pieces)
    ]


def begin(copies):
    for copy in copies:
        copy.start()


def finish(copies):
    for copy in copies:
        copy.wait()


def own_kernel(dims, meta, query_bias, value_bias, x_own, w_qkv, query, kv, x_t):
    rows, local, width = dims
    x = x_own[...]
    got = dot(x, w_qkv[...], 1, 0)
    query[...] = (got[:, :width] + query_bias[...].reshape(1, width)).astype(bf16)
    keys = got[:, width : 2 * width].astype(bf16)
    values = (got[:, 2 * width :] + value_bias[...].reshape(1, width)).astype(bf16)
    for r in range(rows):
        mine = slice(r * local, (r + 1) * local)
        kv[r, :, :width] = keys[mine]
        kv[r, :, width:] = values[mine]
        x_t[r] = x[mine].T


def forward_kernel(
    dims,
    meta,
    value_bias_in,
    out_bias_in,
    gain1_in,
    shift1_in,
    down_bias_in,
    gain2_in,
    shift2_in,
    up_bias_in,
    w_proj,
    query,
    x_own_hbm,
    side_hbm,
    middle_hbm,
    far_hbm,
    kv_own_hbm,
    x_t_own_hbm,
    queries_hbm,
    w_qkv_hbm,
    w_out_hbm,
    w_up_hbm,
    w_down_hbm,
    vectors,
    context_t,
    lse,
    cols,
    norm2,
    hidden2_t,
    proj,
    embed,
    parts,
    kv_hbm,
    x_t_hbm,
    norm1_hbm,
    hidden1_t_hbm,
    act_t_hbm,
    slope_hbm,
    bias_scr,
    context,
    x_own,
    side,
    middle,
    far_part,
    queries,
    w_qkv,
    w_out,
    w_up,
    w_down,
    kv,
    x_t,
    norm1,
    hidden1_t,
    act_t,
    slope,
    hidden_scr,
    ffn_scr,
    sems,
):
    rows, local, far, window, length, width, row_count = dims
    chunks = w_up.shape[0]
    cut_kv = pl.ds(width, 2 * width)
    kv_here = pltpu.make_async_copy(
        w_qkv_hbm.at[:, cut_kv], w_qkv.at[:, cut_kv], sems.at[0]
    )
    out_here = pltpu.make_async_copy(w_out_hbm, w_out, sems.at[1])

    def up_here(c):
        cut = pl.ds(pl.multiple_of(c * width, 128), width)
        return pltpu.make_async_copy(w_up_hbm.at[:, cut], w_up.at[c], sems.at[2 + c])

    def down_here(c):
        cut = pl.ds(pl.multiple_of(c * width, 128), width)
        return pltpu.make_async_copy(
            w_down_hbm.at[cut, :], w_down.at[c], sems.at[2 + chunks + c]
        )

    base = 2 + 2 * chunks
    pieces_here = [
        pltpu.make_async_copy(source, target, sems.at[base + 4 + 2 * chunks + n])
        for n, (source, target) in enumerate(
            ((x_own_hbm, x_own), (side_hbm, side), (middle_hbm, middle), (far_hbm, far_part))
        )
    ]
    queries_here = pltpu.make_async_copy(
        queries_hbm, queries, sems.at[base + 8 + 2 * chunks]
    )
    own = pl.ds(0, local)
    own_here = [
        pltpu.make_async_copy(
            kv_own_hbm, kv.at[:, own, :], sems.at[base + 9 + 2 * chunks]
        ),
        pltpu.make_async_copy(
            x_t_own_hbm, x_t.at[:, :, own], sems.at[base + 10 + 2 * chunks]
        ),
    ]
    begin([kv_here] + pieces_here[1:] + own_here + [pieces_here[0], out_here])
    for c in range(chunks):
        begin([up_here(c), down_here(c)])
    queries_here.start()
    for n, vector in enumerate(
        (
            value_bias_in,
            out_bias_in,
            gain1_in,
            shift1_in,
            down_bias_in,
            gain2_in,
            shift2_in,
        )
    ):
        vectors[n : n + 1, :] = vector[...].reshape(1, width)
    for c in range(chunks):
        vectors[7 + c : 8 + c, :] = up_bias_in[pl.ds(c * width, width)].reshape(1, width)
    value_bias = vectors[0:1, :]
    kv_out = pltpu.make_async_copy(kv, kv_hbm, sems.at[base])
    x_out = pltpu.make_async_copy(x_t, x_t_hbm, sems.at[base + 1])
    norm_out = pltpu.make_async_copy(norm1, norm1_hbm, sems.at[base + 2])
    hidden_out = pltpu.make_async_copy(hidden1_t, hidden1_t_hbm, sems.at[base + 3])

    def act_out(c):
        return pltpu.make_async_copy(act_t.at[c], act_t_hbm.at[c], sems.at[base + 4 + c])

    def slope_out(c):
        return pltpu.make_async_copy(
            slope.at[c], slope_hbm.at[c], sems.at[base + 4 + chunks + c]
        )

    kv_here.wait()
    offset = local
    for n, (piece, size) in enumerate(((side, local), (middle, local), (far_part, far))):
        pieces_here[n + 1].wait()
        got = dot(piece[...], w_qkv[:, width:], 1, 0)
        got_k = got[:, :width].astype(bf16)
        got_v = (got[:, width:] + value_bias).astype(bf16)
        for r in range(rows):
            mine = slice(r * size, (r + 1) * size)
            kv[r, offset : offset + size, :width] = got_k[mine]
            kv[r, offset : offset + size, width:] = got_v[mine]
            x_t[r, :, offset : offset + size] = piece[mine, :].T
        offset += size
    finish(own_here + pieces_here[:1])
    begin([kv_out, x_out])
    even = lax.broadcasted_iota(jnp.int32, (local, 128), 1) < 64
    upper = lax.broadcasted_iota(jnp.int32, (128, local), 0) < 64
    pairs = width // 128

    def attend(r, carry):
        bias_scr[...] = attention_bias(meta, r, local, window, length)
        own = pl.ds(pl.multiple_of(r * local, 128), local)
        for p in range(pairs):
            lanes = slice(p * 128, (p + 1) * 128)
            q2 = pair_rows(query[own, lanes] * bf16(0.125), even)
            k2 = kv[r, :, lanes]
            v2 = kv[r, :, width + p * 128 : width + (p + 1) * 128]
            bias = bias_scr[...]
            s = dot(k2, q2, 1, 1) + jnp.concatenate([bias, bias], axis=1)
            top = jnp.max(s, axis=0, keepdims=True)
            e = jnp.exp(s - top)
            total = jnp.sum(e, axis=0, keepdims=True)
            lse[r, p : p + 1, :] = top + jnp.log(total)
            o = dot(v2, e.astype(bf16), 0, 0) * (1.0 / total)
            o = jnp.where(upper, o[:, :local], o[:, local:])
            context_t[lanes, own] = o.astype(bf16)
            context[own, lanes] = o.T.astype(bf16)
        return carry

    lax.fori_loop(0, rows, attend, 0, unroll=True)
    out_here.wait()
    attended = dot(context[...], w_out[...], 1, 0) + vectors[1:2, :]
    resid = x_own[...].astype(f32) + attended
    centred = resid - jnp.mean(resid, axis=-1, keepdims=True)
    rstd1 = lax.rsqrt(jnp.mean(centred * centred, axis=-1, keepdims=True) + LN_EPS)
    n1 = centred * rstd1
    norm1[...] = n1
    hidden1 = n1 * vectors[2:3, :] + vectors[3:4, :]
    hidden1_low = hidden1.astype(bf16)
    hidden1_t[...] = hidden1_low.T
    begin([norm_out, hidden_out])
    hidden_scr[...] = hidden1_low
    ffn_scr[...] = hidden1 + vectors[4:5, :]

    def feed(c, carry):
        up_here(c).wait()
        up = dot(hidden_scr[...], w_up[c], 1, 0) + vectors[pl.ds(7 + c, 1), :]
        cdf = 0.5 * (1.0 + lax.erf(up * (0.5**0.5)))
        act_low = (up * cdf).astype(bf16)
        act_t[c] = act_low.T
        slope[c] = (cdf + up * (jnp.exp(-0.5 * up * up) * 0.3989422804014327)).astype(bf16)
        begin([act_out(c), slope_out(c)])
        down_here(c).wait()
        ffn_scr[...] += dot(act_low, w_down[c], 1, 0)
        return carry

    lax.fori_loop(0, chunks, feed, 0)
    resid = ffn_scr[...]
    centred = resid - jnp.mean(resid, axis=-1, keepdims=True)
    rstd2 = lax.rsqrt(jnp.mean(centred * centred, axis=-1, keepdims=True) + LN_EPS)
    n2 = centred * rstd2
    norm2[...] = n2
    lane = lax.broadcasted_iota(jnp.int32, cols.shape, 1)
    cols[...] = jnp.where(lane == 0, rstd1, rstd2)
    hidden2_low = (n2 * vectors[5:6, :] + vectors[6:7, :]).astype(bf16)
    hidden2_t[...] = hidden2_low.T
    out = dot(hidden2_low, w_proj[...], 1, 0)
    proj[...] = out
    inv = lax.rsqrt(jnp.sum(out * out, axis=-1, keepdims=True) + NORM_EPS)
    embed[...] = (out * inv).astype(bf16)

    def match(r, carry):
        own = pl.ds(pl.multiple_of(r * local, 128), local)
        sharp = dot(embed[own, :], queries[r // row_count], 1, 1) * SHARP
        seg = ident(meta[0] + lax.broadcasted_iota(jnp.int32, (local, 1), 0), meta, r, length)
        tops = []
        shift = jnp.zeros_like(sharp)
        for s in range(SEGS):
            inside = seg == s
            top = jnp.max(jnp.where(inside, sharp, MASKED), axis=0, keepdims=True)
            tops.append(top)
            shift = jnp.where(inside, top, shift)
        e = jnp.exp(sharp - shift)
        for s in range(SEGS):
            total = jnp.sum(jnp.where(seg == s, e, 0.0), axis=0, keepdims=True)
            some = total > 0.0
            parts[pl.ds(r * SEGS + s, 1), :] = jnp.where(
                some, tops[s] + jnp.log(jnp.where(some, total, 1.0)), MASKED
            )
        return carry

    queries_here.wait()
    lax.fori_loop(0, rows, match, 0, unroll=True)
    finish([kv_out, x_out, norm_out, hidden_out])
    for c in range(chunks):
        finish([act_out(c), slope_out(c)])


def score_kernel(dims, meta, first, second, third, fourth, positives, merged, score, stats):
    rows, length, row_count, query_tokens = dims
    half = rows * SEGS
    parts = [ref[...] for ref in (first, second, third, fourth)]
    top = jnp.maximum(jnp.maximum(parts[0], parts[1]), jnp.maximum(parts[2], parts[3]))
    sums = [jnp.exp(part - top) for part in parts]
    whole = top + jnp.log((sums[0] + sums[1]) + (sums[2] + sums[3]))
    merged[...] = whole
    sub = lax.broadcasted_iota(jnp.int32, (half, 1), 0)
    count = jnp.zeros((half, 1), f32)
    for r in range(rows):
        edges = [0] + [meta[EDGES + r * (SEGS - 1) + s] for s in range(SEGS - 1)] + [length]
        for s in range(SEGS):
            size = (edges[s + 1] - edges[s]).astype(f32)
            count = jnp.where(sub == r * SEGS + s, size, count)
    match = whole - jnp.log(count)
    wide = score.shape[1]
    shape = (match.shape[1], wide)
    group = (
        lax.broadcasted_iota(jnp.int32, shape, 0) // query_tokens
        == lax.broadcasted_iota(jnp.int32, shape, 1)
    ).astype(f32)
    got = dot(match, group, 1, 0, HIGH)
    score[...] = got
    per = row_count * SEGS
    micros = rows // row_count
    stats[...] = jnp.zeros(stats.shape, f32)
    for m in range(micros):
        part = got[m * per : (m + 1) * per]
        at = lax.broadcasted_iota(jnp.int32, (per, wide), 0) + meta[5]
        chosen = at == positives[m : m + 1, :]
        best = jnp.max(part, axis=0, keepdims=True)
        stats[m : m + 1, :] = best + jnp.log(
            jnp.sum(jnp.exp(part - best), axis=0, keepdims=True)
        )
        stats[micros + m : micros + m + 1, :] = jnp.sum(
            jnp.where(chosen, part, 0.0), axis=0, keepdims=True
        )


def upper_kernel(
    dims,
    meta,
    merged,
    score,
    stats,
    positives,
    queries,
    embed,
    proj,
    norm2,
    hidden2_t,
    cols,
    vectors,
    w_proj,
    act_t_hbm,
    loss,
    d_proj,
    g_resid2,
    vec,
    *rest,
):
    outs, (scr, act_t, factor_scr, unit_scr, sems) = rest[:-5], rest[-5:]
    rows, local, length, row_count, query_tokens = dims
    chunks = act_t.shape[0]
    gain2 = vectors[5:6, :]
    act_here = pltpu.make_async_copy(act_t_hbm, act_t, sems.at[0])
    act_here.start()
    micros = rows // row_count
    per = row_count * SEGS
    wide = score.shape[1]
    all_queries = merged.shape[1]
    shape = (wide, all_queries)
    group = (
        lax.broadcasted_iota(jnp.int32, shape, 1) // query_tokens
        == lax.broadcasted_iota(jnp.int32, shape, 0)
    ).astype(f32)
    pieces = []
    for m in range(micros):
        whole = stats[m : m + 1, :]
        loss[m : m + 1, :] = whole - stats[micros + m : micros + m + 1, :]
        part = score[m * per : (m + 1) * per, :]
        at = lax.broadcasted_iota(jnp.int32, (per, wide), 0) + meta[5]
        chosen = (at == positives[m : m + 1, :]).astype(f32)
        pieces.append(jnp.exp(part - whole) - chosen)
    factor_scr[...] = SHARP * dot(jnp.concatenate(pieces, axis=0), group, 1, 0, HIGH)

    def pull(r, carry):
        own = pl.ds(pl.multiple_of(r * local, 128), local)
        m = r // row_count
        sharp = dot(embed[own, :], queries[m], 1, 1) * SHARP
        seg = ident(meta[0] + lax.broadcasted_iota(jnp.int32, (local, 1), 0), meta, r, length)
        shift = jnp.zeros_like(sharp)
        scale = jnp.zeros_like(sharp)
        for s in range(SEGS):
            at = pl.ds(r * SEGS + s, 1)
            shift = jnp.where(seg == s, merged[at, :], shift)
            scale = jnp.where(seg == s, factor_scr[at, :], scale)
        g_sim = (scale * jnp.exp(sharp - shift)).astype(bf16)
        unit_scr[own, :] = dot(g_sim, queries[m], 1, 0)
        return carry

    lax.fori_loop(0, rows, pull, 0, unroll=True)
    g_unit = unit_scr[...]
    out = proj[...]
    inv = lax.rsqrt(jnp.sum(out * out, axis=-1, keepdims=True) + NORM_EPS)
    unit = out * inv
    g_proj = ((g_unit - unit * jnp.sum(unit * g_unit, axis=-1, keepdims=True)) * inv).astype(bf16)
    n2 = norm2[...]
    d_proj[...] = dot(hidden2_t[...], g_proj, 1, 0).astype(bf16)
    g_hidden = dot(g_proj, w_proj[...], 1, 1)
    vec[0:1, :] = jnp.sum(g_hidden * n2, axis=0, keepdims=True)
    vec[1:2, :] = jnp.sum(g_hidden, axis=0, keepdims=True)
    g_n = g_hidden * gain2
    g_v = cols[:, 1:2] * (
        g_n
        - jnp.mean(g_n, axis=-1, keepdims=True)
        - n2 * jnp.mean(g_n * n2, axis=-1, keepdims=True)
    )
    g_resid2[...] = g_v
    low = g_v.astype(bf16)
    vec[2:3, :] = jnp.sum(low.astype(f32), axis=0, keepdims=True)
    act_here.wait()
    columns = slice(0, scr.shape[2])
    each = 2 * (outs[0].shape[0] // chunks) if len(outs) == 2 else 1

    def leaving(c):
        return copies_out(scr.at[c], outs, sems, 1 + c * each, meta[6], columns, c, chunks)

    for c in range(chunks):
        scr[c] = dot(act_t[c], low, 1, 0).astype(bf16)
        begin(leaving(c))
    for c in range(chunks):
        finish(leaving(c))


def lower_kernel(
    meta,
    g_resid2,
    hidden1_t,
    norm1,
    cols,
    vectors,
    context_t,
    w_out,
    d_proj,
    w_down_hbm,
    w_up_hbm,
    slope_hbm,
    d_ubias,
    g_resid1,
    g_context,
    vec,
    *rest,
):
    outs, (w_down, w_up, slope, hidden_scr, low_scr, scr, out_scr, sems) = rest[:-8], rest[-8:]
    chunks, width, _ = w_up.shape
    gain1 = vectors[2:3, :]
    each = 2 * outs[0].shape[0] if len(outs) == 2 else 1

    def here(c):
        cut = pl.ds(pl.multiple_of(c * width, 128), width)
        return [
            pltpu.make_async_copy(w_down_hbm.at[cut, :], w_down.at[c], sems.at[3 * c]),
            pltpu.make_async_copy(slope_hbm.at[c], slope.at[c], sems.at[3 * c + 1]),
            pltpu.make_async_copy(w_up_hbm.at[:, cut], w_up.at[c], sems.at[3 * c + 2]),
        ]

    def leaving(c):
        cut = pl.ds(pl.multiple_of(c * width, 128), width)
        return copies_out(scr.at[c], outs, sems, 3 * chunks + c * each, meta[6], cut)

    for c in range(chunks):
        begin(here(c))
    hidden_scr[...] = g_resid2[...]
    low_scr[...] = g_resid2[...].astype(bf16)

    def gate(c, carry):
        finish(here(c))
        g_act = dot(low_scr[...], w_down[c], 1, 1)
        g_up = (g_act * slope[c].astype(f32)).astype(bf16)
        d_ubias[c] = jnp.sum(g_up.astype(f32), axis=0, keepdims=True)
        scr[c] = dot(hidden1_t[...], g_up, 1, 0).astype(bf16)
        begin(leaving(c))
        hidden_scr[...] += dot(g_up, w_up[c], 1, 1)
        return carry

    lax.fori_loop(0, chunks, gate, 0)
    n1 = norm1[...]
    g_hidden = hidden_scr[...]
    vec[0:1, :] = jnp.sum(g_hidden * n1, axis=0, keepdims=True)
    vec[1:2, :] = jnp.sum(g_hidden, axis=0, keepdims=True)
    g_n = g_hidden * gain1
    g_v = cols[:, 0:1] * (
        g_n
        - jnp.mean(g_n, axis=-1, keepdims=True)
        - n1 * jnp.mean(g_n * n1, axis=-1, keepdims=True)
    )
    g_resid1[...] = g_v
    low = g_v.astype(bf16)
    vec[2:3, :] = jnp.sum(low.astype(f32), axis=0, keepdims=True)
    out_scr[:, :width] = dot(context_t[...], low, 1, 0).astype(bf16)
    out_scr[:, width:] = d_proj[...]
    columns = slice(chunks * width, chunks * width + out_scr.shape[1])
    last = copies_out(out_scr, outs, sems, (3 + each) * chunks, meta[6], columns)
    begin(last)
    g_context[...] = dot(low, w_out[...], 1, 1).astype(bf16)
    for c in range(chunks):
        finish(leaving(c))
    finish(last)


def attention_kernel(
    dims,
    meta,
    g_context,
    query,
    lse,
    vec_c,
    vec_d,
    d_ubias,
    g_resid1,
    kv_hbm,
    x_t_hbm,
    w_qkv_hbm,
    g_own,
    g_side,
    g_middle,
    g_far,
    *rest,
):
    outs, scratch = rest[:-10], rest[-10:]
    kv, x_t, g_query, g_kv, w_qkv, bias_scr, scr, low_scr, vec_scr, sems = scratch
    rows, local, far, window, length, width, devices = dims
    pairs = width // 128
    even = lax.broadcasted_iota(jnp.int32, (local, 128), 1) < 64
    upper = lax.broadcasted_iota(jnp.int32, (128, local), 0) < 64

    def kv_here(r):
        return pltpu.make_async_copy(kv_hbm.at[r], kv.at[r], sems.at[r])

    for r in range(rows):
        kv_here(r).start()
    x_here = pltpu.make_async_copy(x_t_hbm, x_t, sems.at[rows])
    w_here = pltpu.make_async_copy(w_qkv_hbm, w_qkv, sems.at[rows + 1])
    begin([x_here, w_here])

    def attend(r, carry):
        kv_here(r).wait()
        bias_scr[...] = attention_bias(meta, r, local, window, length)
        own = pl.ds(pl.multiple_of(r * local, 128), local)
        for p in range(pairs):
            lanes = slice(p * 128, (p + 1) * 128)
            vlanes = slice(width + p * 128, width + (p + 1) * 128)
            q2 = pair_rows(query[own, lanes] * bf16(0.125), even)
            k2 = kv[r, :, lanes]
            v2 = kv[r, :, vlanes]
            gc2 = pair_rows(g_context[own, lanes], even)
            bias = bias_scr[...]
            s = dot(k2, q2, 1, 1) + jnp.concatenate([bias, bias], axis=1)
            prob = jnp.exp(s - lse[r, p : p + 1, :])
            g_prob = dot(v2, gc2, 1, 1)
            weighted = prob * g_prob
            inner = jnp.sum(weighted, axis=0, keepdims=True)
            g_score = (weighted - prob * inner).astype(bf16)
            g_kv[r, :, vlanes] = dot(prob.astype(bf16), gc2, 1, 0).astype(bf16)
            g_kv[r, :, lanes] = dot(g_score, q2, 1, 0).astype(bf16)
            g_q = dot(k2, g_score, 0, 0)
            g_q = jnp.where(upper, g_q[:, :local], g_q[:, local:]) * 0.125
            g_query[own, lanes] = g_q.T.astype(bf16)
        return carry

    lax.fori_loop(0, rows, attend, 0, unroll=True)
    x_here.wait()
    each = 2 * outs[0].shape[0] if len(outs) == 2 else 1
    copies = []
    for c in range(3):
        total = None
        for r in range(rows):
            if c == 0:
                part = dot(x_t[r, :, :local], g_query[r * local : (r + 1) * local, :], 1, 0)
            else:
                part = dot(x_t[r], g_kv[r, :, (c - 1) * width : c * width], 1, 0)
            total = part if total is None else total + part
        scr[c] = total.astype(bf16)
        columns = slice(c * width, (c + 1) * width)
        got = copies_out(scr.at[c], outs, sems, rows + 2 + c * each, meta[6], columns)
        begin(got)
        copies += got
    d_qbias = jnp.sum(g_query[...].astype(f32), axis=0, keepdims=True)
    d_vbias = None
    for r in range(rows):
        part = jnp.sum(g_kv[r, :, width:].astype(f32), axis=0, keepdims=True)
        d_vbias = part if d_vbias is None else d_vbias + part
    lower = [d_qbias, d_vbias, vec_d[2:3, :], vec_d[0:1, :]]
    higher = [vec_d[1:2, :], vec_c[2:3, :], vec_c[0:1, :], vec_c[1:2, :]]
    higher += [d_ubias[c] for c in range(d_ubias.shape[0])]
    block = width // devices
    some = 4 * width // devices
    vec_scr[...] = jnp.zeros(vec_scr.shape, f32)
    for device in range(devices):
        for row, vectors, start in (
            (0, lower, device * some),
            (1, higher, 2 * device * some),
            (2, higher, (2 * device + 1) * some),
        ):
            source = vectors[start // width]
            at = start % width
            vec_scr[device * block + row : device * block + row + 1, :some] = source[
                :, at : at + some
            ]
    low_scr[...] = vec_scr[...].astype(bf16)
    columns = slice(3 * width, 3 * width + 128)
    got = copies_out(low_scr, outs, sems, rows + 2 + 3 * each, meta[6], columns)
    begin(got)
    w_here.wait()

    def back(r, carry):
        own = pl.ds(pl.multiple_of(r * local, 128), local)
        part = dot(g_kv[r], w_qkv[:, width:], 1, 1)
        g_own[own, :] = (
            g_resid1[own, :] + dot(g_query[own, :], w_qkv[:, :width], 1, 1) + part[:local]
        )
        g_side[own, :] = part[local : 2 * local].astype(bf16)
        g_middle[own, :] = part[2 * local : 3 * local].astype(bf16)
        g_far[pl.ds(pl.multiple_of(r * far, 64), far), :] = part[3 * local :].astype(bf16)
        return carry

    lax.fori_loop(0, rows, back, 0, unroll=True)
    finish(copies + got)


def nothing(meta):
    del meta


def job_index(meta, bits, fixed):
    index = []
    for bit in bits:
        if bit in fixed:
            axis, stride = bit
            at = (meta[1] if axis == "dp" else meta[7]) // stride % 2
            index.append(1 - at if fixed[bit] else at)
        else:
            index.append(slice(None))
    return tuple(index)


def call(
    kernel,
    outs,
    ins,
    scratch=(),
    name=None,
    hbm_outs=0,
    hbm_ins=0,
    deps=(),
    jobs=(),
    us=3,
):
    deps = tuple(deps)
    count = len(ins)
    job_ins, job_outs, job_scratch, job_scratch_out = [], [], [], []
    for job in jobs:
        columns = 0
        for terms, fixed, size in job:
            for value, bits, column in terms:
                free = len([bit for bit in bits if bit not in fixed])
                shape = (2,) * free + (value.shape[-2], size)
                job_ins.append(value)
                job_scratch.append(pltpu.VMEM(shape, bf16))
            columns += size
        job_outs.append((shape[:-1] + (columns,), bf16))
        job_scratch_out.append(pltpu.VMEM(shape[:-1] + (columns,), bf16))
    extra = [pltpu.SemaphoreType.DMA((len(job_ins) + len(jobs),))] if jobs else []
    out_count, scratch_count = len(outs), len(scratch)

    def run(*refs):
        refs = list(refs)

        def pop(number):
            got, refs[:] = refs[:number], refs[number:]
            return got

        mine = pop(count)
        sources = pop(len(job_ins))
        pop(len(deps))
        mine += pop(out_count)
        targets = pop(len(job_outs))
        mine += pop(scratch_count)
        buffers = pop(len(job_ins))
        results = pop(len(job_outs))
        copies = []
        n = 0
        for job in jobs:
            for terms, fixed, size in job:
                for value, bits, column in terms:
                    index = job_index(mine[0], bits, fixed) + (slice(None), pl.ds(column, size))
                    copies.append(
                        pltpu.make_async_copy(sources[n].at[index], buffers[n], refs[0].at[n])
                    )
                    n += 1
        begin(copies)
        kernel(*mine)
        n = 0
        leaving = []
        for job, target, final in zip(jobs, results, targets):
            column = 0
            for terms, fixed, size in job:
                finish(copies[n : n + len(terms)])
                lead = target.shape[:-2]
                for flat in range(2 ** len(lead)):
                    at = tuple((flat >> k) % 2 for k in range(len(lead)))
                    total = None
                    for buffer in buffers[n : n + len(terms)]:
                        part = buffer[at].astype(f32)
                        total = part if total is None else total + part
                    target[at + (slice(None), slice(column, column + size))] = total.astype(bf16)
                n += len(terms)
                column += size
            leaving.append(
                pltpu.make_async_copy(target, final, refs[0].at[len(job_ins) + len(leaving)])
            )
            leaving[-1].start()
        finish(leaving)

    return pl.pallas_call(
        run,
        out_shape=tuple(jax.ShapeDtypeStruct(s, k) for s, k in list(outs) + job_outs),
        in_specs=[SMEM]
        + [VMEM] * (count - 1 - hbm_ins)
        + [HBM] * (hbm_ins + len(job_ins) + len(deps)),
        out_specs=tuple(
            [VMEM] * (out_count - hbm_outs) + [HBM] * (hbm_outs + len(job_outs))
        ),
        scratch_shapes=list(scratch) + job_scratch + job_scratch_out + extra,
        cost_estimate=pl.CostEstimate(flops=int(us * COST), transcendentals=0, bytes_accessed=1),
        compiler_params=PARAMS,
        name=name,
    )(*ins, *job_ins, *deps)


def after(values, *tokens):
    return lax.optimization_barrier((values, tokens))[0]


class Chunk:
    def __init__(self, outs, where, counts):
        self.where, self.counts = where, counts
        if len(outs) == 2:
            self.other, self.mine = outs
        else:
            full = outs[0]
            dp_count = counts["dp"]
            parts = full.reshape(dp_count // 2, 2, full.shape[0] // dp_count, full.shape[1])
            core = where["dp"] % 2
            self.other = lax.dynamic_index_in_dim(parts, 1 - core, 1, keepdims=False)
            self.mine = lax.dynamic_index_in_dim(parts, core, 1, keepdims=False)
        self.bits = [("dp", bit) for bit in bits_of(counts["dp"])[:0:-1]]
        self.bits += [("seq", bit) for bit in bits_of(counts["seq"])[::-1]]
        self.rows = self.mine.shape[1] // counts["seq"]

    def core(self):
        recv = self.recv = swap(self.other, "dp", 1, self.counts["dp"])
        columns = recv.shape[-1]
        half = columns // 256 * 128
        both = [self.shaped(value, self.bits) for value in (self.mine, recv)]
        self.groups = [
            {"terms": [(v, tuple(self.bits), at) for v in both], "fixed": {}, "columns": size}
            for at, size in ((0, half), (half, columns - half))
        ]
        order = [bit for bit in self.bits if bit[0] == "dp"]
        self.orders = list(zip(order[::-1], order))

    def shaped(self, value, bits):
        return value.reshape((2,) * len(bits) + (self.rows, value.shape[-1]))

    def total_at(self, group, flips):
        total = None
        for value, bits, column in group["terms"]:
            start, size = [], []
            for bit in bits:
                at = (self.where[bit[0]] // bit[1]) % 2
                start.append((1 - at if flips[bit] else at) if bit in flips else 0)
                size.append(1 if bit in flips else 2)
            part = lax.dynamic_slice(
                value, start + [0, column], size + [self.rows, group["columns"]]
            )
            free = [n for n in size if n > 1]
            part = part.reshape(free + [self.rows, group["columns"]]).astype(f32)
            total = part if total is None else total + part
        return total

    def jobs(self, bits, joint):
        parts = []
        for group, bit in zip(self.groups, bits):
            parts.append((list(group["terms"]), {**group["fixed"], bit: 1}, group["columns"]))
            group["fixed"][bit] = 0
        self.todo = list(bits[:1]) if joint else list(bits)
        jobs = [parts] if joint else [[part] for part in parts]
        if self.rows % 8 == 0:
            return jobs
        self.accept(
            [
                jnp.concatenate(
                    [
                        self.total_at({"terms": t, "columns": c}, flips)
                        for t, flips, c in job
                    ],
                    axis=-1,
                ).astype(bf16)
                for job in jobs
            ]
        )
        return []

    def across(self):
        return self.jobs(self.orders.pop(0), False)

    def along(self, index):
        return self.jobs([("seq", index)] * len(self.groups), True)

    def plain(self, jobs):
        return [
            jnp.concatenate(
                [self.total_at({"terms": t, "columns": c}, flips) for t, flips, c in job], axis=-1
            ).astype(bf16)
            for job in jobs
        ]

    def wait(self, *tokens):
        values = after([[t[0] for t in group["terms"]] for group in self.groups], *tokens)
        for group, got in zip(self.groups, values):
            group["terms"] = [(v, t[1], t[2]) for v, t in zip(got, group["terms"])]

    def accept(self, values):
        values = list(values)
        if not values:
            return
        self.sent = values
        got = [
            swap(value.reshape(-1, value.shape[-1]), bit[0], bit[1], self.counts[bit[0]])
            for value, bit in zip(values, self.todo)
        ]
        column = 0
        for n, group in enumerate(self.groups):
            recv = got[n] if len(got) > 1 else got[0]
            bits = tuple(bit for bit in self.bits if bit not in group["fixed"])
            group["terms"].append(
                (self.shaped(recv, bits), bits, 0 if len(got) > 1 else column)
            )
            column += group["columns"]

    def rest(self):
        while self.orders:
            self.accept(self.plain(self.across()))

    def straight(self):
        seq = [bit for bit in self.bits if bit[0] == "seq"]
        jobs = []
        for jump in range(1, self.counts["seq"]):
            flips = {bit: jump // bit[1] % 2 for bit in seq}
            jobs.append(
                [
                    (list(g["terms"]), {**g["fixed"], **flips}, g["columns"])
                    for g in self.groups
                ]
            )
        for group in self.groups:
            group["fixed"].update({bit: 0 for bit in seq})
        if self.rows % 8 == 0:
            return jobs
        self.accept_straight(
            [
                jnp.concatenate(
                    [self.total_at({"terms": t, "columns": c}, flips) for t, flips, c in job],
                    axis=-1,
                ).astype(bf16)
                for job in jobs
            ]
        )
        return []

    def accept_straight(self, values):
        values = list(values)
        if not values:
            return
        self.sent = values
        for jump, value in enumerate(values):
            got = swap(value, "seq", jump + 1, self.counts["seq"])
            column = 0
            for group in self.groups:
                group["terms"].append((self.shaped(got, ()), (), column))
                column += group["columns"]

    def total(self, *tokens):
        groups = None
        if tokens:
            values = [[term[0] for term in group["terms"]] for group in self.groups]
            groups = after(values, *tokens)
        parts = []
        for n, group in enumerate(self.groups):
            terms = group["terms"]
            if groups:
                terms = [(v, t[1], t[2]) for v, t in zip(groups[n], terms)]
            parts.append(
                self.total_at({"terms": terms, "columns": group["columns"]}, group["fixed"])
            )
        return jnp.concatenate(parts, axis=-1)


def body(
    hidden_in,
    segment_ids,
    query_emb,
    positives,
    w_qkv,
    query_bias,
    value_bias,
    w_out,
    out_bias,
    norm1_gain,
    norm1_bias,
    w_up,
    up_bias,
    w_down,
    down_bias,
    norm2_gain,
    norm2_bias,
    w_proj,
):
    micro_count, row_count, local_len, width = hidden_in.shape
    full_len = segment_ids.shape[2]
    embed_width = w_proj.shape[1]
    ff = w_up.shape[1]
    queries_local = query_emb.shape[1]
    query_tokens = query_emb.shape[2]
    seq_count = lax.axis_size("seq")
    dp_count = lax.axis_size("dp")
    seq_pos = lax.axis_index("seq")
    dp_pos = lax.axis_index("dp")
    rows = micro_count * row_count
    tokens = rows * local_len
    far = 64
    window = 3 * local_len + far
    assert local_len + far >= PASSAGE_MOST - 1 and seq_count == 4

    x_own = hidden_in.reshape(rows, local_len, width)
    x_flat = x_own.reshape(tokens, width)
    low_half = seq_pos < 2
    inner = [(1, 2), (2, 1), (0, 0), (3, 3)]
    far_send = jnp.where(low_half, x_own[:, local_len - far :], x_own[:, :far])
    middle_x = lax.ppermute(x_flat, "seq", inner)
    far_x = swap(far_send.reshape(rows * far, width), "seq", 2, seq_count)
    side_x = swap(x_flat, "seq", 1, seq_count)
    pieces = [side_x, middle_x, far_x]

    seg_full = segment_ids.reshape(rows, full_len)
    edges = jnp.sum(
        (seg_full[:, None, :] < jnp.arange(1, SEGS, dtype=jnp.int32)[None, :, None]).astype(
            jnp.int32
        ),
        axis=2,
    )
    meta = jnp.concatenate(
        [
            jnp.stack(
                [
                    seq_pos * local_len,
                    dp_pos,
                    (seq_pos ^ 1) * local_len,
                    jnp.where((seq_pos == 1) | (seq_pos == 2), 3 - seq_pos, -9) * local_len,
                    jnp.where(
                        low_half, (seq_pos + 2) * local_len, (seq_pos - 1) * local_len - far
                    ),
                    dp_pos * row_count * SEGS,
                    dp_pos % 2,
                    seq_pos,
                ]
            ).astype(jnp.int32),
            edges.reshape(-1),
        ]
    )

    queries = query_emb.reshape(micro_count, queries_local * query_tokens, embed_width)
    bits = bits_of(dp_count)
    strides = [bits[:1]] + [bits[k : k + 2] for k in range(1, len(bits), 2)]

    queries = lax.all_gather(queries, "dp", axis=1, tiled=True)
    query_all = queries.shape[1]
    query_count = query_all // query_tokens
    wide = max(128, query_count)
    positives_wide = jnp.pad(
        positives, ((0, 0), (0, wide - query_count)), constant_values=-1
    )

    pairs = width // 128
    chunks = ff // width
    query, kv_own, x_t_own = call(
        functools.partial(own_kernel, (rows, local_len, width)),
        [
            ((tokens, width), bf16),
            ((rows, local_len, 2 * width), bf16),
            ((rows, width, local_len), bf16),
        ],
        [meta, query_bias, value_bias, x_flat, w_qkv],
        name="own",
        us=3,
    )
    forward = call(
        functools.partial(
            forward_kernel, (rows, local_len, far, window, full_len, width, row_count)
        ),
        [
            ((7 + chunks, width), f32),
            ((width, tokens), bf16),
            ((rows, pairs, 2 * local_len), f32),
            ((tokens, 128), f32),
            ((tokens, width), f32),
            ((width, tokens), bf16),
            ((tokens, embed_width), f32),
            ((tokens, embed_width), bf16),
            ((rows * SEGS, query_all), f32),
            ((rows, window, 2 * width), bf16),
            ((rows, width, window), bf16),
            ((tokens, width), f32),
            ((width, tokens), bf16),
            ((chunks, width, tokens), bf16),
            ((chunks, tokens, width), bf16),
        ],
        [
            meta,
            value_bias,
            out_bias,
            norm1_gain,
            norm1_bias,
            down_bias,
            norm2_gain,
            norm2_bias,
            up_bias,
            w_proj,
            query,
            x_flat,
            *pieces,
            kv_own,
            x_t_own,
            queries,
            w_qkv,
            w_out,
            w_up,
            w_down,
        ],
        [
            pltpu.VMEM((window, local_len), f32),
            pltpu.VMEM((tokens, width), bf16),
            pltpu.VMEM((tokens, width), bf16),
            pltpu.VMEM((tokens, width), bf16),
            pltpu.VMEM((tokens, width), bf16),
            pltpu.VMEM((rows * far, width), bf16),
            pltpu.VMEM(queries.shape, bf16),
            pltpu.VMEM((width, 3 * width), bf16),
            pltpu.VMEM((width, width), bf16),
            pltpu.VMEM((chunks, width, width), bf16),
            pltpu.VMEM((chunks, width, width), bf16),
            pltpu.VMEM((rows, window, 2 * width), bf16),
            pltpu.VMEM((rows, width, window), bf16),
            pltpu.VMEM((tokens, width), f32),
            pltpu.VMEM((width, tokens), bf16),
            pltpu.VMEM((chunks, width, tokens), bf16),
            pltpu.VMEM((chunks, tokens, width), bf16),
            pltpu.VMEM((tokens, width), bf16),
            pltpu.VMEM((tokens, width), f32),
            pltpu.SemaphoreType.DMA((13 + 4 * chunks,)),
        ],
        name="forward",
        us=20,
        hbm_ins=11,
        hbm_outs=6,
    )
    vectors, context_t, lse, cols, norm2, hidden2_t, proj, embed, parts = forward[:9]
    kv, x_t, norm1, hidden1_t, act_t, slope = forward[9:]

    others = [swap(parts, "seq", bit, seq_count) for bit in (1, 2, 3)]
    stat_rows = 8
    merged, score, stats = call(
        functools.partial(score_kernel, (rows, full_len, row_count, query_tokens)),
        [
            ((rows * SEGS, query_all), f32),
            ((rows * SEGS, wide), f32),
            ((stat_rows, wide), f32),
        ],
        [meta, parts, *others, positives_wide],
        name="score",
        us=2,
    )
    is_whole = lax.broadcasted_iota(jnp.int32, stats.shape, 0) < micro_count
    for group in strides:
        jumps = group if len(group) == 1 else [group[0], group[1], group[0] + group[1]]
        recv = [swap(stats, "dp", jump, dp_count) for jump in jumps]
        if len(recv) == 1:
            best = jnp.maximum(stats, recv[0])
            whole = jnp.exp(stats - best) + jnp.exp(recv[0] - best)
            hits = stats + recv[0]
        else:
            best = jnp.maximum(jnp.maximum(stats, recv[0]), jnp.maximum(recv[1], recv[2]))
            whole = (jnp.exp(stats - best) + jnp.exp(recv[0] - best)) + (
                jnp.exp(recv[1] - best) + jnp.exp(recv[2] - best)
            )
            hits = (stats + recv[0]) + (recv[1] + recv[2])
        stats = jnp.where(is_whole, best + jnp.log(whole), hits)

    devices = dp_count * seq_count

    def places(depth, columns):
        block = depth // dp_count
        if block % 16 == 0:
            return [((dp_count // 2, block, columns), bf16)] * 2
        return [((depth, columns), bf16)]

    where = {"dp": dp_pos, "seq": seq_pos}
    counts = {"dp": dp_count, "seq": seq_count}
    down_places = places(ff, width)
    loss, d_proj, g_resid2, vec_c, *outs = call(
        functools.partial(
            upper_kernel, (rows, local_len, full_len, row_count, query_tokens)
        ),
        [
            ((micro_count, wide), f32),
            ((width, embed_width), bf16),
            ((tokens, width), f32),
            ((8, width), f32),
        ]
        + down_places,
        [
            meta,
            merged,
            score,
            stats,
            positives_wide,
            queries,
            embed,
            proj,
            norm2,
            hidden2_t,
            cols,
            vectors,
            w_proj,
            act_t,
        ],
        [
            pltpu.VMEM((chunks, width, width), bf16),
            pltpu.VMEM((chunks, width, tokens), bf16),
            pltpu.VMEM((rows * SEGS, query_all), f32),
            pltpu.VMEM((tokens, embed_width), f32),
            pltpu.SemaphoreType.DMA((1 + max(dp_count, chunks),)),
        ],
        hbm_ins=1,
        name="upper",
        us=8,
        hbm_outs=len(down_places),
    )
    losses = lax.dynamic_slice_in_dim(loss, dp_pos * queries_local, queries_local, 1)
    down = Chunk(outs, where, counts)
    down.core()

    up_places = places(width, ff + width + embed_width)
    d_ubias, g_resid1, g_context, vec_d, *outs = call(
        lower_kernel,
        [
            ((chunks, 1, width), f32),
            ((tokens, width), f32),
            ((tokens, width), bf16),
            ((8, width), f32),
        ]
        + up_places,
        [
            meta,
            g_resid2,
            hidden1_t,
            norm1,
            cols,
            vectors,
            context_t,
            w_out,
            d_proj,
            w_down,
            w_up,
            slope,
        ],
        [
            pltpu.VMEM((chunks, width, width), bf16),
            pltpu.VMEM((chunks, width, width), bf16),
            pltpu.VMEM((chunks, tokens, width), bf16),
            pltpu.VMEM((tokens, width), f32),
            pltpu.VMEM((tokens, width), bf16),
            pltpu.VMEM((chunks, width, width), bf16),
            pltpu.VMEM((width, width + embed_width), bf16),
            pltpu.SemaphoreType.DMA(((3 + dp_count) * chunks + dp_count,)),
        ],
        name="lower",
        us=13,
        hbm_ins=3,
        hbm_outs=len(up_places),
    )
    up = Chunk(outs, where, counts)
    up.core()

    def fold(chunks_jobs, *tokens, us=FOLD):
        jobs = [job for _, got, _ in chunks_jobs for job in got]
        values = call(nothing, [], [meta], name="fold", deps=tokens, jobs=jobs, us=us) if jobs else []
        at = 0
        sent = []
        for chunk, got, accept in chunks_jobs:
            accept(values[at : at + len(got)])
            at += len(got)
            sent += chunk.sent
        return sent

    sends = fold([(down, down.across(), down.accept)], g_resid1, us=3)
    last_places = places(width, 3 * width + 128)
    sends = fold([(up, up.across(), up.accept)], *sends, us=3)
    g_own, g_side, g_middle, g_far, *outs = call(
        functools.partial(
            attention_kernel, (rows, local_len, far, window, full_len, width, devices)
        ),
        [
            ((tokens, width), f32),
            ((tokens, width), bf16),
            ((tokens, width), bf16),
            ((rows * far, width), bf16),
        ]
        + last_places,
        [meta, g_context, query, lse, vec_c, vec_d, d_ubias, g_resid1, kv, x_t, w_qkv],
        [
            pltpu.VMEM((rows, window, 2 * width), bf16),
            pltpu.VMEM((rows, width, window), bf16),
            pltpu.VMEM((tokens, width), bf16),
            pltpu.VMEM((rows, window, 2 * width), bf16),
            pltpu.VMEM((width, 3 * width), bf16),
            pltpu.VMEM((window, local_len), f32),
            pltpu.VMEM((3, width, width), bf16),
            pltpu.VMEM((width, 128), bf16),
            pltpu.VMEM((width, 128), f32),
            pltpu.SemaphoreType.DMA((rows + 2 + 4 * dp_count,)),
        ],
        name="attention",
        us=20,
        hbm_ins=3,
        hbm_outs=len(last_places),
        deps=sends,
    )
    last = Chunk(outs, where, counts)
    received = [term[0] for group in up.groups for term in group["terms"]]
    halo = {}
    token = [g_own]
    for step in ORDER:
        if step in ("m", "s", "f"):
            token = token + [halo[step.upper()]]
        elif step == "M":
            halo[step] = lax.ppermute(after(g_middle, token), "seq", inner)
        elif step == "S":
            halo[step] = swap(after(g_side, token), "seq", 1, seq_count)
        elif step == "F":
            halo[step] = swap(after(g_far, token), "seq", 2, seq_count)
        elif step == "C0":
            last.other = after(last.other, token, received)
            last.core()
        elif step == "c0":
            token = token + [last.recv]
        elif step == "C1":
            token = fold([(last, last.across(), last.accept)], *token)
        elif step == "C3":
            last.rest()
            token = fold([(last, last.straight(), last.accept_straight)], *token)
        else:
            chunk = {"A": down, "B": up, "C": last}[step[0]]
            if not step[2:]:
                chunk.wait(*token)
            if step[1] == "2":
                jobs = chunk.across()
            else:
                chunk.rest()
                jobs = chunk.along(1 if step[1] == "3" else 2)
            if step[2:] and jobs:
                token = list(call(nothing, [], [meta], name="fold", deps=token, jobs=jobs, us=FOLD))
                chunk.accept(token)
            else:
                chunk.accept(chunk.plain(jobs))
                token = list(chunk.sent)
    g_own, from_side, from_middle, from_far = after(
        (g_own, halo["S"], halo["M"], halo["F"]), *token
    )
    from_far = from_far.reshape(rows, far, width).astype(f32)
    pad = ((0, 0), (local_len - far, 0), (0, 0))
    flip = ((0, 0), (0, local_len - far), (0, 0))
    grad_in = (g_own + from_side.astype(f32) + from_middle.astype(f32)).reshape(
        rows, local_len, width
    ) + jnp.where(low_half, jnp.pad(from_far, pad), jnp.pad(from_far, flip))

    down_part = down.total(grad_in)
    up_part = up.total(down_part)
    last_part = last.total(up_part)
    some = 4 * width // devices
    vec_at = 3 * width
    vec_part = last_part[:3, vec_at : vec_at + some]
    return (
        embed.reshape(micro_count, row_count, local_len, embed_width),
        losses,
        grad_in.reshape(micro_count, row_count, local_len, width),
        last_part[:, : 3 * width].reshape(-1),
        up_part[:, ff : ff + width].reshape(-1),
        up_part[:, :ff].reshape(-1),
        down_part.reshape(-1),
        up_part[:, ff + width :].reshape(-1),
        vec_part[0],
        vec_part[1:].reshape(-1),
    )


def solution(mesh):
    in_specs = (
        P(None, "dp", "seq", None),
        P(None, "dp", None),
        P(None, "dp", None, None),
    ) + (P(),) * 15
    out_specs = (
        P(None, "dp", "seq", None),
        P(None, "dp"),
        P(None, "dp", "seq", None),
    ) + (P(("dp", "seq")),) * 7
    return jax.shard_map(body, mesh=mesh, in_specs=in_specs, out_specs=out_specs, check_vma=False)
```
